512 devices in a mesh: gx: 32 (over y, x, core), vert: 16 (over z).
Axes of the slice: x: 4, y: 4, z: 16, core: 2. Of those that a mesh axis runs over, the one named last changes fastest.
Arguments:
- state: float32 [256, 16, 16384], P('gx', None, 'vert'), may hold values from -6 to 6
- macro: float32 [5, 256, 16], P(None, 'gx'), may hold values from -4 to 4
- relax_rate: float32 [256, 16], P('gx'), may hold values from 0.01 to 300, as said below
- velocity: float32 [3, 16384], P(None, 'vert'), may hold values from -2 to 4
- vel_sign: int32 [16384], P('vert'), may hold values from 0 to 1, as said below
- quad_weight: float32 [16384], P('vert'), may hold values from 0.5 to 2
- freestream: float32 [16, 16384], P(None, 'vert'), may hold values from -6 to 6
- wall_flag: int32 [16], replicated, may hold values 0 or 1
Outputs:
- new_state: float32 [256, 16, 16384], P('gx', None, 'vert')
- new_macro: float32 [5, 256, 16], P(None, 'gx')
The draws below stay inside these ranges and needn't reach their ends.
Inputs may be any that keep to these rules, and one draw needn't show every extreme that they name: Each row of relax_rate varies from cell to cell. `vel_sign`: every aligned block of 1024 velocities holds both signs.
All inputs are finite; a program needn't handle non-finite values.
Results may differ from the reference program's by a relative error of at most 0.00013.
Values sent between devices are 32-bit elements; how exact they have to be, the bound alone decides.
No kernel may reach another device: no remote copies, remote signals or barrier semaphores. Data moves between devices by JAX's collectives and lax.ppermute only.
A program may use at most 64 MiB of HBM per device.

```python
import math
import jax
import jax.numpy as jnp
from jax import lax

CELLS_ACROSS = 16
V_DEV = 1024
FIELDS = 5
CELLS_ALONG = 256
V = 16384


def draw_velocity(key, part):
    key_major = jax.random.fold_in(key, 21)
    key_minor = jax.random.fold_in(key, 22)
    lower_end = 0.1
    magnitude = jnp.exp(jax.random.uniform(key_major, (1, V), jnp.float32, math.log(lower_end), math.log(4.0)))
    transverse = jnp.clip(0.7 * jax.random.normal(key_minor, (2, V), jnp.float32), -2.0, 2.0)
    return jnp.concatenate([magnitude, transverse], axis=0)


def draw_relax_rate(key, part):
    key_background = jax.random.fold_in(key, 11)
    random_key_cells = jax.random.fold_in(key, 12)
    random_key_level = jax.random.fold_in(key, 13)
    lower_end = 0.02
    upper_end = 0.3
    baseline_level = jnp.exp(jax.random.uniform(key_background, (CELLS_ALONG, CELLS_ACROSS), jnp.float32, math.log(lower_end), math.log(upper_end)))
    spike_cells = jax.random.randint(random_key_cells, (4,), 0, CELLS_ALONG)
    spike_level = jnp.exp(jax.random.uniform(random_key_level, (4, CELLS_ACROSS), jnp.float32, math.log(100.0), math.log(300.0)))
    spike_mask = jnp.arange(CELLS_ALONG)[:, None] == spike_cells[None, :]
    spike_rate = jnp.max(jnp.where(spike_mask[:, :, None], spike_level[None, :, :], 0.0), axis=1)
    return jnp.where(jnp.any(spike_mask, axis=1)[:, None], spike_rate, baseline_level)


def draw_vel_sign(key, part):
    coin_flips = jax.random.randint(key, (V,), 0, 2)
    offset = jnp.arange(V) % V_DEV
    return jnp.where(offset == 0, 1, jnp.where(offset == 1, 0, coin_flips)).astype(jnp.int32)


def set_ends(entries, own_key, low, high):
    longest = entries.shape.index(max(entries.shape))
    spots = []
    for shift in (0, 1):
        where = [jax.random.randint(jax.random.fold_in(own_key, axis), (), 0, length) for axis, length in enumerate(entries.shape)]
        where[longest] = (where[longest] + shift) % entries.shape[longest]
        spots.append(tuple(where))
    return entries.at[spots[0]].set(low).at[spots[1]].set(high)


def shard_levels(stream_key, dims, cuts, smallest, top_value):
    def one(dim, parts):
        steps = jax.random.uniform(jax.random.fold_in(jax.random.fold_in(stream_key, 6), dim), (parts,), jnp.float32, smallest / len(cuts), top_value / len(cuts))
        return jnp.repeat(jnp.exp(steps), dims[dim] // parts).reshape((-1,) + (1,) * (len(dims) - dim - 1))

    loudness = one(*cuts[0])
    for cut in cuts[1:]:
        loudness = loudness * one(*cut)
    return loudness


def normal_values(rng, dims, scale, most, split=(), kind=jnp.bfloat16):
    array = scale * jax.random.normal(rng, dims, jnp.float32)
    if split:
        array = array * shard_levels(rng, dims, split, -0.22, 0.18)
    return jnp.clip(array, -most, most).astype(kind)


def setup_inputs(seed: int = 0) -> dict:
    splits = jax.random.split(jax.random.key(seed), 9)
    state = normal_values(splits[0], (CELLS_ALONG, CELLS_ACROSS, V), 1.0, 6.0, ((0, 32), (2, 16)), jnp.float32)
    macro = normal_values(splits[1], (FIELDS, CELLS_ALONG, CELLS_ACROSS), 0.5, 4.0, ((1, 32),), jnp.float32)
    relax_rate = draw_relax_rate(jax.random.fold_in(splits[8], 71), 0)
    velocity = draw_velocity(jax.random.fold_in(splits[8], 71), 0)
    vel_sign = draw_vel_sign(jax.random.fold_in(splits[8], 71), 0)
    quad_weight = jnp.clip(jnp.exp(math.log(2.0) - 1.3862944 * jax.random.uniform(splits[5], (V,), jnp.float32) ** shard_levels(splits[5], (V,), ((0, 16),), -0.2, 0.2)), 0.5, 2.0)
    freestream = normal_values(splits[6], (CELLS_ACROSS, V), 1.0, 6.0, ((1, 16),), jnp.float32)
    wall_flag = set_ends((jax.random.randint(splits[7], (CELLS_ACROSS,), 0, 2) < 1).astype(jnp.int32), jax.random.fold_in(splits[7], 1), 0, 1)
    return dict(state=state, macro=macro, relax_rate=relax_rate, velocity=velocity, vel_sign=vel_sign, quad_weight=quad_weight, freestream=freestream, wall_flag=wall_flag)


exact_mode = lax.Precision.HIGHEST


def basis_sets(velocity, vel_sign, quad_weight, groups):
    magnitude = velocity[0]
    along_x = jnp.where(vel_sign == 1, magnitude, -magnitude)
    along_y = velocity[1]
    along_z = velocity[2]
    square = along_x * along_x + along_y * along_y + along_z * along_z
    ones_row = jnp.ones_like(along_x)
    equil_basis = jnp.stack([ones_row, 2.0 * along_x, 2.0 * along_y, 2.0 * along_z, square - 1.5])
    weights = quad_weight / (quad_weight.shape[0] * groups)
    heat_factor = 0.2 * (square - 2.5)
    moment_rows = jnp.stack([ones_row, along_x, along_y, along_z, (2.0 / 3.0) * square - 1.0,
                             2.0 * along_x * along_y, 2.0 * along_x * along_z, 2.0 * along_y * along_z,
                             2.0 * (along_x * along_x - square / 3.0), 2.0 * (along_y * along_y - square / 3.0),
                             heat_factor * along_x, heat_factor * along_y, heat_factor * along_z])
    outflux = jnp.where(vel_sign == 0, weights * magnitude, 0.0)
    influx = jnp.where(vel_sign == 1, weights * magnitude, 0.0)
    return magnitude, equil_basis, moment_rows * weights, outflux, influx


def sweep_line(decay, driven, inflow, reverse):
    def advance_cell(carried, pieces):
        updated_cell = pieces[0] * carried + pieces[1]
        return updated_cell, updated_cell
    _, values_all = lax.scan(advance_cell, inflow, (decay, driven), reverse=reverse)
    return values_all


def advance(padded, relax_cells):
    fields = padded
    conserved = fields[:5]
    flow_x = jnp.stack([fields[1], fields[0] + fields[4] + fields[8], fields[5], fields[6],
                        (2.0 / 3.0) * (fields[1] + fields[10])])
    flow_y = jnp.stack([fields[2], fields[5], fields[0] + fields[4] + fields[9], fields[7],
                        (2.0 / 3.0) * (fields[2] + fields[11])])
    centre = conserved[:, 1:-1, 1:-1]
    laplace = (conserved[:, 2:, 1:-1] + conserved[:, :-2, 1:-1] + conserved[:, 1:-1, 2:]
               + conserved[:, 1:-1, :-2] - 4.0 * centre)
    divergence = (flow_x[:, 2:, 1:-1] - flow_x[:, :-2, 1:-1] + flow_y[:, 1:-1, 2:] - flow_y[:, 1:-1, :-2])
    diffusivity = 0.2 / (1.0 + relax_cells)
    return centre + diffusivity * laplace - 0.25 * divergence, centre


def reference(state, macro, relax_rate, velocity, vel_sign, quad_weight, freestream, wall_flag):
    magnitude, equil_basis, moment_basis, outflux, influx = basis_sets(velocity, vel_sign, quad_weight, 1)
    courant = CELLS_ALONG * magnitude
    relax_cell = relax_rate[:, :, None]
    equil_state = jnp.einsum("kxy,kv->xyv", macro, equil_basis, precision=exact_mode)
    divisor = 1.0 + courant + relax_cell
    decay = courant / divisor
    driven = (state + relax_cell * equil_state) / divisor
    back = sweep_line(decay, driven, freestream, True)
    rho_wall = jnp.dot(back[0], outflux, precision=exact_mode) / jnp.sum(influx)
    inflow_left = jnp.where(wall_flag[:, None] == 1, rho_wall[:, None], freestream)
    fore = sweep_line(decay, driven, inflow_left, False)
    kinetic = jnp.where(vel_sign == 1, fore, back)
    moments = jnp.einsum("xyv,kv->kxy", kinetic, moment_basis, precision=exact_mode)
    padded = jnp.pad(moments, ((0, 0), (1, 1), (0, 0)))
    padded = jnp.concatenate([padded[:, :, -1:], padded, padded[:, :, :1]], axis=2)
    updated, centre = advance(padded, relax_rate)
    change = updated - centre
    new_state = kinetic + jnp.einsum("kxy,kv->xyv", change, equil_basis, precision=exact_mode)
    return new_state, updated
```

```python
import jax
import jax.numpy as jnp
from jax import lax
from jax.experimental import pallas as pl
from jax.experimental.pallas import tpu as pltpu
from jax.sharding import PartitionSpec as P

LANES = 128
QUAD = 4
SENT_ROWS = 32
INTERPRET = False


def signed_velocity(velocity_ref, sign_ref, lanes):
    magnitude = velocity_ref[0:1, lanes]
    positive = sign_ref[0:1, lanes] == 1
    along_x = jnp.where(positive, magnitude, -magnitude)
    along_y = velocity_ref[1:2, lanes]
    along_z = velocity_ref[2:3, lanes]
    square = along_x * along_x + along_y * along_y + along_z * along_z
    return magnitude, positive, along_x, along_y, along_z, square


def maps_kernel(
    total_cells,
    state_ref,
    macro_ref,
    relax_ref,
    velocity_ref,
    sign_ref,
    free_ref,
    wall_ref,
    reach_ref,
    run_ref,
    sent_ref,
    side_ref,
    pad_ref,
    spread_ref,
):
    fields, cells_x, cells_y = macro_ref.shape
    tiles = state_ref.shape[2] // LANES
    pad_ref[...] = jnp.zeros_like(pad_ref)
    for k in range(fields):
        pad_ref[k * cells_x : (k + 1) * cells_x, 0:cells_y] = macro_ref[k]
    base_row = fields * cells_x
    pad_ref[base_row : base_row + cells_x, 0:cells_y] = relax_ref[...]
    wall_row = base_row + cells_x
    pad_ref[wall_row : wall_row + 1, 0:cells_y] = (wall_ref[...] == 1).astype(jnp.float32)
    columns = pad_ref[...].T
    for c in range(wall_row + 1):
        spread_ref[c] = jnp.broadcast_to(columns[0:cells_y, c : c + 1], (cells_y, LANES))
    for tile in range(tiles):
        lanes = slice(tile * LANES, (tile + 1) * LANES)
        magnitude, positive, along_x, along_y, along_z, square = signed_velocity(
            velocity_ref, sign_ref, lanes
        )
        courant = total_cells * magnitude
        base = 1.0 + courant
        basis = [2.0 * along_x, 2.0 * along_y, 2.0 * along_z, square - 1.5]
        for half in range(cells_y // 8):
            rows = slice(half * 8, half * 8 + 8)
            forward = jnp.broadcast_to(positive, (8, LANES))
            decay = []
            driven = []
            for x in range(cells_x):
                relax = spread_ref[base_row + x, rows]
                equil = spread_ref[x, rows]
                for k in range(1, fields):
                    equil = equil + spread_ref[k * cells_x + x, rows] * basis[k - 1]
                inverse = 1.0 / (base + relax)
                decay.append(courant * inverse)
                driven.append((state_ref[x, rows, lanes] + relax * equil) * inverse)
            last = cells_x - 1
            steps = [jnp.where(forward, decay[t], decay[last - t]) for t in range(cells_x)]
            gains = [jnp.where(forward, driven[t], driven[last - t]) for t in range(cells_x)]
            products = [steps[0]]
            runs = [gains[0]]
            for t in range(1, cells_x):
                products.append(steps[t] * products[-1])
                runs.append(steps[t] * runs[-1] + gains[t])
            for x in range(cells_x):
                reach_ref[x, rows, lanes] = jnp.where(forward, products[x], products[last - x])
                run_ref[x, rows, lanes] = jnp.where(forward, runs[x], runs[last - x])
            wall = spread_ref[wall_row, rows] > 0.5
            free = free_ref[rows, lanes]
            diffuse = jnp.logical_and(forward, wall)
            fixed = jnp.where(diffuse, 0.0, free)
            unit = jnp.where(diffuse, 1.0, 0.0)
            direction = jnp.where(forward, 1.0, 0.0)
            for part in range(8 // QUAD):
                owner = (half * (8 // QUAD) + part) * tiles + tile
                quad = slice(part * QUAD, (part + 1) * QUAD)
                for slot, value in enumerate((products[last], runs[last], steps[0], gains[0])):
                    sent_ref[owner, slot * QUAD : (slot + 1) * QUAD, :] = value[quad]
                for slot, value in enumerate((fixed, unit, direction)):
                    side_ref[owner, slot * QUAD : (slot + 1) * QUAD, :] = value[quad]


def scan_kernel(maps_ref, side_ref, sent_ref, entry_ref, near_ref):
    slabs = maps_ref.shape[0]
    me = lax.axis_index("gx")
    side = side_ref[me]
    fixed = side[0:QUAD]
    unit = side[QUAD : 2 * QUAD]
    forward = side[2 * QUAD : 3 * QUAD] > 0.5
    nothing = jnp.zeros_like(fixed)
    value = fixed
    near_ref[0] = nothing
    for i in range(slabs - 1, -1, -1):
        slab = maps_ref[i]
        entry_ref[i] = value
        if i < slabs - 1:
            near_ref[i + 1] = slab[2 * QUAD : 3 * QUAD] * value + slab[3 * QUAD : 4 * QUAD]
        value = slab[0:QUAD] * value + slab[QUAD : 2 * QUAD]
    near_ref[slabs] = slab[2 * QUAD : 3 * QUAD] * entry_ref[0] + slab[3 * QUAD : 4 * QUAD]
    leaving = value
    value = fixed
    answer = unit
    for i in range(slabs):
        slab = maps_ref[i]
        sent_ref[i, 0:QUAD] = jnp.where(forward, value, entry_ref[i])
        sent_ref[i, QUAD : 2 * QUAD] = jnp.where(forward, answer, leaving)
        value = slab[0:QUAD] * value + slab[QUAD : 2 * QUAD]
        answer = slab[0:QUAD] * answer
        upwind = near_ref[i] if i > 0 else nothing
        if i < slabs - 1:
            ahead = maps_ref[i + 1]
            step = ahead[2 * QUAD : 3 * QUAD]
            next_value = step * value + ahead[3 * QUAD : 4 * QUAD]
            next_answer = step * answer
        else:
            next_value = nothing
            next_answer = nothing
        sent_ref[i, 2 * QUAD : 3 * QUAD] = jnp.where(forward, next_value, upwind)
        sent_ref[i, 3 * QUAD : 4 * QUAD] = jnp.where(forward, next_answer, 0.0)


def whole_rows(back_ref, slot, tile, tiles, cells_y):
    return jnp.concatenate(
        [
            back_ref[quad * tiles + tile, slot * QUAD : (slot + 1) * QUAD]
            for quad in range(cells_y // QUAD)
        ],
        axis=0,
    )


def diffusivity(relax_ref, line_ref):
    cells_x, cells_y = relax_ref.shape
    line_ref[...] = jnp.zeros_like(line_ref)
    for x in range(cells_x):
        line_ref[0:1, x * cells_y : (x + 1) * cells_y] = relax_ref[x : x + 1, :]
    return 0.2 / (1.0 + line_ref[0:1, :])


def across_neighbours(m, cells_y):
    cells = m.shape[1]
    y = lax.broadcasted_iota(jnp.int32, m.shape, 1) % cells_y
    yp = jnp.where(y == cells_y - 1, pltpu.roll(m, cells_y - 1, 1), pltpu.roll(m, cells - 1, 1))
    ym = jnp.where(y == 0, pltpu.roll(m, cells - cells_y + 1, 1), pltpu.roll(m, 1, 1))
    return yp, ym


def moments_kernel(
    groups,
    slabs,
    reach_ref,
    run_ref,
    back_ref,
    velocity_ref,
    sign_ref,
    weight_ref,
    relax_ref,
    sent_ref,
    left_ref,
    psi_ref,
    line_ref,
):
    cells_x, cells_y, velocities = reach_ref.shape
    tiles = velocities // LANES
    cells = cells_x * cells_y
    half = left_ref.shape[0] // 2
    me = lax.axis_index("gx")
    from_left = jnp.where(me > 0, 1.0, 0.0)
    from_right = jnp.where(me < slabs - 1, 1.0, 0.0)

    def put(row, value, lanes):
        high = value.astype(jnp.bfloat16)
        low = (value - high.astype(jnp.float32)).astype(jnp.bfloat16)
        left_ref[row : row + cells_y, lanes] = high
        left_ref[half + row : half + row + cells_y, lanes] = low

    psi_ref[...] = jnp.zeros_like(psi_ref)
    for tile in range(tiles):
        lanes = slice(tile * LANES, (tile + 1) * LANES)
        magnitude, positive, cx, cy, cz, square = signed_velocity(velocity_ref, sign_ref, lanes)
        weight = weight_ref[0:1, lanes] / (velocities * groups)
        heat = 0.2 * (square - 2.5)
        moment_rows = [
            jnp.ones_like(cx),
            cx,
            cy,
            cz,
            2.0 / 3.0 * square - 1.0,
            2.0 * cx * cy,
            2.0 * cx * cz,
            2.0 * cy * cz,
            2.0 * (cx * cx - square / 3.0),
            2.0 * (cy * cy - square / 3.0),
            heat * cx,
            heat * cy,
            heat * cz,
            magnitude,
        ]
        for k, row in enumerate(moment_rows):
            value = weight * row
            high = value.astype(jnp.bfloat16).astype(jnp.float32)
            psi_ref[k : k + 1, lanes] = high
            psi_ref[16 + k : 17 + k, lanes] = value - high
        forward = jnp.broadcast_to(positive, (cells_y, LANES))
        entry = whole_rows(back_ref, 0, tile, tiles, cells_y)
        mixed = whole_rows(back_ref, 1, tile, tiles, cells_y)
        near = whole_rows(back_ref, 2, tile, tiles, cells_y)
        near_answer = whole_rows(back_ref, 3, tile, tiles, cells_y)
        answer = jnp.where(forward, mixed, 0.0)
        leaving = jnp.where(forward, 0.0, mixed)
        for x in range(cells_x):
            reach = reach_ref[x, :, lanes]
            put(x * cells_y, reach * entry + run_ref[x, :, lanes], lanes)
            put(cells + x * cells_y, reach * answer, lanes)
        row = 2 * cells
        put(row, jnp.where(forward, entry * from_left, near), lanes)
        put(row + cells_y, jnp.where(forward, near, entry * from_right), lanes)
        put(row + 2 * cells_y, answer * from_left, lanes)
        put(row + 3 * cells_y, near_answer, lanes)
        put(row + 4 * cells_y, leaving, lanes)
        put(row + 5 * cells_y, jnp.where(forward, 1.0, 0.0), lanes)
        put(row + 6 * cells_y, jnp.zeros_like(entry), lanes)
        put(row + 7 * cells_y, jnp.zeros_like(entry), lanes)

    product = lax.dot_general(
        left_ref[...],
        psi_ref[...].astype(jnp.bfloat16),
        (((1,), (1,)), ((), ())),
        preferred_element_type=jnp.float32,
    )
    upper = product[0:half]
    total = upper + pltpu.roll(upper, LANES - 16, 1) + product[half:]
    fixed = total[0:cells].T[0:16]
    answer = total[cells : 2 * cells].T[0:16]
    edges = total[2 * cells : 3 * cells].T[0:16]

    spread = diffusivity(relax_ref, line_ref)
    lane = lax.broadcasted_iota(jnp.int32, (16, cells), 1)

    def along(m, at_left, at_right):
        xm = jnp.where(lane < cells_y, at_left, pltpu.roll(m, cells_y, 1))
        xp = jnp.where(lane >= cells - cells_y, at_right, pltpu.roll(m, cells - cells_y, 1))
        dx = xp - xm
        flow = jnp.concatenate(
            [
                dx[1:2],
                dx[0:1] + dx[4:5] + dx[8:9],
                dx[5:6],
                dx[6:7],
                2.0 / 3.0 * (dx[1:2] + dx[10:11]),
            ],
            axis=0,
        )
        return (xp + xm - 4.0 * m)[0:5], flow

    def across(m):
        yp, ym = across_neighbours(m, cells_y)
        dy = yp - ym
        flow = jnp.concatenate(
            [
                dy[2:3],
                dy[5:6],
                dy[0:1] + dy[4:5] + dy[9:10],
                dy[7:8],
                2.0 / 3.0 * (dy[2:3] + dy[11:12]),
            ],
            axis=0,
        )
        return (yp + ym)[0:5], flow

    shifts = [0, cells - 2 * cells_y, cells - 2 * cells_y, cells - 4 * cells_y]
    placed = [edges if s == 0 else pltpu.roll(edges, s, 1) for s in shifts]
    laplace, flow = along(fixed, placed[0], placed[1])
    laplace_across, flow_across = across(fixed)
    change = spread * (laplace + laplace_across) - 0.25 * (flow + flow_across)
    laplace, flow = along(answer, placed[2], placed[3])
    change_answer = spread * laplace - 0.25 * flow
    message = jnp.concatenate(
        [
            fixed[0:5],
            change,
            answer[0:5],
            answer[5:6],
            answer[7:8],
            answer[9:10],
            answer[11:12],
            change_answer,
            edges[13:14],
            jnp.zeros((SENT_ROWS - 25, cells), jnp.float32),
        ],
        axis=0,
    )
    for group in range(groups):
        sent_ref[group] = message


def finish_kernel(
    parts_ref,
    reach_ref,
    run_ref,
    back_ref,
    velocity_ref,
    sign_ref,
    relax_ref,
    state_ref,
    macro_ref,
    spread_ref,
    line_ref,
):
    cells_x, cells_y, velocities = reach_ref.shape
    groups = parts_ref.shape[0]
    tiles = velocities // LANES
    cells = cells_x * cells_y
    total = parts_ref[0]
    for group in range(1, groups):
        total = total + parts_ref[group]
    lane = lax.broadcasted_iota(jnp.int32, (1, cells), 1)
    sums = total[24:25]
    here = jnp.logical_and(lane >= 4 * cells_y, lane < 5 * cells_y)
    incoming = jnp.where(here, pltpu.roll(sums, cells - cells_y, 1), 1.0)
    rho = jnp.where(here, sums, 0.0) / incoming
    width = cells_y
    while width < cells:
        rho = rho + pltpu.roll(rho, width, 1)
        width *= 2
    answer = rho * total[8:24]
    yp, ym = across_neighbours(answer, cells_y)
    dy = yp - ym
    flow = jnp.concatenate(
        [
            dy[4:5],
            dy[7:8],
            dy[2:3] + dy[6:7] + dy[9:10],
            dy[8:9],
            2.0 / 3.0 * (dy[4:5] + dy[10:11]),
        ],
        axis=0,
    )
    spread = diffusivity(relax_ref, line_ref)
    change = total[5:10] + rho * total[19:24] + spread * (yp + ym)[2:7] - 0.25 * flow
    updated = total[0:5] + answer[2:7] + change
    for x in range(cells_x):
        macro_ref[:, x, :] = updated[:, x * cells_y : (x + 1) * cells_y]
    columns = jnp.concatenate([change, rho, jnp.zeros((2, cells), jnp.float32)], axis=0).T
    for x in range(cells_x):
        for k in range(5):
            spread_ref[k * cells_x + x] = jnp.broadcast_to(
                columns[x * cells_y : (x + 1) * cells_y, k : k + 1], (cells_y, LANES)
            )
    density = jnp.broadcast_to(columns[0:cells_y, 5:6], (cells_y, LANES))
    for tile in range(tiles):
        lanes = slice(tile * LANES, (tile + 1) * LANES)
        _, positive, cx, cy, cz, square = signed_velocity(velocity_ref, sign_ref, lanes)
        basis = [2.0 * cx, 2.0 * cy, 2.0 * cz, square - 1.5]
        forward = jnp.broadcast_to(positive, (cells_y, LANES))
        entry = whole_rows(back_ref, 0, tile, tiles, cells_y)
        mixed = whole_rows(back_ref, 1, tile, tiles, cells_y)
        entry = entry + jnp.where(forward, density * mixed, 0.0)
        for x in range(cells_x):
            value = reach_ref[x, :, lanes] * entry + run_ref[x, :, lanes] + spread_ref[x]
            for k in range(1, 5):
                value = value + spread_ref[k * cells_x + x] * basis[k - 1]
            state_ref[x, :, lanes] = value


def local(state, macro, relax_rate, velocity, vel_sign, quad_weight, freestream, wall_flag):
    cells_x, cells_y, velocities = state.shape
    fields = macro.shape[0]
    slabs = lax.axis_size("gx")
    groups = lax.axis_size("vert")
    cells = cells_x * cells_y
    tiles = velocities // LANES
    assert slabs == tiles * (cells_y // QUAD) and cells == LANES
    f32 = jnp.float32
    sign = vel_sign.reshape(1, velocities)
    weight = quad_weight.reshape(1, velocities)
    wall = wall_flag.reshape(1, cells_y)
    shape = jax.ShapeDtypeStruct

    def call(body, outs, scratch, *args):
        return pl.pallas_call(
            body, out_shape=outs, scratch_shapes=scratch, interpret=INTERPRET
        )(*args)

    reach, run, sent, side = call(
        lambda *refs: maps_kernel(float(cells_x * slabs), *refs),
        (
            shape(state.shape, f32),
            shape(state.shape, f32),
            shape((slabs, 4 * QUAD, LANES), f32),
            shape((slabs, 4 * QUAD, LANES), f32),
        ),
        [
            pltpu.VMEM((fields * cells_x + 2 * cells_x, LANES), f32),
            pltpu.VMEM((fields * cells_x + cells_x + 1, cells_y, LANES), f32),
        ],
        state,
        macro,
        relax_rate,
        velocity,
        sign,
        freestream,
        wall,
    )
    maps = lax.all_to_all(sent, "gx", 0, 0)
    entries = call(
        scan_kernel,
        shape((slabs, 4 * QUAD, LANES), f32),
        [
            pltpu.VMEM((slabs, QUAD, LANES), f32),
            pltpu.VMEM((slabs + 1, QUAD, LANES), f32),
        ],
        maps,
        side,
    )
    back = lax.all_to_all(entries, "gx", 0, 0)
    partial_sums = call(
        lambda *refs: moments_kernel(groups, slabs, *refs),
        shape((groups, SENT_ROWS, cells), f32),
        [
            pltpu.VMEM((6 * cells, velocities), jnp.bfloat16),
            pltpu.VMEM((LANES, velocities), f32),
            pltpu.VMEM((8, cells), f32),
        ],
        reach,
        run,
        back,
        velocity,
        sign,
        weight,
        relax_rate,
    )
    parts = lax.all_to_all(partial_sums, "vert", 0, 0)
    new_state, new_macro = call(
        finish_kernel,
        (shape(state.shape, f32), shape(macro.shape, f32)),
        [pltpu.VMEM((5 * cells_x, cells_y, LANES), f32), pltpu.VMEM((8, cells), f32)],
        parts,
        reach,
        run,
        back,
        velocity,
        sign,
        relax_rate,
    )
    return new_state, new_macro


def solution(mesh):
    return jax.shard_map(
        local,
        mesh=mesh,
        in_specs=(
            P("gx", None, "vert"),
            P(None, "gx", None),
            P("gx", None),
            P(None, "vert"),
            P("vert"),
            P("vert"),
            P(None, "vert"),
            P(),
        ),
        out_specs=(P("gx", None, "vert"), P(None, "gx", None)),
        check_vma=False,
    )
```

```python
import jax
import jax.numpy as jnp
from jax import lax
from jax.experimental import pallas as pl
from jax.experimental.pallas import tpu as pltpu
from jax.sharding import PartitionSpec as P

LANES = 128
QUAD = 4
SENT_ROWS = 32
INTERPRET = False


def signed_velocity(velocity_ref, sign_ref, lanes):
    magnitude = velocity_ref[0:1, lanes]
    positive = sign_ref[0:1, lanes] == 1
    along_x = jnp.where(positive, magnitude, -magnitude)
    along_y = velocity_ref[1:2, lanes]
    along_z = velocity_ref[2:3, lanes]
    square = along_x * along_x + along_y * along_y + along_z * along_z
    return magnitude, positive, along_x, along_y, along_z, square


def maps_kernel(
    total_cells,
    state_ref,
    macro_ref,
    relax_ref,
    velocity_ref,
    sign_ref,
    free_ref,
    wall_ref,
    reach_ref,
    run_ref,
    sent_ref,
    side_ref,
    pad_ref,
    spread_ref,
):
    fields, cells_x, cells_y = macro_ref.shape
    tiles = state_ref.shape[2] // LANES
    pad_ref[...] = jnp.zeros_like(pad_ref)
    for k in range(fields):
        pad_ref[k * cells_x : (k + 1) * cells_x, 0:cells_y] = macro_ref[k]
    base_row = fields * cells_x
    pad_ref[base_row : base_row + cells_x, 0:cells_y] = relax_ref[...]
    wall_row = base_row + cells_x
    pad_ref[wall_row : wall_row + 1, 0:cells_y] = (wall_ref[...] == 1).astype(jnp.float32)
    columns = pad_ref[...].T
    for c in range(wall_row + 1):
        spread_ref[c] = jnp.broadcast_to(columns[0:cells_y, c : c + 1], (cells_y, LANES))
    for tile in range(tiles):
        lanes = slice(tile * LANES, (tile + 1) * LANES)
        magnitude, positive, along_x, along_y, along_z, square = signed_velocity(
            velocity_ref, sign_ref, lanes
        )
        courant = total_cells * magnitude
        base = 1.0 + courant
        basis = [2.0 * along_x, 2.0 * along_y, 2.0 * along_z, square - 1.5]
        for half in range(cells_y // 8):
            rows = slice(half * 8, half * 8 + 8)
            forward = jnp.broadcast_to(positive, (8, LANES))
            decay = []
            driven = []
            for x in range(cells_x):
                relax = spread_ref[base_row + x, rows]
                equil = spread_ref[x, rows]
                for k in range(1, fields):
                    equil = equil + spread_ref[k * cells_x + x, rows] * basis[k - 1]
                inverse = 1.0 / (base + relax)
                decay.append(courant * inverse)
                driven.append((state_ref[x, rows, lanes] + relax * equil) * inverse)
            last = cells_x - 1
            steps = [jnp.where(forward, decay[t], decay[last - t]) for t in range(cells_x)]
            gains = [jnp.where(forward, driven[t], driven[last - t]) for t in range(cells_x)]
            products = [steps[0]]
            runs = [gains[0]]
            for t in range(1, cells_x):
                products.append(steps[t] * products[-1])
                runs.append(steps[t] * runs[-1] + gains[t])
            for x in range(cells_x):
                reach_ref[x, rows, lanes] = jnp.where(forward, products[x], products[last - x])
                run_ref[x, rows, lanes] = jnp.where(forward, runs[x], runs[last - x])
            wall = spread_ref[wall_row, rows] > 0.5
            free = free_ref[rows, lanes]
            diffuse = jnp.logical_and(forward, wall)
            fixed = jnp.where(diffuse, 0.0, free)
            unit = jnp.where(diffuse, 1.0, 0.0)
            direction = jnp.where(forward, 1.0, 0.0)
            for part in range(8 // QUAD):
                owner = (half * (8 // QUAD) + part) * tiles + tile
                quad = slice(part * QUAD, (part + 1) * QUAD)
                for slot, value in enumerate((products[last], runs[last], steps[0], gains[0])):
                    sent_ref[owner, slot * QUAD : (slot + 1) * QUAD, :] = value[quad]
                for slot, value in enumerate((fixed, unit, direction)):
                    side_ref[owner, slot * QUAD : (slot + 1) * QUAD, :] = value[quad]


def scan_kernel(maps_ref, side_ref, sent_ref, entry_ref, near_ref):
    slabs = maps_ref.shape[0]
    me = lax.axis_index("gx")
    side = side_ref[me]
    fixed = side[0:QUAD]
    unit = side[QUAD : 2 * QUAD]
    forward = side[2 * QUAD : 3 * QUAD] > 0.5
    nothing = jnp.zeros_like(fixed)
    value = fixed
    near_ref[0] = nothing
    for i in range(slabs - 1, -1, -1):
        slab = maps_ref[i]
        entry_ref[i] = value
        if i < slabs - 1:
            near_ref[i + 1] = slab[2 * QUAD : 3 * QUAD] * value + slab[3 * QUAD : 4 * QUAD]
        value = slab[0:QUAD] * value + slab[QUAD : 2 * QUAD]
    near_ref[slabs] = slab[2 * QUAD : 3 * QUAD] * entry_ref[0] + slab[3 * QUAD : 4 * QUAD]
    leaving = value
    value = fixed
    answer = unit
    for i in range(slabs):
        slab = maps_ref[i]
        sent_ref[i, 0:QUAD] = jnp.where(forward, value, entry_ref[i])
        sent_ref[i, QUAD : 2 * QUAD] = jnp.where(forward, answer, leaving)
        value = slab[0:QUAD] * value + slab[QUAD : 2 * QUAD]
        answer = slab[0:QUAD] * answer
        upwind = near_ref[i] if i > 0 else nothing
        if i < slabs - 1:
            ahead = maps_ref[i + 1]
            step = ahead[2 * QUAD : 3 * QUAD]
            next_value = step * value + ahead[3 * QUAD : 4 * QUAD]
            next_answer = step * answer
        else:
            next_value = nothing
            next_answer = nothing
        sent_ref[i, 2 * QUAD : 3 * QUAD] = jnp.where(forward, next_value, upwind)
        sent_ref[i, 3 * QUAD : 4 * QUAD] = jnp.where(forward, next_answer, 0.0)


def whole_rows(back_ref, slot, tile, tiles, cells_y):
    return jnp.concatenate(
        [
            back_ref[quad * tiles + tile, slot * QUAD : (slot + 1) * QUAD]
            for quad in range(cells_y // QUAD)
        ],
        axis=0,
    )


def diffusivity(relax_ref, line_ref):
    cells_x, cells_y = relax_ref.shape
    line_ref[...] = jnp.zeros_like(line_ref)
    for x in range(cells_x):
        line_ref[0:1, x * cells_y : (x + 1) * cells_y] = relax_ref[x : x + 1, :]
    return 0.2 / (1.0 + line_ref[0:1, :])


def across_neighbours(m, cells_y):
    cells = m.shape[1]
    y = lax.broadcasted_iota(jnp.int32, m.shape, 1) % cells_y
    yp = jnp.where(y == cells_y - 1, pltpu.roll(m, cells_y - 1, 1), pltpu.roll(m, cells - 1, 1))
    ym = jnp.where(y == 0, pltpu.roll(m, cells - cells_y + 1, 1), pltpu.roll(m, 1, 1))
    return yp, ym


def moments_kernel(
    groups,
    slabs,
    reach_ref,
    run_ref,
    back_ref,
    velocity_ref,
    sign_ref,
    weight_ref,
    relax_ref,
    sent_ref,
    left_ref,
    psi_ref,
    line_ref,
):
    cells_x, cells_y, velocities = reach_ref.shape
    tiles = velocities // LANES
    cells = cells_x * cells_y
    half = left_ref.shape[0] // 2
    me = lax.axis_index("gx")
    from_left = jnp.where(me > 0, 1.0, 0.0)
    from_right = jnp.where(me < slabs - 1, 1.0, 0.0)

    def put(row, value, lanes):
        high = value.astype(jnp.bfloat16)
        low = (value - high.astype(jnp.float32)).astype(jnp.bfloat16)
        left_ref[row : row + cells_y, lanes] = high
        left_ref[half + row : half + row + cells_y, lanes] = low

    psi_ref[...] = jnp.zeros_like(psi_ref)
    for tile in range(tiles):
        lanes = slice(tile * LANES, (tile + 1) * LANES)
        magnitude, positive, cx, cy, cz, square = signed_velocity(velocity_ref, sign_ref, lanes)
        weight = weight_ref[0:1, lanes] / (velocities * groups)
        heat = 0.2 * (square - 2.5)
        moment_rows = [
            jnp.ones_like(cx),
            cx,
            cy,
            cz,
            2.0 / 3.0 * square - 1.0,
            2.0 * cx * cy,
            2.0 * cx * cz,
            2.0 * cy * cz,
            2.0 * (cx * cx - square / 3.0),
            2.0 * (cy * cy - square / 3.0),
            heat * cx,
            heat * cy,
            heat * cz,
            magnitude,
        ]
        for k, row in enumerate(moment_rows):
            value = weight * row
            high = value.astype(jnp.bfloat16).astype(jnp.float32)
            psi_ref[k : k + 1, lanes] = high
            psi_ref[16 + k : 17 + k, lanes] = value - high
        forward = jnp.broadcast_to(positive, (cells_y, LANES))
        entry = whole_rows(back_ref, 0, tile, tiles, cells_y)
        mixed = whole_rows(back_ref, 1, tile, tiles, cells_y)
        near = whole_rows(back_ref, 2, tile, tiles, cells_y)
        near_answer = whole_rows(back_ref, 3, tile, tiles, cells_y)
        answer = jnp.where(forward, mixed, 0.0)
        leaving = jnp.where(forward, 0.0, mixed)
        for x in range(cells_x):
            reach = reach_ref[x, :, lanes]
            put(x * cells_y, reach * entry + run_ref[x, :, lanes], lanes)
            put(cells + x * cells_y, reach * answer, lanes)
        row = 2 * cells
        put(row, jnp.where(forward, entry * from_left, near), lanes)
        put(row + cells_y, jnp.where(forward, near, entry * from_right), lanes)
        put(row + 2 * cells_y, answer * from_left, lanes)
        put(row + 3 * cells_y, near_answer, lanes)
        put(row + 4 * cells_y, leaving, lanes)
        put(row + 5 * cells_y, jnp.where(forward, 1.0, 0.0), lanes)
        put(row + 6 * cells_y, jnp.zeros_like(entry), lanes)
        put(row + 7 * cells_y, jnp.zeros_like(entry), lanes)

    product = lax.dot_general(
        left_ref[...],
        psi_ref[...].astype(jnp.bfloat16),
        (((1,), (1,)), ((), ())),
        preferred_element_type=jnp.float32,
    )
    upper = product[0:half]
    total = upper + pltpu.roll(upper, LANES - 16, 1) + product[half:]
    fixed = total[0:cells].T[0:16]
    answer = total[cells : 2 * cells].T[0:16]
    edges = total[2 * cells : 3 * cells].T[0:16]

    spread = diffusivity(relax_ref, line_ref)
    lane = lax.broadcasted_iota(jnp.int32, (16, cells), 1)

    def along(m, at_left, at_right):
        xm = jnp.where(lane < cells_y, at_left, pltpu.roll(m, cells_y, 1))
        xp = jnp.where(lane >= cells - cells_y, at_right, pltpu.roll(m, cells - cells_y, 1))
        dx = xp - xm
        flow = jnp.concatenate(
            [
                dx[1:2],
                dx[0:1] + dx[4:5] + dx[8:9],
                dx[5:6],
                dx[6:7],
                2.0 / 3.0 * (dx[1:2] + dx[10:11]),
            ],
            axis=0,
        )
        return (xp + xm - 4.0 * m)[0:5], flow

    def across(m):
        yp, ym = across_neighbours(m, cells_y)
        dy = yp - ym
        flow = jnp.concatenate(
            [
                dy[2:3],
                dy[5:6],
                dy[0:1] + dy[4:5] + dy[9:10],
                dy[7:8],
                2.0 / 3.0 * (dy[2:3] + dy[11:12]),
            ],
            axis=0,
        )
        return (yp + ym)[0:5], flow

    shifts = [0, cells - 2 * cells_y, cells - 2 * cells_y, cells - 4 * cells_y]
    placed = [edges if s == 0 else pltpu.roll(edges, s, 1) for s in shifts]
    laplace, flow = along(fixed, placed[0], placed[1])
    laplace_across, flow_across = across(fixed)
    change = spread * (laplace + laplace_across) - 0.25 * (flow + flow_across)
    laplace, flow = along(answer, placed[2], placed[3])
    change_answer = spread * laplace - 0.25 * flow
    message = jnp.concatenate(
        [
            fixed[0:5],
            change,
            answer[0:5],
            answer[5:6],
            answer[7:8],
            answer[9:10],
            answer[11:12],
            change_answer,
            edges[13:14],
            jnp.zeros((SENT_ROWS - 25, cells), jnp.float32),
        ],
        axis=0,
    )
    for group in range(groups):
        sent_ref[group] = message


def finish_kernel(
    parts_ref,
    reach_ref,
    run_ref,
    back_ref,
    velocity_ref,
    sign_ref,
    relax_ref,
    state_ref,
    macro_ref,
    spread_ref,
    line_ref,
):
    cells_x, cells_y, velocities = reach_ref.shape
    groups = parts_ref.shape[0]
    tiles = velocities // LANES
    cells = cells_x * cells_y
    total = parts_ref[0]
    for group in range(1, groups):
        total = total + parts_ref[group]
    lane = lax.broadcasted_iota(jnp.int32, (1, cells), 1)
    sums = total[24:25]
    here = jnp.logical_and(lane >= 4 * cells_y, lane < 5 * cells_y)
    incoming = jnp.where(here, pltpu.roll(sums, cells - cells_y, 1), 1.0)
    rho = jnp.where(here, sums, 0.0) / incoming
    width = cells_y
    while width < cells:
        rho = rho + pltpu.roll(rho, width, 1)
        width *= 2
    answer = rho * total[8:24]
    yp, ym = across_neighbours(answer, cells_y)
    dy = yp - ym
    flow = jnp.concatenate(
        [
            dy[4:5],
            dy[7:8],
            dy[2:3] + dy[6:7] + dy[9:10],
            dy[8:9],
            2.0 / 3.0 * (dy[4:5] + dy[10:11]),
        ],
        axis=0,
    )
    spread = diffusivity(relax_ref, line_ref)
    change = total[5:10] + rho * total[19:24] + spread * (yp + ym)[2:7] - 0.25 * flow
    updated = total[0:5] + answer[2:7] + change
    for x in range(cells_x):
        macro_ref[:, x, :] = updated[:, x * cells_y : (x + 1) * cells_y]
    columns = jnp.concatenate([change, rho, jnp.zeros((2, cells), jnp.float32)], axis=0).T
    for x in range(cells_x):
        for k in range(5):
            spread_ref[k * cells_x + x] = jnp.broadcast_to(
                columns[x * cells_y : (x + 1) * cells_y, k : k + 1], (cells_y, LANES)
            )
    density = jnp.broadcast_to(columns[0:cells_y, 5:6], (cells_y, LANES))
    for tile in range(tiles):
        lanes = slice(tile * LANES, (tile + 1) * LANES)
        _, positive, cx, cy, cz, square = signed_velocity(velocity_ref, sign_ref, lanes)
        basis = [2.0 * cx, 2.0 * cy, 2.0 * cz, square - 1.5]
        forward = jnp.broadcast_to(positive, (cells_y, LANES))
        entry = whole_rows(back_ref, 0, tile, tiles, cells_y)
        mixed = whole_rows(back_ref, 1, tile, tiles, cells_y)
        entry = entry + jnp.where(forward, density * mixed, 0.0)
        for x in range(cells_x):
            value = reach_ref[x, :, lanes] * entry + run_ref[x, :, lanes] + spread_ref[x]
            for k in range(1, 5):
                value = value + spread_ref[k * cells_x + x] * basis[k - 1]
            state_ref[x, :, lanes] = value


def local(state, macro, relax_rate, velocity, vel_sign, quad_weight, freestream, wall_flag):
    cells_x, cells_y, velocities = state.shape
    fields = macro.shape[0]
    slabs = lax.axis_size("gx")
    groups = lax.axis_size("vert")
    cells = cells_x * cells_y
    tiles = velocities // LANES
    assert slabs == tiles * (cells_y // QUAD) and cells == LANES
    f32 = jnp.float32
    sign = vel_sign.reshape(1, velocities)
    weight = quad_weight.reshape(1, velocities)
    wall = wall_flag.reshape(1, cells_y)
    shape = jax.ShapeDtypeStruct
    near = shape if INTERPRET else pltpu.VMEM

    def held(x):
        return x if INTERPRET else pltpu.with_memory_space_constraint(x, pltpu.VMEM)

    def call(body, outs, scratch, *args):
        return pl.pallas_call(
            body, out_shape=outs, scratch_shapes=scratch, interpret=INTERPRET
        )(*args)

    reach, run, sent, side = call(
        lambda *refs: maps_kernel(float(cells_x * slabs), *refs),
        (
            near(state.shape, f32),
            near(state.shape, f32),
            near((slabs, 4 * QUAD, LANES), f32),
            near((slabs, 4 * QUAD, LANES), f32),
        ),
        [
            pltpu.VMEM((fields * cells_x + 2 * cells_x, LANES), f32),
            pltpu.VMEM((fields * cells_x + cells_x + 1, cells_y, LANES), f32),
        ],
        state,
        macro,
        relax_rate,
        velocity,
        sign,
        freestream,
        wall,
    )
    reach, run, side = (held(value) for value in (reach, run, side))
    maps = held(lax.all_to_all(sent, "gx", 0, 0))
    entries = call(
        scan_kernel,
        near((slabs, 4 * QUAD, LANES), f32),
        [
            pltpu.VMEM((slabs, QUAD, LANES), f32),
            pltpu.VMEM((slabs + 1, QUAD, LANES), f32),
        ],
        maps,
        side,
    )
    back = held(lax.all_to_all(entries, "gx", 0, 0))
    partial_sums = call(
        lambda *refs: moments_kernel(groups, slabs, *refs),
        near((groups, SENT_ROWS, cells), f32),
        [
            pltpu.VMEM((6 * cells, velocities), jnp.bfloat16),
            pltpu.VMEM((LANES, velocities), f32),
            pltpu.VMEM((8, cells), f32),
        ],
        reach,
        run,
        back,
        velocity,
        sign,
        weight,
        relax_rate,
    )
    parts = held(lax.all_to_all(partial_sums, "vert", 0, 0))
    new_state, new_macro = call(
        finish_kernel,
        (shape(state.shape, f32), shape(macro.shape, f32)),
        [pltpu.VMEM((5 * cells_x, cells_y, LANES), f32), pltpu.VMEM((8, cells), f32)],
        parts,
        reach,
        run,
        back,
        velocity,
        sign,
        relax_rate,
    )
    return new_state, new_macro


def solution(mesh):
    return jax.shard_map(
        local,
        mesh=mesh,
        in_specs=(
            P("gx", None, "vert"),
            P(None, "gx", None),
            P("gx", None),
            P(None, "vert"),
            P("vert"),
            P("vert"),
            P(None, "vert"),
            P(),
        ),
        out_specs=(P("gx", None, "vert"), P(None, "gx", None)),
        check_vma=False,
    )
```

```python
import jax
import jax.numpy as jnp
from jax import lax
from jax.experimental import pallas as pl
from jax.experimental.pallas import tpu as pltpu
from jax.sharding import PartitionSpec as P

LANES = 128
QUAD = 4
SENT_PARTS = 7
INTERPRET = False


def maps_kernel(
    total_cells,
    groups,
    state_hbm,
    macro_hbm,
    relax_hbm,
    velocity_hbm,
    sign_hbm,
    weight_hbm,
    free_hbm,
    wall_hbm,
    reach_ref,
    run_ref,
    sent_ref,
    side_ref,
    psi_ref,
    table_ref,
    line_ref,
    state_ref,
    macro_ref,
    relax_ref,
    velocity_ref,
    sign_ref,
    weight_ref,
    free_ref,
    wall_ref,
    pad_ref,
    spread_ref,
    sems,
):
    fields, cells_x, cells_y = macro_ref.shape
    velocities = state_ref.shape[2]
    tiles = velocities // LANES
    halves = cells_y // 8
    small = [
        pltpu.make_async_copy(source, target, sems.at[halves + n])
        for n, (source, target) in enumerate(
            (
                (velocity_hbm, velocity_ref),
                (sign_hbm, sign_ref),
                (weight_hbm, weight_ref),
                (macro_hbm, macro_ref),
                (relax_hbm, relax_ref),
                (wall_hbm, wall_ref),
                (free_hbm, free_ref),
            )
        )
    ]
    large = [
        pltpu.make_async_copy(
            state_hbm.at[:, pl.ds(half * 8, 8), :],
            state_ref.at[:, pl.ds(half * 8, 8), :],
            sems.at[half],
        )
        for half in range(halves)
    ]
    for copy in small + large:
        copy.start()
    pad_ref[...] = jnp.zeros_like(pad_ref)
    psi_ref[...] = jnp.zeros_like(psi_ref)
    table_ref[...] = jnp.zeros_like(table_ref)
    line_ref[...] = jnp.zeros_like(line_ref)
    for copy in small:
        copy.wait()
    for k in range(fields):
        pad_ref[k * cells_x : (k + 1) * cells_x, 0:cells_y] = macro_ref[k]
    base_row = fields * cells_x
    pad_ref[base_row : base_row + cells_x, 0:cells_y] = relax_ref[...]
    wall_row = base_row + cells_x
    pad_ref[wall_row : wall_row + 1, 0:cells_y] = (wall_ref[...] == 1).astype(jnp.float32)
    columns = pad_ref[...].T
    for c in range(wall_row + 1):
        spread_ref[c] = jnp.broadcast_to(columns[0:cells_y, c : c + 1], (cells_y, LANES))
    for x in range(cells_x):
        line_ref[0:1, x * cells_y : (x + 1) * cells_y] = relax_ref[x : x + 1, :]
    line_ref[0:1, :] = 0.2 / (1.0 + line_ref[0:1, :])

    magnitude = velocity_ref[0:1, :]
    positive = sign_ref[...] == 1
    cx = jnp.where(positive, magnitude, -magnitude)
    cy = velocity_ref[1:2, :]
    cz = velocity_ref[2:3, :]
    square = cx * cx + cy * cy + cz * cz
    for k, row in enumerate(
        (
            2.0 * cx,
            2.0 * cy,
            2.0 * cz,
            square - 1.5,
            jnp.where(positive, 1.0, 0.0),
            total_cells * magnitude,
        )
    ):
        table_ref[k : k + 1, :] = row
    weight = weight_ref[...] / (velocities * groups)
    heat = 0.2 * (square - 2.5)
    for k, row in enumerate(
        (
            jnp.ones_like(cx),
            cx,
            cy,
            cz,
            2.0 / 3.0 * square - 1.0,
            2.0 * cx * cy,
            2.0 * cx * cz,
            2.0 * cy * cz,
            2.0 * (cx * cx - square / 3.0),
            2.0 * (cy * cy - square / 3.0),
            heat * cx,
            heat * cy,
            heat * cz,
            magnitude,
        )
    ):
        value = weight * row
        high = value.astype(jnp.bfloat16).astype(jnp.float32)
        psi_ref[k : k + 1, :] = high
        psi_ref[16 + k : 17 + k, :] = value - high

    last = cells_x - 1
    for half in range(halves):
        large[half].wait()
        rows = slice(half * 8, half * 8 + 8)
        for tile in range(tiles):
            lanes = slice(tile * LANES, (tile + 1) * LANES)
            forward = jnp.broadcast_to(table_ref[4:5, lanes], (8, LANES)) > 0.5
            courant = jnp.broadcast_to(table_ref[5:6, lanes], (8, LANES))
            base = 1.0 + courant
            basis = [jnp.broadcast_to(table_ref[k : k + 1, lanes], (8, LANES)) for k in range(4)]
            decay = []
            driven = []
            for x in range(cells_x):
                relax = spread_ref[base_row + x, rows]
                equil = spread_ref[x, rows]
                for k in range(1, fields):
                    equil = equil + spread_ref[k * cells_x + x, rows] * basis[k - 1]
                inverse = 1.0 / (base + relax)
                decay.append(courant * inverse)
                driven.append((state_ref[x, rows, lanes] + relax * equil) * inverse)
            steps = [jnp.where(forward, decay[t], decay[last - t]) for t in range(cells_x)]
            gains = [jnp.where(forward, driven[t], driven[last - t]) for t in range(cells_x)]
            products = [steps[0]]
            runs = [gains[0]]
            for t in range(1, cells_x):
                products.append(steps[t] * products[-1])
                runs.append(steps[t] * runs[-1] + gains[t])
            for x in range(cells_x):
                reach_ref[x, rows, lanes] = jnp.where(forward, products[x], products[last - x])
                run_ref[x, rows, lanes] = jnp.where(forward, runs[x], runs[last - x])
            wall = spread_ref[wall_row, rows] > 0.5
            diffuse = jnp.logical_and(forward, wall)
            fixed = jnp.where(diffuse, 0.0, free_ref[rows, lanes])
            unit = jnp.where(diffuse, 1.0, 0.0)
            direction = jnp.where(forward, 1.0, 0.0)
            for part in range(8 // QUAD):
                owner = (half * (8 // QUAD) + part) * tiles + tile
                quad = slice(part * QUAD, (part + 1) * QUAD)
                for slot, value in enumerate((products[last], runs[last], steps[0], gains[0])):
                    sent_ref[owner, slot * QUAD : (slot + 1) * QUAD, :] = value[quad]
                for slot, value in enumerate((fixed, unit, direction)):
                    side_ref[owner, slot * QUAD : (slot + 1) * QUAD, :] = value[quad]


def scan_kernel(maps_ref, side_ref, sent_ref, entry_ref, near_ref):
    slabs = maps_ref.shape[0]
    me = lax.axis_index("gx")
    side = side_ref[me]
    fixed = side[0:QUAD]
    unit = side[QUAD : 2 * QUAD]
    forward = side[2 * QUAD : 3 * QUAD] > 0.5
    nothing = jnp.zeros_like(fixed)
    value = fixed
    near_ref[0] = nothing
    for i in range(slabs - 1, -1, -1):
        slab = maps_ref[i]
        entry_ref[i] = value
        if i < slabs - 1:
            near_ref[i + 1] = slab[2 * QUAD : 3 * QUAD] * value + slab[3 * QUAD : 4 * QUAD]
        value = slab[0:QUAD] * value + slab[QUAD : 2 * QUAD]
    near_ref[slabs] = slab[2 * QUAD : 3 * QUAD] * entry_ref[0] + slab[3 * QUAD : 4 * QUAD]
    leaving = value
    value = fixed
    answer = unit
    for i in range(slabs):
        slab = maps_ref[i]
        sent_ref[i, 0:QUAD] = jnp.where(forward, value, entry_ref[i])
        sent_ref[i, QUAD : 2 * QUAD] = jnp.where(forward, answer, leaving)
        value = slab[0:QUAD] * value + slab[QUAD : 2 * QUAD]
        answer = slab[0:QUAD] * answer
        upwind = near_ref[i] if i > 0 else nothing
        if i < slabs - 1:
            ahead = maps_ref[i + 1]
            step = ahead[2 * QUAD : 3 * QUAD]
            next_value = step * value + ahead[3 * QUAD : 4 * QUAD]
            next_answer = step * answer
        else:
            next_value = nothing
            next_answer = nothing
        sent_ref[i, 2 * QUAD : 3 * QUAD] = jnp.where(forward, next_value, upwind)
        sent_ref[i, 3 * QUAD : 4 * QUAD] = jnp.where(forward, next_answer, 0.0)


def whole_rows(back_ref, slot, tile, tiles, cells_y):
    return jnp.concatenate(
        [
            back_ref[quad * tiles + tile, slot * QUAD : (slot + 1) * QUAD]
            for quad in range(cells_y // QUAD)
        ],
        axis=0,
    )


def across_neighbours(m, cells_y):
    cells = m.shape[1]
    y = lax.broadcasted_iota(jnp.int32, m.shape, 1) % cells_y
    yp = jnp.where(y == cells_y - 1, pltpu.roll(m, cells_y - 1, 1), pltpu.roll(m, cells - 1, 1))
    ym = jnp.where(y == 0, pltpu.roll(m, cells - cells_y + 1, 1), pltpu.roll(m, 1, 1))
    return yp, ym


def moments_kernel(
    groups, slabs, reach_ref, run_ref, back_ref, psi_ref, table_ref, line_ref, sent_ref, left_ref
):
    cells_x, cells_y, velocities = reach_ref.shape
    tiles = velocities // LANES
    cells = cells_x * cells_y
    half = left_ref.shape[0] // 2
    me = lax.axis_index("gx")
    from_left = jnp.where(me > 0, 1.0, 0.0)
    from_right = jnp.where(me < slabs - 1, 1.0, 0.0)

    def put(row, value, lanes):
        high = value.astype(jnp.bfloat16)
        low = (value - high.astype(jnp.float32)).astype(jnp.bfloat16)
        left_ref[row : row + cells_y, lanes] = high
        left_ref[half + row : half + row + cells_y, lanes] = low

    for tile in range(tiles):
        lanes = slice(tile * LANES, (tile + 1) * LANES)
        positive = table_ref[4:5, lanes] > 0.5
        forward = jnp.broadcast_to(positive, (cells_y, LANES))
        entry = whole_rows(back_ref, 0, tile, tiles, cells_y)
        mixed = whole_rows(back_ref, 1, tile, tiles, cells_y)
        near = whole_rows(back_ref, 2, tile, tiles, cells_y)
        near_answer = whole_rows(back_ref, 3, tile, tiles, cells_y)
        answer = jnp.where(forward, mixed, 0.0)
        leaving = jnp.where(forward, 0.0, mixed)
        for x in range(cells_x):
            reach = reach_ref[x, :, lanes]
            put(x * cells_y, reach * entry + run_ref[x, :, lanes], lanes)
            put(cells + x * cells_y, reach * answer, lanes)
        row = 2 * cells
        put(row, jnp.where(forward, entry * from_left, near), lanes)
        put(row + cells_y, jnp.where(forward, near, entry * from_right), lanes)
        put(row + 2 * cells_y, answer * from_left, lanes)
        put(row + 3 * cells_y, near_answer, lanes)
        put(row + 4 * cells_y, leaving, lanes)
        put(row + 5 * cells_y, jnp.where(forward, 1.0, 0.0), lanes)
        put(row + 6 * cells_y, jnp.zeros_like(entry), lanes)
        put(row + 7 * cells_y, jnp.zeros_like(entry), lanes)

    product = lax.dot_general(
        left_ref[...],
        psi_ref[...].astype(jnp.bfloat16),
        (((1,), (1,)), ((), ())),
        preferred_element_type=jnp.float32,
    )
    upper = product[0:half]
    total = upper[:, 0:16] + upper[:, 16:32] + product[half:, 0:16]
    fixed = total[0:cells].T
    answer = total[cells : 2 * cells].T
    edges = total[2 * cells : 3 * cells].T

    spread = line_ref[0:1, :]
    lane = lax.broadcasted_iota(jnp.int32, (16, cells), 1)

    def along(m, at_left, at_right):
        xm = jnp.where(lane < cells_y, at_left, pltpu.roll(m, cells_y, 1))
        xp = jnp.where(lane >= cells - cells_y, at_right, pltpu.roll(m, cells - cells_y, 1))
        dx = xp - xm
        flow = jnp.concatenate(
            [
                dx[1:2],
                dx[0:1] + dx[4:5] + dx[8:9],
                dx[5:6],
                dx[6:7],
                2.0 / 3.0 * (dx[1:2] + dx[10:11]),
            ],
            axis=0,
        )
        return (xp + xm - 4.0 * m)[0:5], flow

    def across(m):
        yp, ym = across_neighbours(m, cells_y)
        dy = yp - ym
        flow = jnp.concatenate(
            [
                dy[2:3],
                dy[5:6],
                dy[0:1] + dy[4:5] + dy[9:10],
                dy[7:8],
                2.0 / 3.0 * (dy[2:3] + dy[11:12]),
            ],
            axis=0,
        )
        return (yp + ym)[0:5], flow

    shifts = [0, cells - 2 * cells_y, cells - 2 * cells_y, cells - 4 * cells_y]
    placed = [edges if s == 0 else pltpu.roll(edges, s, 1) for s in shifts]
    laplace, flow = along(fixed, placed[0], placed[1])
    laplace_across, flow_across = across(fixed)
    change = spread * (laplace + laplace_across) - 0.25 * (flow + flow_across)
    laplace, flow = along(answer, placed[2], placed[3])
    change_answer = spread * laplace - 0.25 * flow
    message = [
        fixed[0:5],
        change,
        answer[0:5],
        answer[5:6],
        answer[7:8],
        answer[9:10],
        answer[11:12],
        change_answer,
        edges[13:14],
    ]
    spare = QUAD * (sent_ref.shape[2] // cells) - 25
    message = jnp.concatenate(message + [jnp.zeros((spare, cells), jnp.float32)], axis=0)
    for part in range(sent_ref.shape[2] // cells):
        piece = message[part * QUAD : (part + 1) * QUAD]
        for group in range(groups):
            sent_ref[group, :, part * cells : (part + 1) * cells] = piece


def finish_kernel(
    parts_ref,
    reach_ref,
    run_ref,
    back_ref,
    table_ref,
    line_ref,
    state_hbm,
    macro_hbm,
    state_ref,
    macro_ref,
    spread_ref,
    entry_ref,
    sems,
):
    cells_x, cells_y, velocities = reach_ref.shape
    groups = parts_ref.shape[0]
    tiles = velocities // LANES
    cells = cells_x * cells_y
    sums = [parts_ref[group] for group in range(groups)]
    while len(sums) > 1:
        sums = [sums[n] + sums[n + 1] for n in range(0, len(sums), 2)]
    total = jnp.concatenate(
        [sums[0][:, n * cells : (n + 1) * cells] for n in range(parts_ref.shape[2] // cells)],
        axis=0,
    )
    lane = lax.broadcasted_iota(jnp.int32, (1, cells), 1)
    sums = total[24:25]
    here = jnp.logical_and(lane >= 4 * cells_y, lane < 5 * cells_y)
    incoming = jnp.where(here, pltpu.roll(sums, cells - cells_y, 1), 1.0)
    rho = jnp.where(here, sums, 0.0) / incoming
    width = cells_y
    while width < cells:
        rho = rho + pltpu.roll(rho, width, 1)
        width *= 2
    answer = rho * total[8:24]
    yp, ym = across_neighbours(answer, cells_y)
    dy = yp - ym
    flow = jnp.concatenate(
        [
            dy[4:5],
            dy[7:8],
            dy[2:3] + dy[6:7] + dy[9:10],
            dy[8:9],
            2.0 / 3.0 * (dy[4:5] + dy[10:11]),
        ],
        axis=0,
    )
    spread = line_ref[0:1, :]
    change = total[5:10] + rho * total[19:24] + spread * (yp + ym)[2:7] - 0.25 * flow
    updated = total[0:5] + answer[2:7] + change
    for x in range(cells_x):
        macro_ref[:, x, :] = updated[:, x * cells_y : (x + 1) * cells_y]
    macro_copy = pltpu.make_async_copy(macro_ref, macro_hbm, sems.at[cells_x])
    macro_copy.start()
    columns = jnp.concatenate([change, rho, jnp.zeros((2, cells), jnp.float32)], axis=0).T
    for x in range(cells_x):
        for k in range(5):
            spread_ref[k * cells_x + x] = jnp.broadcast_to(
                columns[x * cells_y : (x + 1) * cells_y, k : k + 1], (cells_y, LANES)
            )
    density = jnp.broadcast_to(columns[0:cells_y, 5:6], (cells_y, LANES))
    for tile in range(tiles):
        lanes = slice(tile * LANES, (tile + 1) * LANES)
        forward = jnp.broadcast_to(table_ref[4:5, lanes], (cells_y, LANES)) > 0.5
        entry = whole_rows(back_ref, 0, tile, tiles, cells_y)
        mixed = whole_rows(back_ref, 1, tile, tiles, cells_y)
        entry_ref[:, lanes] = entry + jnp.where(forward, density * mixed, 0.0)
    copies = []
    span = 2
    for first in range(0, cells_x, span):
        for tile in range(tiles):
            lanes = slice(tile * LANES, (tile + 1) * LANES)
            basis = [table_ref[k : k + 1, lanes] for k in range(4)]
            entry = entry_ref[:, lanes]
            for x in range(first, first + span):
                value = reach_ref[x, :, lanes] * entry + run_ref[x, :, lanes] + spread_ref[x]
                for k in range(1, 5):
                    value = value + spread_ref[k * cells_x + x] * basis[k - 1]
                state_ref[x, :, lanes] = value
        copy = pltpu.make_async_copy(
            state_ref.at[pl.ds(first, span)], state_hbm.at[pl.ds(first, span)], sems.at[first]
        )
        copy.start()
        copies.append(copy)
    for copy in copies + [macro_copy]:
        copy.wait()


def local(state, macro, relax_rate, velocity, vel_sign, quad_weight, freestream, wall_flag):
    cells_x, cells_y, velocities = state.shape
    fields = macro.shape[0]
    slabs = lax.axis_size("gx")
    groups = lax.axis_size("vert")
    cells = cells_x * cells_y
    tiles = velocities // LANES
    assert slabs == tiles * (cells_y // QUAD) and cells == LANES
    f32 = jnp.float32
    sign = vel_sign.reshape(1, velocities)
    weight = quad_weight.reshape(1, velocities)
    wall = wall_flag.reshape(1, cells_y)
    shape = jax.ShapeDtypeStruct
    near = shape if INTERPRET else pltpu.VMEM

    def held(x):
        return x if INTERPRET else pltpu.with_memory_space_constraint(x, pltpu.VMEM)

    def call(body, outs, scratch, *args, **kwargs):
        return pl.pallas_call(
            body, out_shape=outs, scratch_shapes=scratch, interpret=INTERPRET, **kwargs
        )(*args)

    anywhere = pl.BlockSpec(memory_space=pl.ANY)
    sources = (state, macro, relax_rate, velocity, sign, weight, freestream, wall)
    exchanged = near((slabs, 4 * QUAD, LANES), f32)
    reach, run, sent, side, psi, table, line = call(
        lambda *refs: maps_kernel(float(cells_x * slabs), groups, *refs),
        (
            near(state.shape, f32),
            near(state.shape, f32),
            exchanged,
            exchanged,
            near((32, velocities), f32),
            near((8, velocities), f32),
            near((8, cells), f32),
        ),
        [pltpu.VMEM(value.shape, value.dtype) for value in sources]
        + [
            pltpu.VMEM((fields * cells_x + 2 * cells_x, LANES), f32),
            pltpu.VMEM((fields * cells_x + cells_x + 1, cells_y, LANES), f32),
            pltpu.SemaphoreType.DMA((cells_y // 8 + 7,)),
        ],
        *sources,
        in_specs=[anywhere] * len(sources),
    )
    reach, run, side, psi, table, line = map(held, (reach, run, side, psi, table, line))
    maps = held(lax.all_to_all(sent, "gx", 0, 0))
    entries = call(
        scan_kernel,
        exchanged,
        [
            pltpu.VMEM((slabs, QUAD, LANES), f32),
            pltpu.VMEM((slabs + 1, QUAD, LANES), f32),
        ],
        maps,
        side,
    )
    back = held(lax.all_to_all(entries, "gx", 0, 0))
    partial_sums = call(
        lambda *refs: moments_kernel(groups, slabs, *refs),
        near((groups, QUAD, SENT_PARTS * cells), f32),
        [pltpu.VMEM((6 * cells, velocities), jnp.bfloat16)],
        reach,
        run,
        back,
        psi,
        table,
        line,
    )
    parts = held(lax.all_to_all(partial_sums, "vert", 0, 0))
    new_state, new_macro = call(
        finish_kernel,
        (shape(state.shape, f32), shape(macro.shape, f32)),
        [
            pltpu.VMEM(state.shape, f32),
            pltpu.VMEM(macro.shape, f32),
            pltpu.VMEM((5 * cells_x, cells_y, LANES), f32),
            pltpu.VMEM((cells_y, velocities), f32),
            pltpu.SemaphoreType.DMA((cells_x + 1,)),
        ],
        parts,
        reach,
        run,
        back,
        table,
        line,
        out_specs=(anywhere, anywhere),
    )
    return new_state, new_macro


def solution(mesh):
    return jax.shard_map(
        local,
        mesh=mesh,
        in_specs=(
            P("gx", None, "vert"),
            P(None, "gx", None),
            P("gx", None),
            P(None, "vert"),
            P("vert"),
            P("vert"),
            P(None, "vert"),
            P(),
        ),
        out_specs=(P("gx", None, "vert"), P(None, "gx", None)),
        check_vma=False,
    )
```

```python
import jax
import jax.numpy as jnp
from jax import lax
from jax.experimental import pallas as pl
from jax.experimental.pallas import tpu as pltpu
from jax.sharding import PartitionSpec as P

LANES = 128
QUAD = 4
SENT_PARTS = 7
INTERPRET = False


def maps_kernel(
    total_cells,
    groups,
    state_hbm,
    macro_hbm,
    relax_hbm,
    velocity_hbm,
    sign_hbm,
    weight_hbm,
    free_hbm,
    wall_hbm,
    reach_ref,
    run_ref,
    sent_ref,
    side_ref,
    psi_ref,
    table_ref,
    line_ref,
    state_ref,
    macro_ref,
    relax_ref,
    velocity_ref,
    sign_ref,
    weight_ref,
    free_ref,
    wall_ref,
    pad_ref,
    spread_ref,
    rows_ref,
    sems,
):
    fields, cells_x, cells_y = macro_ref.shape
    velocities = state_ref.shape[2]
    tiles = velocities // LANES
    halves = cells_y // 8
    small = [
        pltpu.make_async_copy(source, target, sems.at[halves + n])
        for n, (source, target) in enumerate(
            (
                (velocity_hbm, velocity_ref),
                (sign_hbm, sign_ref),
                (weight_hbm, weight_ref),
                (macro_hbm, macro_ref),
                (relax_hbm, relax_ref),
                (wall_hbm, wall_ref),
                (free_hbm, free_ref),
            )
        )
    ]
    large = [
        pltpu.make_async_copy(
            state_hbm.at[:, pl.ds(half * 8, 8), :],
            state_ref.at[:, pl.ds(half * 8, 8), :],
            sems.at[half],
        )
        for half in range(halves)
    ]
    for copy in large + small:
        copy.start()
    pad_ref[...] = jnp.zeros_like(pad_ref)
    psi_ref[...] = jnp.zeros_like(psi_ref)
    table_ref[...] = jnp.zeros_like(table_ref)
    line_ref[...] = jnp.zeros_like(line_ref)
    rows_ref[...] = jnp.zeros_like(rows_ref)
    for copy in small:
        copy.wait()
    for k in range(fields):
        pad_ref[k * cells_x : (k + 1) * cells_x, 0:cells_y] = macro_ref[k]
    base_row = fields * cells_x
    pad_ref[base_row : base_row + cells_x, 0:cells_y] = relax_ref[...]
    wall_row = base_row + cells_x
    pad_ref[wall_row : wall_row + 1, 0:cells_y] = (wall_ref[...] == 1).astype(jnp.float32)
    columns = pad_ref[...].T
    for c in range(wall_row + 1):
        spread_ref[c] = jnp.broadcast_to(columns[0:cells_y, c : c + 1], (cells_y, LANES))
    for x in range(cells_x):
        line_ref[0:1, x * cells_y : (x + 1) * cells_y] = relax_ref[x : x + 1, :]
    line_ref[0:1, :] = 0.2 / (1.0 + line_ref[0:1, :])
    quads = cells_y // QUAD
    for x in range(cells_x):
        for quad in range(quads):
            rows_ref[quad : quad + 1, x * QUAD : (x + 1) * QUAD] = relax_ref[
                x : x + 1, quad * QUAD : (quad + 1) * QUAD
            ]
    rows_ref[quads : quads + 1, 0:cells_y] = relax_ref[0:1, :]
    rows_ref[quads : quads + 1, cells_y : 2 * cells_y] = relax_ref[cells_x - 1 : cells_x, :]

    magnitude = velocity_ref[0:1, :]
    positive = sign_ref[...] == 1
    cx = jnp.where(positive, magnitude, -magnitude)
    cy = velocity_ref[1:2, :]
    cz = velocity_ref[2:3, :]
    square = cx * cx + cy * cy + cz * cz
    for k, row in enumerate(
        (
            2.0 * cx,
            2.0 * cy,
            2.0 * cz,
            square - 1.5,
            jnp.where(positive, 1.0, 0.0),
            total_cells * magnitude,
        )
    ):
        table_ref[k : k + 1, :] = row
    weight = weight_ref[...] / (velocities * groups)
    heat = 0.2 * (square - 2.5)
    for k, row in enumerate(
        (
            jnp.ones_like(cx),
            cx,
            cy,
            cz,
            2.0 / 3.0 * square - 1.0,
            2.0 * cx * cy,
            2.0 * cx * cz,
            2.0 * cy * cz,
            2.0 * (cx * cx - square / 3.0),
            2.0 * (cy * cy - square / 3.0),
            heat * cx,
            heat * cy,
            heat * cz,
            magnitude,
        )
    ):
        value = weight * row
        high = value.astype(jnp.bfloat16).astype(jnp.float32)
        psi_ref[k : k + 1, :] = high
        psi_ref[16 + k : 17 + k, :] = value - high

    last = cells_x - 1
    for half in range(halves):
        large[half].wait()
        rows = slice(half * 8, half * 8 + 8)
        for tile in range(tiles):
            lanes = slice(tile * LANES, (tile + 1) * LANES)
            forward = jnp.broadcast_to(table_ref[4:5, lanes], (8, LANES)) > 0.5
            courant = jnp.broadcast_to(table_ref[5:6, lanes], (8, LANES))
            base = 1.0 + courant
            basis = [jnp.broadcast_to(table_ref[k : k + 1, lanes], (8, LANES)) for k in range(4)]
            decay = []
            driven = []
            for x in range(cells_x):
                relax = spread_ref[base_row + x, rows]
                equil = spread_ref[x, rows]
                for k in range(1, fields):
                    equil = equil + spread_ref[k * cells_x + x, rows] * basis[k - 1]
                inverse = 1.0 / (base + relax)
                decay.append(courant * inverse)
                driven.append((state_ref[x, rows, lanes] + relax * equil) * inverse)
            steps = [jnp.where(forward, decay[t], decay[last - t]) for t in range(cells_x)]
            gains = [jnp.where(forward, driven[t], driven[last - t]) for t in range(cells_x)]
            products = [steps[0]]
            runs = [gains[0]]
            for t in range(1, cells_x):
                products.append(steps[t] * products[-1])
                runs.append(steps[t] * runs[-1] + gains[t])
            for x in range(cells_x):
                reach_ref[x, rows, lanes] = jnp.where(forward, products[x], products[last - x])
                run_ref[x, rows, lanes] = jnp.where(forward, runs[x], runs[last - x])
            wall = spread_ref[wall_row, rows] > 0.5
            diffuse = jnp.logical_and(forward, wall)
            fixed = jnp.where(diffuse, 0.0, free_ref[rows, lanes])
            unit = jnp.where(diffuse, 1.0, 0.0)
            direction = jnp.where(forward, 1.0, 0.0)
            for part in range(8 // QUAD):
                owner = (half * (8 // QUAD) + part) * tiles + tile
                quad = slice(part * QUAD, (part + 1) * QUAD)
                for slot, value in enumerate((runs[last], gains[0])):
                    for pair in range(QUAD // 2):
                        start = (slot * (QUAD // 2) + pair) * LANES
                        first = part * QUAD + 2 * pair
                        sent_ref[owner, :, start : start + LANES] = value[first : first + 2]
                index = half * (8 // QUAD) + part
                sent_ref[owner, 0:1, QUAD * LANES :] = rows_ref[index : index + 1, :]
                sent_ref[owner, 1:2, QUAD * LANES :] = rows_ref[quads : quads + 1, :]
                for slot, value in enumerate((fixed, unit, direction, courant)):
                    side_ref[owner, slot * QUAD : (slot + 1) * QUAD, :] = value[quad]


def scan_kernel(cells_x, maps_ref, side_ref, sent_ref, edges_ref, entry_ref, product_ref, gain_ref):
    slabs = maps_ref.shape[0]
    me = lax.axis_index("gx")
    side = side_ref[me]
    fixed = side[0:QUAD]
    unit = side[QUAD : 2 * QUAD]
    forward = side[2 * QUAD : 3 * QUAD] > 0.5
    courant = side[3 * QUAD : 4 * QUAD]
    base = 1.0 + side[3 * QUAD : 3 * QUAD + 1]
    power = courant
    reach = 1
    while reach < cells_x:
        power = power * power
        reach *= 2
    edges_ref[...] = jnp.zeros_like(edges_ref)
    below = jnp.maximum(me - 1, 0)
    above = jnp.minimum(me + 1, slabs - 1)
    edges_ref[0:1] = maps_ref[below, 1:2, QUAD * LANES :]
    edges_ref[1:2] = maps_ref[above, 1:2, QUAD * LANES :]

    def part(i, slot):
        start = slot * (QUAD // 2) * LANES
        return jnp.concatenate(
            [
                maps_ref[i, :, start + pair * LANES : start + (pair + 1) * LANES]
                for pair in range(QUAD // 2)
            ],
            axis=0,
        )

    relax = jnp.concatenate(
        [maps_ref[i, 0:1, QUAD * LANES :] for i in range(slabs)], axis=0
    ).T
    cells = cells_x * QUAD
    for i in range(slabs):
        divisors = base + jnp.broadcast_to(relax[0:cells, i : i + 1], (cells, LANES))
        product = divisors[0:8]
        for first in range(8, cells, 8):
            product = product * divisors[first : first + 8]
        product = product[0:QUAD] * product[QUAD:8]
        product_ref[i] = power * (1.0 / product)
        gain_ref[i] = part(i, 0)
    value = fixed
    for i in range(slabs - 1, -1, -1):
        entry_ref[i] = value
        value = product_ref[i] * value + gain_ref[i]
    leaving = value
    value = fixed
    answer = unit
    nothing = jnp.zeros_like(fixed)
    for i in range(slabs):
        sent_ref[i, :, 0:LANES] = jnp.where(forward, value, entry_ref[i])
        sent_ref[i, :, LANES : 2 * LANES] = jnp.where(forward, answer, leaving)
        ahead = part(i + 1, 1) if i < slabs - 1 else nothing
        behind = part(i - 1, 1) if i > 0 else nothing
        sent_ref[i, :, 2 * LANES :] = jnp.where(forward, ahead, behind)
        value = product_ref[i] * value + gain_ref[i]
        answer = product_ref[i] * answer


def whole_rows(back_ref, slot, tile, tiles, cells_y):
    return jnp.concatenate(
        [
            back_ref[quad * tiles + tile, :, slot * LANES : (slot + 1) * LANES]
            for quad in range(cells_y // QUAD)
        ],
        axis=0,
    )


def across_neighbours(m, cells_y):
    cells = m.shape[1]
    y = lax.broadcasted_iota(jnp.int32, m.shape, 1) % cells_y
    yp = jnp.where(y == cells_y - 1, pltpu.roll(m, cells_y - 1, 1), pltpu.roll(m, cells - 1, 1))
    ym = jnp.where(y == 0, pltpu.roll(m, cells - cells_y + 1, 1), pltpu.roll(m, 1, 1))
    return yp, ym


def moments_kernel(
    groups,
    slabs,
    reach_ref,
    run_ref,
    back_ref,
    psi_ref,
    table_ref,
    line_ref,
    edges_ref,
    sent_ref,
    left_ref,
):
    cells_x, cells_y, velocities = reach_ref.shape
    tiles = velocities // LANES
    cells = cells_x * cells_y
    half = left_ref.shape[0] // 2
    me = lax.axis_index("gx")
    from_left = jnp.where(me > 0, 1.0, 0.0)
    from_right = jnp.where(me < slabs - 1, 1.0, 0.0)

    def put(row, value, lanes):
        high = value.astype(jnp.bfloat16)
        low = (value - high.astype(jnp.float32)).astype(jnp.bfloat16)
        left_ref[row : row + cells_y, lanes] = high
        left_ref[half + row : half + row + cells_y, lanes] = low

    columns = edges_ref[...].T
    relax_left = jnp.broadcast_to(columns[cells_y : 2 * cells_y, 0:1], (cells_y, LANES))
    relax_right = jnp.broadcast_to(columns[0:cells_y, 1:2], (cells_y, LANES))
    for tile in range(tiles):
        lanes = slice(tile * LANES, (tile + 1) * LANES)
        forward = jnp.broadcast_to(table_ref[4:5, lanes], (cells_y, LANES)) > 0.5
        courant = jnp.broadcast_to(table_ref[5:6, lanes], (cells_y, LANES))
        entry = whole_rows(back_ref, 0, tile, tiles, cells_y)
        mixed = whole_rows(back_ref, 1, tile, tiles, cells_y)
        gain = whole_rows(back_ref, 2, tile, tiles, cells_y)
        answer = jnp.where(forward, mixed, 0.0)
        leaving = jnp.where(forward, 0.0, mixed)
        for x in range(cells_x):
            reach = reach_ref[x, :, lanes]
            value = reach * entry + run_ref[x, :, lanes]
            put(x * cells_y, value, lanes)
            put(cells + x * cells_y, reach * answer, lanes)
            if x == 0:
                outgoing = value
            if x == cells_x - 1:
                outgoing = jnp.where(forward, value, outgoing)
                outgoing_answer = reach * answer
        decay = courant / (1.0 + courant + jnp.where(forward, relax_right, relax_left))
        inside = jnp.where(forward, from_right, from_left)
        near = (decay * outgoing + gain) * inside
        near_answer = decay * outgoing_answer * inside
        row = 2 * cells
        put(row, jnp.where(forward, entry * from_left, near), lanes)
        put(row + cells_y, jnp.where(forward, near, entry * from_right), lanes)
        put(row + 2 * cells_y, answer * from_left, lanes)
        put(row + 3 * cells_y, near_answer, lanes)
        put(row + 4 * cells_y, leaving, lanes)
        put(row + 5 * cells_y, jnp.where(forward, 1.0, 0.0), lanes)
        put(row + 6 * cells_y, jnp.zeros_like(entry), lanes)
        put(row + 7 * cells_y, jnp.zeros_like(entry), lanes)

    product = lax.dot_general(
        left_ref[...],
        psi_ref[...].astype(jnp.bfloat16),
        (((1,), (1,)), ((), ())),
        preferred_element_type=jnp.float32,
    )
    upper = product[0:half]
    total = upper[:, 0:16] + upper[:, 16:32] + product[half:, 0:16]
    fixed = total[0:cells].T
    answer = total[cells : 2 * cells].T
    edges = total[2 * cells : 3 * cells].T

    spread = line_ref[0:1, :]
    lane = lax.broadcasted_iota(jnp.int32, (16, cells), 1)

    def along(m, at_left, at_right):
        xm = jnp.where(lane < cells_y, at_left, pltpu.roll(m, cells_y, 1))
        xp = jnp.where(lane >= cells - cells_y, at_right, pltpu.roll(m, cells - cells_y, 1))
        dx = xp - xm
        flow = jnp.concatenate(
            [
                dx[1:2],
                dx[0:1] + dx[4:5] + dx[8:9],
                dx[5:6],
                dx[6:7],
                2.0 / 3.0 * (dx[1:2] + dx[10:11]),
            ],
            axis=0,
        )
        return (xp + xm - 4.0 * m)[0:5], flow

    def across(m):
        yp, ym = across_neighbours(m, cells_y)
        dy = yp - ym
        flow = jnp.concatenate(
            [
                dy[2:3],
                dy[5:6],
                dy[0:1] + dy[4:5] + dy[9:10],
                dy[7:8],
                2.0 / 3.0 * (dy[2:3] + dy[11:12]),
            ],
            axis=0,
        )
        return (yp + ym)[0:5], flow

    shifts = [0, cells - 2 * cells_y, cells - 2 * cells_y, cells - 4 * cells_y]
    placed = [edges if s == 0 else pltpu.roll(edges, s, 1) for s in shifts]
    laplace, flow = along(fixed, placed[0], placed[1])
    laplace_across, flow_across = across(fixed)
    change = spread * (laplace + laplace_across) - 0.25 * (flow + flow_across)
    laplace, flow = along(answer, placed[2], placed[3])
    change_answer = spread * laplace - 0.25 * flow
    message = [
        fixed[0:5],
        change,
        answer[0:5],
        answer[5:6],
        answer[7:8],
        answer[9:10],
        answer[11:12],
        change_answer,
        edges[13:14],
    ]
    spare = QUAD * (sent_ref.shape[2] // cells) - 25
    message = jnp.concatenate(message + [jnp.zeros((spare, cells), jnp.float32)], axis=0)
    for part in range(sent_ref.shape[2] // cells):
        piece = message[part * QUAD : (part + 1) * QUAD]
        for group in range(groups):
            sent_ref[group, :, part * cells : (part + 1) * cells] = piece


def finish_kernel(
    parts_ref,
    reach_ref,
    run_ref,
    back_ref,
    table_ref,
    line_ref,
    state_hbm,
    macro_hbm,
    state_ref,
    macro_ref,
    spread_ref,
    entry_ref,
    sems,
):
    cells_x, cells_y, velocities = reach_ref.shape
    groups = parts_ref.shape[0]
    tiles = velocities // LANES
    cells = cells_x * cells_y
    sums = [parts_ref[group] for group in range(groups)]
    while len(sums) > 1:
        sums = [sums[n] + sums[n + 1] for n in range(0, len(sums), 2)]
    total = jnp.concatenate(
        [sums[0][:, n * cells : (n + 1) * cells] for n in range(parts_ref.shape[2] // cells)],
        axis=0,
    )
    lane = lax.broadcasted_iota(jnp.int32, (1, cells), 1)
    sums = total[24:25]
    here = jnp.logical_and(lane >= 4 * cells_y, lane < 5 * cells_y)
    incoming = jnp.where(here, pltpu.roll(sums, cells - cells_y, 1), 1.0)
    rho = jnp.where(here, sums, 0.0) / incoming
    width = cells_y
    while width < cells:
        rho = rho + pltpu.roll(rho, width, 1)
        width *= 2
    answer = rho * total[8:24]
    yp, ym = across_neighbours(answer, cells_y)
    dy = yp - ym
    flow = jnp.concatenate(
        [
            dy[4:5],
            dy[7:8],
            dy[2:3] + dy[6:7] + dy[9:10],
            dy[8:9],
            2.0 / 3.0 * (dy[4:5] + dy[10:11]),
        ],
        axis=0,
    )
    spread = line_ref[0:1, :]
    change = total[5:10] + rho * total[19:24] + spread * (yp + ym)[2:7] - 0.25 * flow
    updated = total[0:5] + answer[2:7] + change
    for x in range(cells_x):
        macro_ref[:, x, :] = updated[:, x * cells_y : (x + 1) * cells_y]
    macro_copy = pltpu.make_async_copy(macro_ref, macro_hbm, sems.at[cells_x])
    macro_copy.start()
    columns = jnp.concatenate([change, rho, jnp.zeros((2, cells), jnp.float32)], axis=0).T
    for x in range(cells_x):
        for k in range(5):
            spread_ref[k * cells_x + x] = jnp.broadcast_to(
                columns[x * cells_y : (x + 1) * cells_y, k : k + 1], (cells_y, LANES)
            )
    density = jnp.broadcast_to(columns[0:cells_y, 5:6], (cells_y, LANES))
    for tile in range(tiles):
        lanes = slice(tile * LANES, (tile + 1) * LANES)
        forward = jnp.broadcast_to(table_ref[4:5, lanes], (cells_y, LANES)) > 0.5
        entry = whole_rows(back_ref, 0, tile, tiles, cells_y)
        mixed = whole_rows(back_ref, 1, tile, tiles, cells_y)
        entry_ref[:, lanes] = entry + jnp.where(forward, density * mixed, 0.0)
    copies = []
    span = 2
    for first in range(0, cells_x, span):
        for tile in range(tiles):
            lanes = slice(tile * LANES, (tile + 1) * LANES)
            basis = [table_ref[k : k + 1, lanes] for k in range(4)]
            entry = entry_ref[:, lanes]
            for x in range(first, first + span):
                value = reach_ref[x, :, lanes] * entry + run_ref[x, :, lanes] + spread_ref[x]
                for k in range(1, 5):
                    value = value + spread_ref[k * cells_x + x] * basis[k - 1]
                state_ref[x, :, lanes] = value
        copy = pltpu.make_async_copy(
            state_ref.at[pl.ds(first, span)], state_hbm.at[pl.ds(first, span)], sems.at[first]
        )
        copy.start()
        copies.append(copy)
    for copy in copies + [macro_copy]:
        copy.wait()


def local(state, macro, relax_rate, velocity, vel_sign, quad_weight, freestream, wall_flag):
    cells_x, cells_y, velocities = state.shape
    fields = macro.shape[0]
    slabs = lax.axis_size("gx")
    groups = lax.axis_size("vert")
    cells = cells_x * cells_y
    tiles = velocities // LANES
    assert slabs == tiles * (cells_y // QUAD) and cells == LANES
    f32 = jnp.float32
    sign = vel_sign.reshape(1, velocities)
    weight = quad_weight.reshape(1, velocities)
    wall = wall_flag.reshape(1, cells_y)
    shape = jax.ShapeDtypeStruct
    near = shape if INTERPRET else pltpu.VMEM

    def held(x):
        return x if INTERPRET else pltpu.with_memory_space_constraint(x, pltpu.VMEM)

    def call(body, outs, scratch, *args, **kwargs):
        return pl.pallas_call(
            body, out_shape=outs, scratch_shapes=scratch, interpret=INTERPRET, **kwargs
        )(*args)

    anywhere = pl.BlockSpec(memory_space=pl.ANY)
    sources = (state, macro, relax_rate, velocity, sign, weight, freestream, wall)
    reach, run, sent, side, psi, table, line = call(
        lambda *refs: maps_kernel(float(cells_x * slabs), groups, *refs),
        (
            near(state.shape, f32),
            near(state.shape, f32),
            near((slabs, 2, (QUAD + 1) * LANES), f32),
            near((slabs, 4 * QUAD, LANES), f32),
            near((32, velocities), f32),
            near((8, velocities), f32),
            near((8, cells), f32),
        ),
        [pltpu.VMEM(value.shape, value.dtype) for value in sources]
        + [
            pltpu.VMEM((fields * cells_x + 2 * cells_x, LANES), f32),
            pltpu.VMEM((fields * cells_x + cells_x + 1, cells_y, LANES), f32),
            pltpu.VMEM((8, LANES), f32),
            pltpu.SemaphoreType.DMA((cells_y // 8 + 7,)),
        ],
        *sources,
        in_specs=[anywhere] * len(sources),
    )
    reach, run, side, psi, table, line = map(held, (reach, run, side, psi, table, line))
    maps = held(lax.all_to_all(sent, "gx", 0, 0))
    entries, edges = call(
        lambda *refs: scan_kernel(cells_x, *refs),
        (near((slabs, QUAD, 3 * LANES), f32), near((8, LANES), f32)),
        [pltpu.VMEM((slabs, QUAD, LANES), f32)] * 3,
        maps,
        side,
    )
    edges = held(edges)
    back = held(lax.all_to_all(entries, "gx", 0, 0))
    partial_sums = call(
        lambda *refs: moments_kernel(groups, slabs, *refs),
        near((groups, QUAD, SENT_PARTS * cells), f32),
        [pltpu.VMEM((6 * cells, velocities), jnp.bfloat16)],
        reach,
        run,
        back,
        psi,
        table,
        line,
        edges,
    )
    parts = held(lax.all_to_all(partial_sums, "vert", 0, 0))
    new_state, new_macro = call(
        finish_kernel,
        (shape(state.shape, f32), shape(macro.shape, f32)),
        [
            pltpu.VMEM(state.shape, f32),
            pltpu.VMEM(macro.shape, f32),
            pltpu.VMEM((5 * cells_x, cells_y, LANES), f32),
            pltpu.VMEM((cells_y, velocities), f32),
            pltpu.SemaphoreType.DMA((cells_x + 1,)),
        ],
        parts,
        reach,
        run,
        back,
        table,
        line,
        out_specs=(anywhere, anywhere),
    )
    return new_state, new_macro


def solution(mesh):
    return jax.shard_map(
        local,
        mesh=mesh,
        in_specs=(
            P("gx", None, "vert"),
            P(None, "gx", None),
            P("gx", None),
            P(None, "vert"),
            P("vert"),
            P("vert"),
            P(None, "vert"),
            P(),
        ),
        out_specs=(P("gx", None, "vert"), P(None, "gx", None)),
        check_vma=False,
    )
```

```python
import jax
import jax.numpy as jnp
from jax import lax
from jax.experimental import pallas as pl
from jax.experimental.pallas import tpu as pltpu
from jax.sharding import PartitionSpec as P

LANES = 128
QUAD = 4
SENT_PARTS = 7
INTERPRET = False


def left_parts(value):
    high = value.astype(jnp.bfloat16).astype(jnp.float32)
    return jnp.concatenate([high, value - high, high, jnp.zeros_like(high)], axis=0).astype(
        jnp.bfloat16
    )


def right_parts(value):
    high = value.astype(jnp.bfloat16).astype(jnp.float32)
    return jnp.concatenate([high, high, value - high, jnp.zeros_like(high)], axis=0).astype(
        jnp.bfloat16
    )


def columns_product(left, right):
    return lax.dot_general(
        left, right, (((0,), (0,)), ((), ())), preferred_element_type=jnp.float32
    )


def maps_kernel(
    total_cells,
    groups,
    state_hbm,
    macro_hbm,
    relax_hbm,
    velocity_hbm,
    sign_hbm,
    weight_hbm,
    free_hbm,
    wall_hbm,
    reach_ref,
    run_ref,
    sent_ref,
    side_ref,
    psi_ref,
    phi_ref,
    table_ref,
    line_ref,
    state_ref,
    macro_ref,
    relax_ref,
    velocity_ref,
    sign_ref,
    weight_ref,
    free_ref,
    wall_ref,
    cells_ref,
    basis_ref,
    moment_ref,
    equil_ref,
    spread_ref,
    sems,
):
    fields, cells_x, cells_y = macro_ref.shape
    velocities = state_ref.shape[2]
    tiles = velocities // LANES
    halves = cells_y // 8
    small = [
        pltpu.make_async_copy(source, target, sems.at[halves + n])
        for n, (source, target) in enumerate(
            (
                (velocity_hbm, velocity_ref),
                (sign_hbm, sign_ref),
                (weight_hbm, weight_ref),
                (macro_hbm, macro_ref),
                (relax_hbm, relax_ref),
                (wall_hbm, wall_ref),
                (free_hbm, free_ref),
            )
        )
    ]
    large = [
        pltpu.make_async_copy(
            state_hbm.at[:, pl.ds(half * 8, 8), :],
            state_ref.at[:, pl.ds(half * 8, 8), :],
            sems.at[half],
        )
        for half in range(halves)
    ]
    for copy in large + small:
        copy.start()
    for ref in (cells_ref, basis_ref, moment_ref, table_ref, line_ref):
        ref[...] = jnp.zeros_like(ref)
    for copy in small:
        copy.wait()
    for x in range(cells_x):
        where = slice(x * cells_y, (x + 1) * cells_y)
        cells_ref[0:fields, where] = macro_ref[:, x, :]
        line_ref[0:1, where] = relax_ref[x : x + 1, :]
    line_ref[1:2, 0:cells_y] = (wall_ref[...] == 1).astype(jnp.float32)
    columns = line_ref[...].T
    for x in range(cells_x):
        spread_ref[x] = jnp.broadcast_to(
            columns[x * cells_y : (x + 1) * cells_y, 0:1], (cells_y, LANES)
        )
    spread_ref[cells_x] = jnp.broadcast_to(columns[0:cells_y, 1:2], (cells_y, LANES))
    relax_row = line_ref[0:1, :]
    line_ref[2:3, :] = 0.2 / (1.0 + relax_row)

    magnitude = velocity_ref[0:1, :]
    positive = sign_ref[...] == 1
    cx = jnp.where(positive, magnitude, -magnitude)
    cy = velocity_ref[1:2, :]
    cz = velocity_ref[2:3, :]
    square = cx * cx + cy * cy + cz * cz
    for k, row in enumerate((jnp.ones_like(cx), 2.0 * cx, 2.0 * cy, 2.0 * cz, square - 1.5)):
        basis_ref[k : k + 1, :] = row
    table_ref[0:1, :] = jnp.where(positive, 1.0, 0.0)
    table_ref[1:2, :] = total_cells * magnitude
    phi = right_parts(basis_ref[...])
    phi_ref[...] = phi
    equil_ref[...] = columns_product(left_parts(cells_ref[...]), phi)
    weight = weight_ref[...] / (velocities * groups)
    heat = 0.2 * (square - 2.5)
    for k, row in enumerate(
        (
            jnp.ones_like(cx),
            cx,
            cy,
            cz,
            2.0 / 3.0 * square - 1.0,
            2.0 * cx * cy,
            2.0 * cx * cz,
            2.0 * cy * cz,
            2.0 * (cx * cx - square / 3.0),
            2.0 * (cy * cy - square / 3.0),
            heat * cx,
            heat * cy,
            heat * cz,
            magnitude,
        )
    ):
        moment_ref[k : k + 1, :] = weight * row
    high = moment_ref[...].astype(jnp.bfloat16)
    psi_ref[0:16] = high
    psi_ref[16:32] = (moment_ref[...] - high.astype(jnp.float32)).astype(jnp.bfloat16)

    last = cells_x - 1
    for half in range(halves):
        large[half].wait()
        rows = slice(half * 8, half * 8 + 8)
        for tile in range(tiles):
            lanes = slice(tile * LANES, (tile + 1) * LANES)
            forward = jnp.broadcast_to(table_ref[0:1, lanes], (8, LANES)) > 0.5
            courant = jnp.broadcast_to(table_ref[1:2, lanes], (8, LANES))
            base = 1.0 + courant
            decay = []
            driven = []
            for x in range(cells_x):
                relax = spread_ref[x, rows]
                first = x * cells_y + half * 8
                equil = equil_ref[first : first + 8, lanes]
                inverse = 1.0 / (base + relax)
                decay.append(courant * inverse)
                driven.append((state_ref[x, rows, lanes] + relax * equil) * inverse)
            steps = [jnp.where(forward, decay[t], decay[last - t]) for t in range(cells_x)]
            gains = [jnp.where(forward, driven[t], driven[last - t]) for t in range(cells_x)]
            products = [steps[0]]
            runs = [gains[0]]
            for t in range(1, cells_x):
                products.append(steps[t] * products[-1])
                runs.append(steps[t] * runs[-1] + gains[t])
            for x in range(cells_x):
                reach_ref[x, rows, lanes] = jnp.where(forward, products[x], products[last - x])
                run_ref[x, rows, lanes] = jnp.where(forward, runs[x], runs[last - x])
            wall = spread_ref[cells_x, rows] > 0.5
            diffuse = jnp.logical_and(forward, wall)
            fixed = jnp.where(diffuse, 0.0, free_ref[rows, lanes])
            unit = jnp.where(diffuse, 1.0, 0.0)
            direction = jnp.where(forward, 1.0, 0.0)
            for part in range(8 // QUAD):
                owner = (half * (8 // QUAD) + part) * tiles + tile
                quad = slice(part * QUAD, (part + 1) * QUAD)
                for slot, value in enumerate((runs[last], gains[0])):
                    for pair in range(QUAD // 2):
                        start = (slot * (QUAD // 2) + pair) * LANES
                        first = part * QUAD + 2 * pair
                        sent_ref[owner, :, start : start + LANES] = value[first : first + 2]
                sent_ref[owner, 0:1, QUAD * LANES :] = relax_row
                for slot, value in enumerate((fixed, unit, direction, courant)):
                    side_ref[owner, slot * QUAD : (slot + 1) * QUAD, :] = value[quad]


def scan_kernel(cells_x, maps_ref, side_ref, sent_ref, edges_ref, entry_ref, product_ref, gain_ref):
    slabs = maps_ref.shape[0]
    me = lax.axis_index("gx")
    side = side_ref[me]
    fixed = side[0:QUAD]
    unit = side[QUAD : 2 * QUAD]
    forward = side[2 * QUAD : 3 * QUAD] > 0.5
    courant = side[3 * QUAD : 4 * QUAD]
    base = 1.0 + side[3 * QUAD : 3 * QUAD + 1]
    power = courant
    reach = 1
    while reach < cells_x:
        power = power * power
        reach *= 2
    edges_ref[...] = jnp.zeros_like(edges_ref)
    below = jnp.maximum(me - 1, 0)
    above = jnp.minimum(me + 1, slabs - 1)
    edges_ref[0:1] = maps_ref[below, 0:1, QUAD * LANES :]
    edges_ref[1:2] = maps_ref[above, 0:1, QUAD * LANES :]

    def part(i, slot):
        start = slot * (QUAD // 2) * LANES
        return jnp.concatenate(
            [
                maps_ref[i, :, start + pair * LANES : start + (pair + 1) * LANES]
                for pair in range(QUAD // 2)
            ],
            axis=0,
        )

    relax = jnp.concatenate(
        [maps_ref[i, 0:1, QUAD * LANES :] for i in range(slabs)], axis=0
    ).T
    cells_y = relax.shape[0] // cells_x
    quads = cells_y // QUAD
    index = me // (slabs // quads)
    high = index // 2 == 1
    odd = index % 2 == 1
    picked = []
    for x in range(cells_x):
        rows = relax[x * cells_y : (x + 1) * cells_y]
        rows = jnp.where(high, rows[8:16], rows[0:8])
        picked.append(jnp.where(odd, rows[QUAD:8], rows[0:QUAD]))
    relax = jnp.concatenate(picked, axis=0)
    cells = cells_x * QUAD
    for i in range(slabs):
        divisors = base + jnp.broadcast_to(relax[:, i : i + 1], (cells, LANES))
        product = divisors[0:8]
        for first in range(8, cells, 8):
            product = product * divisors[first : first + 8]
        product = product[0:QUAD] * product[QUAD:8]
        product_ref[i] = power * (1.0 / product)
        gain_ref[i] = part(i, 0)
    value = fixed
    for i in range(slabs - 1, -1, -1):
        entry_ref[i] = value
        value = product_ref[i] * value + gain_ref[i]
    leaving = value
    value = fixed
    answer = unit
    nothing = jnp.zeros_like(fixed)
    for i in range(slabs):
        sent_ref[i, :, 0:LANES] = jnp.where(forward, value, entry_ref[i])
        sent_ref[i, :, LANES : 2 * LANES] = jnp.where(forward, answer, leaving)
        ahead = part(i + 1, 1) if i < slabs - 1 else nothing
        behind = part(i - 1, 1) if i > 0 else nothing
        sent_ref[i, :, 2 * LANES :] = jnp.where(forward, ahead, behind)
        value = product_ref[i] * value + gain_ref[i]
        answer = product_ref[i] * answer


def whole_rows(back_ref, slot, tile, tiles, cells_y):
    return jnp.concatenate(
        [
            back_ref[quad * tiles + tile, :, slot * LANES : (slot + 1) * LANES]
            for quad in range(cells_y // QUAD)
        ],
        axis=0,
    )


def across_neighbours(m, cells_y):
    cells = m.shape[1]
    y = lax.broadcasted_iota(jnp.int32, m.shape, 1) % cells_y
    yp = jnp.where(y == cells_y - 1, pltpu.roll(m, cells_y - 1, 1), pltpu.roll(m, cells - 1, 1))
    ym = jnp.where(y == 0, pltpu.roll(m, cells - cells_y + 1, 1), pltpu.roll(m, 1, 1))
    return yp, ym


def moments_kernel(
    groups,
    slabs,
    reach_ref,
    run_ref,
    back_ref,
    psi_ref,
    table_ref,
    line_ref,
    edges_ref,
    sent_ref,
    left_ref,
):
    cells_x, cells_y, velocities = reach_ref.shape
    tiles = velocities // LANES
    cells = cells_x * cells_y
    half = left_ref.shape[0] // 2
    me = lax.axis_index("gx")
    from_left = jnp.where(me > 0, 1.0, 0.0)
    from_right = jnp.where(me < slabs - 1, 1.0, 0.0)

    def put(row, value, lanes):
        high = value.astype(jnp.bfloat16)
        low = (value - high.astype(jnp.float32)).astype(jnp.bfloat16)
        left_ref[row : row + cells_y, lanes] = high
        left_ref[half + row : half + row + cells_y, lanes] = low

    columns = edges_ref[...].T
    relax_left = jnp.broadcast_to(columns[cells - cells_y : cells, 0:1], (cells_y, LANES))
    relax_right = jnp.broadcast_to(columns[0:cells_y, 1:2], (cells_y, LANES))
    for tile in range(tiles):
        lanes = slice(tile * LANES, (tile + 1) * LANES)
        forward = jnp.broadcast_to(table_ref[0:1, lanes], (cells_y, LANES)) > 0.5
        courant = jnp.broadcast_to(table_ref[1:2, lanes], (cells_y, LANES))
        entry = whole_rows(back_ref, 0, tile, tiles, cells_y)
        mixed = whole_rows(back_ref, 1, tile, tiles, cells_y)
        gain = whole_rows(back_ref, 2, tile, tiles, cells_y)
        answer = jnp.where(forward, mixed, 0.0)
        leaving = jnp.where(forward, 0.0, mixed)
        for x in range(cells_x):
            reach = reach_ref[x, :, lanes]
            value = reach * entry + run_ref[x, :, lanes]
            put(x * cells_y, value, lanes)
            put(cells + x * cells_y, reach * answer, lanes)
            if x == 0:
                outgoing = value
            if x == cells_x - 1:
                outgoing = jnp.where(forward, value, outgoing)
                outgoing_answer = reach * answer
        decay = courant / (1.0 + courant + jnp.where(forward, relax_right, relax_left))
        inside = jnp.where(forward, from_right, from_left)
        near = (decay * outgoing + gain) * inside
        near_answer = decay * outgoing_answer * inside
        row = 2 * cells
        put(row, jnp.where(forward, entry * from_left, near), lanes)
        put(row + cells_y, jnp.where(forward, near, entry * from_right), lanes)
        put(row + 2 * cells_y, answer * from_left, lanes)
        put(row + 3 * cells_y, near_answer, lanes)
        put(row + 4 * cells_y, leaving, lanes)
        put(row + 5 * cells_y, jnp.where(forward, 1.0, 0.0), lanes)
        put(row + 6 * cells_y, jnp.zeros_like(entry), lanes)
        put(row + 7 * cells_y, jnp.zeros_like(entry), lanes)

    product = lax.dot_general(
        psi_ref[...],
        left_ref[...],
        (((1,), (1,)), ((), ())),
        preferred_element_type=jnp.float32,
    )
    upper = product[:, 0:half]
    total = upper[0:16] + upper[16:32] + product[0:16, half:]
    fixed = total[:, 0:cells]
    answer = total[:, cells : 2 * cells]
    edges = total[:, 2 * cells : 3 * cells]

    spread = line_ref[2:3, :]
    lane = lax.broadcasted_iota(jnp.int32, (16, cells), 1)

    def along(m, at_left, at_right):
        xm = jnp.where(lane < cells_y, at_left, pltpu.roll(m, cells_y, 1))
        xp = jnp.where(lane >= cells - cells_y, at_right, pltpu.roll(m, cells - cells_y, 1))
        dx = xp - xm
        flow = jnp.concatenate(
            [
                dx[1:2],
                dx[0:1] + dx[4:5] + dx[8:9],
                dx[5:6],
                dx[6:7],
                2.0 / 3.0 * (dx[1:2] + dx[10:11]),
            ],
            axis=0,
        )
        return (xp + xm - 4.0 * m)[0:5], flow

    def across(m):
        yp, ym = across_neighbours(m, cells_y)
        dy = yp - ym
        flow = jnp.concatenate(
            [
                dy[2:3],
                dy[5:6],
                dy[0:1] + dy[4:5] + dy[9:10],
                dy[7:8],
                2.0 / 3.0 * (dy[2:3] + dy[11:12]),
            ],
            axis=0,
        )
        return (yp + ym)[0:5], flow

    shifts = [0, cells - 2 * cells_y, cells - 2 * cells_y, cells - 4 * cells_y]
    placed = [edges if s == 0 else pltpu.roll(edges, s, 1) for s in shifts]
    laplace, flow = along(fixed, placed[0], placed[1])
    laplace_across, flow_across = across(fixed)
    change = spread * (laplace + laplace_across) - 0.25 * (flow + flow_across)
    laplace, flow = along(answer, placed[2], placed[3])
    change_answer = spread * laplace - 0.25 * flow
    message = [
        fixed[0:5],
        change,
        answer[0:5],
        answer[5:6],
        answer[7:8],
        answer[9:10],
        answer[11:12],
        change_answer,
        edges[13:14],
    ]
    spare = QUAD * (sent_ref.shape[2] // cells) - 25
    message = jnp.concatenate(message + [jnp.zeros((spare, cells), jnp.float32)], axis=0)
    for part in range(sent_ref.shape[2] // cells):
        piece = message[part * QUAD : (part + 1) * QUAD]
        for group in range(groups):
            sent_ref[group, :, part * cells : (part + 1) * cells] = piece


def finish_kernel(
    parts_ref,
    reach_ref,
    run_ref,
    back_ref,
    phi_ref,
    table_ref,
    line_ref,
    state_hbm,
    macro_hbm,
    state_ref,
    macro_ref,
    change_ref,
    entry_ref,
    sems,
):
    cells_x, cells_y, velocities = reach_ref.shape
    groups = parts_ref.shape[0]
    tiles = velocities // LANES
    cells = cells_x * cells_y
    sums = [parts_ref[group] for group in range(groups)]
    while len(sums) > 1:
        sums = [sums[n] + sums[n + 1] for n in range(0, len(sums), 2)]
    total = jnp.concatenate(
        [sums[0][:, n * cells : (n + 1) * cells] for n in range(parts_ref.shape[2] // cells)],
        axis=0,
    )
    lane = lax.broadcasted_iota(jnp.int32, (1, cells), 1)
    sums = total[24:25]
    here = jnp.logical_and(lane >= 4 * cells_y, lane < 5 * cells_y)
    incoming = jnp.where(here, pltpu.roll(sums, cells - cells_y, 1), 1.0)
    rho = jnp.where(here, sums, 0.0) / incoming
    width = cells_y
    while width < cells:
        rho = rho + pltpu.roll(rho, width, 1)
        width *= 2
    answer = rho * total[8:24]
    yp, ym = across_neighbours(answer, cells_y)
    dy = yp - ym
    flow = jnp.concatenate(
        [
            dy[4:5],
            dy[7:8],
            dy[2:3] + dy[6:7] + dy[9:10],
            dy[8:9],
            2.0 / 3.0 * (dy[4:5] + dy[10:11]),
        ],
        axis=0,
    )
    spread = line_ref[2:3, :]
    change = total[5:10] + rho * total[19:24] + spread * (yp + ym)[2:7] - 0.25 * flow
    updated = total[0:5] + answer[2:7] + change
    for x in range(cells_x):
        macro_ref[:, x, :] = updated[:, x * cells_y : (x + 1) * cells_y]
    macro_copy = pltpu.make_async_copy(macro_ref, macro_hbm, sems.at[cells_x])
    macro_copy.start()
    spare = jnp.zeros((3, cells), jnp.float32)
    change_ref[...] = columns_product(
        left_parts(jnp.concatenate([change, spare], axis=0)), phi_ref[...]
    )
    columns = jnp.broadcast_to(rho, (8, cells)).T
    density = jnp.broadcast_to(columns[0:cells_y, 0:1], (cells_y, LANES))
    for tile in range(tiles):
        lanes = slice(tile * LANES, (tile + 1) * LANES)
        forward = jnp.broadcast_to(table_ref[0:1, lanes], (cells_y, LANES)) > 0.5
        entry = whole_rows(back_ref, 0, tile, tiles, cells_y)
        mixed = whole_rows(back_ref, 1, tile, tiles, cells_y)
        entry_ref[:, lanes] = entry + jnp.where(forward, density * mixed, 0.0)
    copies = []
    span = 2
    for first in range(0, cells_x, span):
        for tile in range(tiles):
            lanes = slice(tile * LANES, (tile + 1) * LANES)
            entry = entry_ref[:, lanes]
            for x in range(first, first + span):
                change = change_ref[x * cells_y : (x + 1) * cells_y, lanes]
                value = reach_ref[x, :, lanes] * entry + run_ref[x, :, lanes] + change
                state_ref[x, :, lanes] = value
        copy = pltpu.make_async_copy(
            state_ref.at[pl.ds(first, span)], state_hbm.at[pl.ds(first, span)], sems.at[first]
        )
        copy.start()
        copies.append(copy)
    for copy in copies + [macro_copy]:
        copy.wait()


def local(state, macro, relax_rate, velocity, vel_sign, quad_weight, freestream, wall_flag):
    cells_x, cells_y, velocities = state.shape
    fields = macro.shape[0]
    slabs = lax.axis_size("gx")
    groups = lax.axis_size("vert")
    cells = cells_x * cells_y
    tiles = velocities // LANES
    assert slabs == tiles * (cells_y // QUAD) and cells == LANES
    f32 = jnp.float32
    sign = vel_sign.reshape(1, velocities)
    weight = quad_weight.reshape(1, velocities)
    wall = wall_flag.reshape(1, cells_y)
    shape = jax.ShapeDtypeStruct
    near = shape if INTERPRET else pltpu.VMEM

    def held(x):
        return x if INTERPRET else pltpu.with_memory_space_constraint(x, pltpu.VMEM)

    def call(body, outs, scratch, *args, **kwargs):
        return pl.pallas_call(
            body, out_shape=outs, scratch_shapes=scratch, interpret=INTERPRET, **kwargs
        )(*args)

    anywhere = pl.BlockSpec(memory_space=pl.ANY)
    sources = (state, macro, relax_rate, velocity, sign, weight, freestream, wall)
    reach, run, sent, side, psi, phi, table, line = call(
        lambda *refs: maps_kernel(float(cells_x * slabs), groups, *refs),
        (
            near(state.shape, f32),
            near(state.shape, f32),
            near((slabs, 2, (QUAD + 1) * LANES), f32),
            near((slabs, 4 * QUAD, LANES), f32),
            near((32, velocities), jnp.bfloat16),
            near((32, velocities), jnp.bfloat16),
            near((8, velocities), f32),
            near((8, cells), f32),
        ),
        [pltpu.VMEM(value.shape, value.dtype) for value in sources]
        + [
            pltpu.VMEM((8, cells), f32),
            pltpu.VMEM((8, velocities), f32),
            pltpu.VMEM((16, velocities), f32),
            pltpu.VMEM((cells, velocities), f32),
            pltpu.VMEM((cells_x + 1, cells_y, LANES), f32),
            pltpu.SemaphoreType.DMA((cells_y // 8 + 7,)),
        ],
        *sources,
        in_specs=[anywhere] * len(sources),
    )
    reach, run, side = map(held, (reach, run, side))
    psi, phi, table, line = map(held, (psi, phi, table, line))
    maps = held(lax.all_to_all(sent, "gx", 0, 0))
    entries, edges = call(
        lambda *refs: scan_kernel(cells_x, *refs),
        (near((slabs, QUAD, 3 * LANES), f32), near((8, LANES), f32)),
        [pltpu.VMEM((slabs, QUAD, LANES), f32)] * 3,
        maps,
        side,
    )
    edges = held(edges)
    back = held(lax.all_to_all(entries, "gx", 0, 0))
    partial_sums = call(
        lambda *refs: moments_kernel(groups, slabs, *refs),
        near((groups, QUAD, SENT_PARTS * cells), f32),
        [pltpu.VMEM((6 * cells, velocities), jnp.bfloat16)],
        reach,
        run,
        back,
        psi,
        table,
        line,
        edges,
    )
    parts = held(lax.all_to_all(partial_sums, "vert", 0, 0))
    new_state, new_macro = call(
        finish_kernel,
        (shape(state.shape, f32), shape(macro.shape, f32)),
        [
            pltpu.VMEM(state.shape, f32),
            pltpu.VMEM(macro.shape, f32),
            pltpu.VMEM((cells, velocities), f32),
            pltpu.VMEM((cells_y, velocities), f32),
            pltpu.SemaphoreType.DMA((cells_x + 1,)),
        ],
        parts,
        reach,
        run,
        back,
        phi,
        table,
        line,
        out_specs=(anywhere, anywhere),
    )
    return new_state, new_macro


def solution(mesh):
    return jax.shard_map(
        local,
        mesh=mesh,
        in_specs=(
            P("gx", None, "vert"),
            P(None, "gx", None),
            P("gx", None),
            P(None, "vert"),
            P("vert"),
            P("vert"),
            P(None, "vert"),
            P(),
        ),
        out_specs=(P("gx", None, "vert"), P(None, "gx", None)),
        check_vma=False,
    )
```

```python
import jax
import jax.numpy as jnp
from jax import lax
from jax.experimental import pallas as pl
from jax.experimental.pallas import tpu as pltpu
from jax.sharding import PartitionSpec as P

LANES = 128
QUAD = 4
EDGE_ROWS = (0, 1, 2, 3, 4, 5, 6, 8, 10)
SENT_PARTS = 7
INTERPRET = False


def left_parts(value):
    high = value.astype(jnp.bfloat16).astype(jnp.float32)
    return jnp.concatenate([high, value - high, high, jnp.zeros_like(high)], axis=0).astype(
        jnp.bfloat16
    )


def right_parts(value):
    high = value.astype(jnp.bfloat16).astype(jnp.float32)
    return jnp.concatenate([high, high, value - high, jnp.zeros_like(high)], axis=0).astype(
        jnp.bfloat16
    )


def columns_product(left, right):
    return lax.dot_general(
        left, right, (((0,), (0,)), ((), ())), preferred_element_type=jnp.float32
    )


def split_put(ref, row, lanes, value):
    half = ref.shape[0] // 2
    count = value.shape[0]
    high = value.astype(jnp.bfloat16)
    ref[row : row + count, lanes] = high
    ref[half + row : half + row + count, lanes] = (value - high.astype(jnp.float32)).astype(
        jnp.bfloat16
    )


def split_moments(psi_ref, left_ref):
    half = left_ref.shape[0] // 2
    product = lax.dot_general(
        psi_ref[...],
        left_ref[...],
        (((1,), (1,)), ((), ())),
        preferred_element_type=jnp.float32,
    )
    return product[0:16, 0:half] + product[16:32, 0:half] + product[0:16, half:]


def maps_kernel(
    total_cells,
    groups,
    state_hbm,
    macro_hbm,
    relax_hbm,
    velocity_hbm,
    sign_hbm,
    weight_hbm,
    free_hbm,
    wall_hbm,
    reach_ref,
    run_ref,
    sent_ref,
    side_ref,
    psi_ref,
    phi_ref,
    table_ref,
    line_ref,
    state_ref,
    macro_ref,
    relax_ref,
    velocity_ref,
    sign_ref,
    weight_ref,
    free_ref,
    wall_ref,
    cells_ref,
    basis_ref,
    moment_ref,
    equil_ref,
    spread_ref,
    left_ref,
    message_ref,
    sems,
):
    fields, cells_x, cells_y = macro_ref.shape
    velocities = state_ref.shape[2]
    tiles = velocities // LANES
    halves = cells_y // 8
    small = [
        pltpu.make_async_copy(source, target, sems.at[halves + n])
        for n, (source, target) in enumerate(
            (
                (velocity_hbm, velocity_ref),
                (sign_hbm, sign_ref),
                (weight_hbm, weight_ref),
                (macro_hbm, macro_ref),
                (relax_hbm, relax_ref),
                (wall_hbm, wall_ref),
                (free_hbm, free_ref),
            )
        )
    ]
    large = [
        pltpu.make_async_copy(
            state_hbm.at[:, pl.ds(half * 8, 8), :],
            state_ref.at[:, pl.ds(half * 8, 8), :],
            sems.at[half],
        )
        for half in range(halves)
    ]
    for copy in large + small:
        copy.start()
    for ref in (cells_ref, basis_ref, moment_ref, table_ref, line_ref, message_ref, left_ref):
        ref[...] = jnp.zeros_like(ref)
    for copy in small:
        copy.wait()
    for x in range(cells_x):
        where = slice(x * cells_y, (x + 1) * cells_y)
        cells_ref[0:fields, where] = macro_ref[:, x, :]
        line_ref[0:1, where] = relax_ref[x : x + 1, :]
    line_ref[1:2, 0:cells_y] = (wall_ref[...] == 1).astype(jnp.float32)
    columns = line_ref[...].T
    for x in range(cells_x):
        spread_ref[x] = jnp.broadcast_to(
            columns[x * cells_y : (x + 1) * cells_y, 0:1], (cells_y, LANES)
        )
    spread_ref[cells_x] = jnp.broadcast_to(columns[0:cells_y, 1:2], (cells_y, LANES))
    relax_row = line_ref[0:1, :]
    line_ref[2:3, :] = 0.2 / (1.0 + relax_row)

    magnitude = velocity_ref[0:1, :]
    positive = sign_ref[...] == 1
    cx = jnp.where(positive, magnitude, -magnitude)
    cy = velocity_ref[1:2, :]
    cz = velocity_ref[2:3, :]
    square = cx * cx + cy * cy + cz * cz
    for k, row in enumerate((jnp.ones_like(cx), 2.0 * cx, 2.0 * cy, 2.0 * cz, square - 1.5)):
        basis_ref[k : k + 1, :] = row
    table_ref[0:1, :] = jnp.where(positive, 1.0, 0.0)
    table_ref[1:2, :] = total_cells * magnitude
    phi = right_parts(basis_ref[...])
    phi_ref[...] = phi
    equil_ref[...] = columns_product(left_parts(cells_ref[...]), phi)
    weight = weight_ref[...] / (velocities * groups)
    heat = 0.2 * (square - 2.5)
    for k, row in enumerate(
        (
            jnp.ones_like(cx),
            cx,
            cy,
            cz,
            2.0 / 3.0 * square - 1.0,
            2.0 * cx * cy,
            2.0 * cx * cz,
            2.0 * cy * cz,
            2.0 * (cx * cx - square / 3.0),
            2.0 * (cy * cy - square / 3.0),
            heat * cx,
            heat * cy,
            heat * cz,
            magnitude,
        )
    ):
        moment_ref[k : k + 1, :] = weight * row
    high = moment_ref[...].astype(jnp.bfloat16)
    psi_ref[0:16] = high
    psi_ref[16:32] = (moment_ref[...] - high.astype(jnp.float32)).astype(jnp.bfloat16)

    last = cells_x - 1
    for half in range(halves):
        large[half].wait()
        rows = slice(half * 8, half * 8 + 8)
        for tile in range(tiles):
            lanes = slice(tile * LANES, (tile + 1) * LANES)
            forward = jnp.broadcast_to(table_ref[0:1, lanes], (8, LANES)) > 0.5
            courant = jnp.broadcast_to(table_ref[1:2, lanes], (8, LANES))
            base = 1.0 + courant
            decay = []
            driven = []
            for x in range(cells_x):
                relax = spread_ref[x, rows]
                first = x * cells_y + half * 8
                equil = equil_ref[first : first + 8, lanes]
                inverse = 1.0 / (base + relax)
                decay.append(courant * inverse)
                driven.append((state_ref[x, rows, lanes] + relax * equil) * inverse)
            steps = [jnp.where(forward, decay[t], decay[last - t]) for t in range(cells_x)]
            gains = [jnp.where(forward, driven[t], driven[last - t]) for t in range(cells_x)]
            products = [steps[0]]
            runs = [gains[0]]
            for t in range(1, cells_x):
                products.append(steps[t] * products[-1])
                runs.append(steps[t] * runs[-1] + gains[t])
            for x in range(cells_x):
                reach_ref[x, rows, lanes] = jnp.where(forward, products[x], products[last - x])
                run_ref[x, rows, lanes] = jnp.where(forward, runs[x], runs[last - x])
            wall = spread_ref[cells_x, rows] > 0.5
            diffuse = jnp.logical_and(forward, wall)
            fixed = jnp.where(diffuse, 0.0, free_ref[rows, lanes])
            unit = jnp.where(diffuse, 1.0, 0.0)
            direction = jnp.where(forward, 1.0, 0.0)
            first_gain = gains[0]
            outward = jnp.where(forward, first_gain, 0.0)
            split_put(left_ref, half * 8, lanes, outward)
            split_put(left_ref, cells_y + half * 8, lanes, first_gain - outward)
            for part in range(8 // QUAD):
                owner = (half * (8 // QUAD) + part) * tiles + tile
                quad = slice(part * QUAD, (part + 1) * QUAD)
                sent_ref[owner, 0:QUAD, :] = runs[last][quad]
                for slot, value in enumerate((fixed, unit, direction, courant)):
                    side_ref[owner, slot * QUAD : (slot + 1) * QUAD, :] = value[quad]
    message_ref[0:1, :] = relax_row
    edge_moments = split_moments(psi_ref, left_ref)
    for n, k in enumerate(EDGE_ROWS):
        row = 1 + n // QUAD
        start = (n % QUAD) * 2 * cells_y
        message_ref[row : row + 1, start : start + 2 * cells_y] = edge_moments[
            k : k + 1, 0 : 2 * cells_y
        ]
    message = message_ref[0:QUAD]
    for owner in range(sent_ref.shape[0]):
        sent_ref[owner, QUAD : 2 * QUAD, :] = message


def scan_kernel(cells_x, maps_ref, side_ref, sent_ref, edges_ref, entry_ref, product_ref):
    slabs = maps_ref.shape[0]
    me = lax.axis_index("gx")
    side = side_ref[me]
    fixed = side[0:QUAD]
    unit = side[QUAD : 2 * QUAD]
    forward = side[2 * QUAD : 3 * QUAD] > 0.5
    courant = side[3 * QUAD : 4 * QUAD]
    base = 1.0 + side[3 * QUAD : 3 * QUAD + 1]
    power = courant
    reach = 1
    while reach < cells_x:
        power = power * power
        reach *= 2
    below = jnp.maximum(me - 1, 0)
    above = jnp.minimum(me + 1, slabs - 1)
    edges_ref[0:QUAD] = maps_ref[below, QUAD : 2 * QUAD]
    edges_ref[QUAD : 2 * QUAD] = maps_ref[above, QUAD : 2 * QUAD]
    relax = jnp.concatenate([maps_ref[i, QUAD : QUAD + 1] for i in range(slabs)], axis=0).T
    cells_y = relax.shape[0] // cells_x
    quads = cells_y // QUAD
    index = me // (slabs // quads)
    high = index // 2 == 1
    odd = index % 2 == 1
    picked = []
    for x in range(cells_x):
        rows = relax[x * cells_y : (x + 1) * cells_y]
        rows = jnp.where(high, rows[8:16], rows[0:8])
        picked.append(jnp.where(odd, rows[QUAD:8], rows[0:QUAD]))
    relax = jnp.concatenate(picked, axis=0)
    cells = cells_x * QUAD
    for i in range(slabs):
        divisors = base + jnp.broadcast_to(relax[:, i : i + 1], (cells, LANES))
        product = divisors[0:8]
        for first in range(8, cells, 8):
            product = product * divisors[first : first + 8]
        product = product[0:QUAD] * product[QUAD:8]
        product_ref[i] = power * (1.0 / product)
    value = fixed
    for i in range(slabs - 1, -1, -1):
        entry_ref[i] = value
        value = product_ref[i] * value + maps_ref[i, 0:QUAD]
    leaving = value
    value = fixed
    answer = unit
    for i in range(slabs):
        sent_ref[i, 0:QUAD] = jnp.where(forward, value, entry_ref[i])
        sent_ref[i, QUAD : 2 * QUAD] = jnp.where(forward, answer, leaving)
        value = product_ref[i] * value + maps_ref[i, 0:QUAD]
        answer = product_ref[i] * answer


def whole_rows(back_ref, slot, tile, tiles, cells_y):
    return jnp.concatenate(
        [
            back_ref[quad * tiles + tile, slot * QUAD : (slot + 1) * QUAD]
            for quad in range(cells_y // QUAD)
        ],
        axis=0,
    )


def across_neighbours(m, cells_y):
    cells = m.shape[1]
    y = lax.broadcasted_iota(jnp.int32, m.shape, 1) % cells_y
    yp = jnp.where(y == cells_y - 1, pltpu.roll(m, cells_y - 1, 1), pltpu.roll(m, cells - 1, 1))
    ym = jnp.where(y == 0, pltpu.roll(m, cells - cells_y + 1, 1), pltpu.roll(m, 1, 1))
    return yp, ym


def moments_kernel(
    groups,
    slabs,
    reach_ref,
    run_ref,
    back_ref,
    psi_ref,
    table_ref,
    line_ref,
    edges_ref,
    sent_ref,
    left_ref,
    near_ref,
):
    cells_x, cells_y, velocities = reach_ref.shape
    tiles = velocities // LANES
    cells = cells_x * cells_y
    me = lax.axis_index("gx")
    from_left = jnp.where(me > 0, 1.0, 0.0)
    from_right = jnp.where(me < slabs - 1, 1.0, 0.0)

    def put(row, value, lanes):
        split_put(left_ref, row, lanes, value)

    near_ref[...] = jnp.zeros_like(near_ref)
    for n, k in enumerate(EDGE_ROWS):
        row = 1 + n // QUAD
        start = (n % QUAD) * 2 * cells_y
        near_ref[k : k + 1, 0:cells_y] = (
            edges_ref[row : row + 1, start + cells_y : start + 2 * cells_y] * from_left
        )
        near_ref[k : k + 1, cells_y : 2 * cells_y] = (
            edges_ref[QUAD + row : QUAD + row + 1, start : start + cells_y] * from_right
        )
    columns = edges_ref[...].T
    relax_left = jnp.broadcast_to(columns[cells - cells_y : cells, 0:1], (cells_y, LANES))
    relax_right = jnp.broadcast_to(columns[0:cells_y, QUAD : QUAD + 1], (cells_y, LANES))
    for tile in range(tiles):
        lanes = slice(tile * LANES, (tile + 1) * LANES)
        forward = jnp.broadcast_to(table_ref[0:1, lanes], (cells_y, LANES)) > 0.5
        courant = jnp.broadcast_to(table_ref[1:2, lanes], (cells_y, LANES))
        entry = whole_rows(back_ref, 0, tile, tiles, cells_y)
        mixed = whole_rows(back_ref, 1, tile, tiles, cells_y)
        answer = jnp.where(forward, mixed, 0.0)
        leaving = jnp.where(forward, 0.0, mixed)
        for x in range(cells_x):
            reach = reach_ref[x, :, lanes]
            value = reach * entry + run_ref[x, :, lanes]
            put(x * cells_y, value, lanes)
            put(cells + x * cells_y, reach * answer, lanes)
            if x == 0:
                outgoing = value
            if x == cells_x - 1:
                outgoing = jnp.where(forward, value, outgoing)
                outgoing_answer = reach * answer
        decay = courant / (1.0 + courant + jnp.where(forward, relax_right, relax_left))
        inside = jnp.where(forward, from_right, from_left)
        near = decay * outgoing * inside
        near_answer = decay * outgoing_answer * inside
        row = 2 * cells
        put(row, jnp.where(forward, entry * from_left, near), lanes)
        put(row + cells_y, jnp.where(forward, near, entry * from_right), lanes)
        put(row + 2 * cells_y, answer * from_left, lanes)
        put(row + 3 * cells_y, near_answer, lanes)
        put(row + 4 * cells_y, leaving, lanes)
        put(row + 5 * cells_y, jnp.where(forward, 1.0, 0.0), lanes)
        put(row + 6 * cells_y, jnp.zeros_like(entry), lanes)
        put(row + 7 * cells_y, jnp.zeros_like(entry), lanes)

    total = split_moments(psi_ref, left_ref)
    fixed = total[:, 0:cells]
    answer = total[:, cells : 2 * cells]
    edges = total[:, 2 * cells : 3 * cells] + near_ref[...]

    spread = line_ref[2:3, :]
    lane = lax.broadcasted_iota(jnp.int32, (16, cells), 1)

    def along(m, at_left, at_right):
        xm = jnp.where(lane < cells_y, at_left, pltpu.roll(m, cells_y, 1))
        xp = jnp.where(lane >= cells - cells_y, at_right, pltpu.roll(m, cells - cells_y, 1))
        dx = xp - xm
        flow = jnp.concatenate(
            [
                dx[1:2],
                dx[0:1] + dx[4:5] + dx[8:9],
                dx[5:6],
                dx[6:7],
                2.0 / 3.0 * (dx[1:2] + dx[10:11]),
            ],
            axis=0,
        )
        return (xp + xm - 4.0 * m)[0:5], flow

    def across(m):
        yp, ym = across_neighbours(m, cells_y)
        dy = yp - ym
        flow = jnp.concatenate(
            [
                dy[2:3],
                dy[5:6],
                dy[0:1] + dy[4:5] + dy[9:10],
                dy[7:8],
                2.0 / 3.0 * (dy[2:3] + dy[11:12]),
            ],
            axis=0,
        )
        return (yp + ym)[0:5], flow

    shifts = [0, cells - 2 * cells_y, cells - 2 * cells_y, cells - 4 * cells_y]
    placed = [edges if s == 0 else pltpu.roll(edges, s, 1) for s in shifts]
    laplace, flow = along(fixed, placed[0], placed[1])
    laplace_across, flow_across = across(fixed)
    change = spread * (laplace + laplace_across) - 0.25 * (flow + flow_across)
    laplace, flow = along(answer, placed[2], placed[3])
    change_answer = spread * laplace - 0.25 * flow
    message = [
        fixed[0:5],
        change,
        answer[0:5],
        answer[5:6],
        answer[7:8],
        answer[9:10],
        answer[11:12],
        change_answer,
        edges[13:14],
    ]
    spare = QUAD * (sent_ref.shape[2] // cells) - 25
    message = jnp.concatenate(message + [jnp.zeros((spare, cells), jnp.float32)], axis=0)
    for part in range(sent_ref.shape[2] // cells):
        piece = message[part * QUAD : (part + 1) * QUAD]
        for group in range(groups):
            sent_ref[group, :, part * cells : (part + 1) * cells] = piece


def finish_kernel(
    parts_ref,
    reach_ref,
    run_ref,
    back_ref,
    phi_ref,
    table_ref,
    line_ref,
    state_hbm,
    macro_hbm,
    state_ref,
    macro_ref,
    change_ref,
    entry_ref,
    sems,
):
    cells_x, cells_y, velocities = reach_ref.shape
    groups = parts_ref.shape[0]
    tiles = velocities // LANES
    cells = cells_x * cells_y
    sums = [parts_ref[group] for group in range(groups)]
    while len(sums) > 1:
        sums = [sums[n] + sums[n + 1] for n in range(0, len(sums), 2)]
    total = jnp.concatenate(
        [sums[0][:, n * cells : (n + 1) * cells] for n in range(parts_ref.shape[2] // cells)],
        axis=0,
    )
    lane = lax.broadcasted_iota(jnp.int32, (1, cells), 1)
    sums = total[24:25]
    here = jnp.logical_and(lane >= 4 * cells_y, lane < 5 * cells_y)
    incoming = jnp.where(here, pltpu.roll(sums, cells - cells_y, 1), 1.0)
    rho = jnp.where(here, sums, 0.0) / incoming
    width = cells_y
    while width < cells:
        rho = rho + pltpu.roll(rho, width, 1)
        width *= 2
    answer = rho * total[8:24]
    yp, ym = across_neighbours(answer, cells_y)
    dy = yp - ym
    flow = jnp.concatenate(
        [
            dy[4:5],
            dy[7:8],
            dy[2:3] + dy[6:7] + dy[9:10],
            dy[8:9],
            2.0 / 3.0 * (dy[4:5] + dy[10:11]),
        ],
        axis=0,
    )
    spread = line_ref[2:3, :]
    change = total[5:10] + rho * total[19:24] + spread * (yp + ym)[2:7] - 0.25 * flow
    updated = total[0:5] + answer[2:7] + change
    for x in range(cells_x):
        macro_ref[:, x, :] = updated[:, x * cells_y : (x + 1) * cells_y]
    macro_copy = pltpu.make_async_copy(macro_ref, macro_hbm, sems.at[cells_x])
    macro_copy.start()
    spare = jnp.zeros((3, cells), jnp.float32)
    change_ref[...] = columns_product(
        left_parts(jnp.concatenate([change, spare], axis=0)), phi_ref[...]
    )
    columns = jnp.broadcast_to(rho, (8, cells)).T
    density = jnp.broadcast_to(columns[0:cells_y, 0:1], (cells_y, LANES))
    for tile in range(tiles):
        lanes = slice(tile * LANES, (tile + 1) * LANES)
        forward = jnp.broadcast_to(table_ref[0:1, lanes], (cells_y, LANES)) > 0.5
        entry = whole_rows(back_ref, 0, tile, tiles, cells_y)
        mixed = whole_rows(back_ref, 1, tile, tiles, cells_y)
        entry_ref[:, lanes] = entry + jnp.where(forward, density * mixed, 0.0)
    copies = []
    span = 2
    for first in range(0, cells_x, span):
        for tile in range(tiles):
            lanes = slice(tile * LANES, (tile + 1) * LANES)
            entry = entry_ref[:, lanes]
            for x in range(first, first + span):
                change = change_ref[x * cells_y : (x + 1) * cells_y, lanes]
                value = reach_ref[x, :, lanes] * entry + run_ref[x, :, lanes] + change
                state_ref[x, :, lanes] = value
        copy = pltpu.make_async_copy(
            state_ref.at[pl.ds(first, span)], state_hbm.at[pl.ds(first, span)], sems.at[first]
        )
        copy.start()
        copies.append(copy)
    for copy in copies + [macro_copy]:
        copy.wait()


def local(state, macro, relax_rate, velocity, vel_sign, quad_weight, freestream, wall_flag):
    cells_x, cells_y, velocities = state.shape
    fields = macro.shape[0]
    slabs = lax.axis_size("gx")
    groups = lax.axis_size("vert")
    cells = cells_x * cells_y
    tiles = velocities // LANES
    assert slabs == tiles * (cells_y // QUAD) and cells == LANES
    f32 = jnp.float32
    sign = vel_sign.reshape(1, velocities)
    weight = quad_weight.reshape(1, velocities)
    wall = wall_flag.reshape(1, cells_y)
    shape = jax.ShapeDtypeStruct
    near = shape if INTERPRET else pltpu.VMEM

    def held(x):
        return x if INTERPRET else pltpu.with_memory_space_constraint(x, pltpu.VMEM)

    def call(body, outs, scratch, *args, **kwargs):
        return pl.pallas_call(
            body, out_shape=outs, scratch_shapes=scratch, interpret=INTERPRET, **kwargs
        )(*args)

    anywhere = pl.BlockSpec(memory_space=pl.ANY)
    sources = (state, macro, relax_rate, velocity, sign, weight, freestream, wall)
    reach, run, sent, side, psi, phi, table, line = call(
        lambda *refs: maps_kernel(float(cells_x * slabs), groups, *refs),
        (
            near(state.shape, f32),
            near(state.shape, f32),
            near((slabs, 2 * QUAD, LANES), f32),
            near((slabs, 4 * QUAD, LANES), f32),
            near((32, velocities), jnp.bfloat16),
            near((32, velocities), jnp.bfloat16),
            near((8, velocities), f32),
            near((8, cells), f32),
        ),
        [pltpu.VMEM(value.shape, value.dtype) for value in sources]
        + [
            pltpu.VMEM((8, cells), f32),
            pltpu.VMEM((8, velocities), f32),
            pltpu.VMEM((16, velocities), f32),
            pltpu.VMEM((cells, velocities), f32),
            pltpu.VMEM((cells_x + 1, cells_y, LANES), f32),
            pltpu.VMEM((8 * cells_y, velocities), jnp.bfloat16),
            pltpu.VMEM((8, LANES), f32),
            pltpu.SemaphoreType.DMA((cells_y // 8 + 7,)),
        ],
        *sources,
        in_specs=[anywhere] * len(sources),
    )
    reach, run, side = map(held, (reach, run, side))
    psi, phi, table, line = map(held, (psi, phi, table, line))
    maps = held(lax.all_to_all(sent, "gx", 0, 0))
    entries, edges = call(
        lambda *refs: scan_kernel(cells_x, *refs),
        (near((slabs, 2 * QUAD, LANES), f32), near((8, LANES), f32)),
        [pltpu.VMEM((slabs, QUAD, LANES), f32)] * 2,
        maps,
        side,
    )
    edges = held(edges)
    back = held(lax.all_to_all(entries, "gx", 0, 0))
    partial_sums = call(
        lambda *refs: moments_kernel(groups, slabs, *refs),
        near((groups, QUAD, SENT_PARTS * cells), f32),
        [
            pltpu.VMEM((6 * cells, velocities), jnp.bfloat16),
            pltpu.VMEM((16, cells), f32),
        ],
        reach,
        run,
        back,
        psi,
        table,
        line,
        edges,
    )
    parts = held(lax.all_to_all(partial_sums, "vert", 0, 0))
    new_state, new_macro = call(
        finish_kernel,
        (shape(state.shape, f32), shape(macro.shape, f32)),
        [
            pltpu.VMEM(state.shape, f32),
            pltpu.VMEM(macro.shape, f32),
            pltpu.VMEM((cells, velocities), f32),
            pltpu.VMEM((cells_y, velocities), f32),
            pltpu.SemaphoreType.DMA((cells_x + 1,)),
        ],
        parts,
        reach,
        run,
        back,
        phi,
        table,
        line,
        out_specs=(anywhere, anywhere),
    )
    return new_state, new_macro


def solution(mesh):
    return jax.shard_map(
        local,
        mesh=mesh,
        in_specs=(
            P("gx", None, "vert"),
            P(None, "gx", None),
            P("gx", None),
            P(None, "vert"),
            P("vert"),
            P("vert"),
            P(None, "vert"),
            P(),
        ),
        out_specs=(P("gx", None, "vert"), P(None, "gx", None)),
        check_vma=False,
    )
```

```python
import jax
import jax.numpy as jnp
from jax import lax
from jax.experimental import pallas as pl
from jax.experimental.pallas import tpu as pltpu
from jax.sharding import PartitionSpec as P

LANES = 128
QUAD = 4
EDGE_ROWS = (0, 1, 2, 3, 4, 5, 6, 8, 10)
SENT_PARTS = 7
INTERPRET = False


def left_parts(value):
    high = value.astype(jnp.bfloat16).astype(jnp.float32)
    return jnp.concatenate([high, value - high, high, jnp.zeros_like(high)], axis=0).astype(
        jnp.bfloat16
    )


def right_parts(value):
    high = value.astype(jnp.bfloat16).astype(jnp.float32)
    return jnp.concatenate([high, high, value - high, jnp.zeros_like(high)], axis=0).astype(
        jnp.bfloat16
    )


def columns_product(left, right):
    return lax.dot_general(
        left, right, (((0,), (0,)), ((), ())), preferred_element_type=jnp.float32
    )


def split_put(ref, row, lanes, value):
    half = ref.shape[0] // 2
    count = value.shape[0]
    high = value.astype(jnp.bfloat16)
    ref[row : row + count, lanes] = high
    ref[half + row : half + row + count, lanes] = (value - high.astype(jnp.float32)).astype(
        jnp.bfloat16
    )


def split_moments(psi_ref, left_ref):
    half = left_ref.shape[0] // 2
    product = lax.dot_general(
        psi_ref[...],
        left_ref[...],
        (((1,), (1,)), ((), ())),
        preferred_element_type=jnp.float32,
    )
    return product[0:16, 0:half] + product[16:32, 0:half] + product[0:16, half:]


def maps_kernel(
    total_cells,
    groups,
    state_hbm,
    macro_hbm,
    relax_hbm,
    velocity_hbm,
    sign_hbm,
    weight_hbm,
    free_hbm,
    wall_hbm,
    reach_ref,
    run_ref,
    sent_ref,
    side_ref,
    psi_ref,
    phi_ref,
    table_ref,
    line_ref,
    state_ref,
    macro_ref,
    relax_ref,
    velocity_ref,
    sign_ref,
    weight_ref,
    free_ref,
    wall_ref,
    cells_ref,
    basis_ref,
    moment_ref,
    equil_ref,
    spread_ref,
    left_ref,
    right_ref,
    message_ref,
    sems,
):
    fields, cells_x, cells_y = macro_ref.shape
    velocities = state_ref.shape[2]
    tiles = velocities // LANES
    halves = cells_y // 8
    small = [
        pltpu.make_async_copy(source, target, sems.at[halves + n])
        for n, (source, target) in enumerate(
            (
                (velocity_hbm, velocity_ref),
                (sign_hbm, sign_ref),
                (weight_hbm, weight_ref),
                (macro_hbm, macro_ref),
                (relax_hbm, relax_ref),
                (wall_hbm, wall_ref),
                (free_hbm, free_ref),
            )
        )
    ]
    large = [
        pltpu.make_async_copy(
            state_hbm.at[:, pl.ds(half * 8, 8), :],
            state_ref.at[:, pl.ds(half * 8, 8), :],
            sems.at[half],
        )
        for half in range(halves)
    ]
    for copy in large + small:
        copy.start()
    for ref in (cells_ref, basis_ref, moment_ref, table_ref, line_ref, message_ref):
        ref[...] = jnp.zeros_like(ref)
    for copy in small:
        copy.wait()
    for x in range(cells_x):
        where = slice(x * cells_y, (x + 1) * cells_y)
        cells_ref[0:fields, where] = macro_ref[:, x, :]
        line_ref[0:1, where] = relax_ref[x : x + 1, :]
    line_ref[1:2, 0:cells_y] = (wall_ref[...] == 1).astype(jnp.float32)
    columns = line_ref[...].T
    for x in range(cells_x):
        spread_ref[x] = jnp.broadcast_to(
            columns[x * cells_y : (x + 1) * cells_y, 0:1], (cells_y, LANES)
        )
    spread_ref[cells_x] = jnp.broadcast_to(columns[0:cells_y, 1:2], (cells_y, LANES))
    relax_row = line_ref[0:1, :]
    line_ref[2:3, :] = 0.2 / (1.0 + relax_row)
    message_ref[0:1, :] = relax_row

    magnitude = velocity_ref[0:1, :]
    positive = sign_ref[...] == 1
    cx = jnp.where(positive, magnitude, -magnitude)
    cy = velocity_ref[1:2, :]
    cz = velocity_ref[2:3, :]
    square = cx * cx + cy * cy + cz * cz
    for k, row in enumerate((jnp.ones_like(cx), 2.0 * cx, 2.0 * cy, 2.0 * cz, square - 1.5)):
        basis_ref[k : k + 1, :] = row
    table_ref[0:1, :] = jnp.where(positive, 1.0, 0.0)
    table_ref[1:2, :] = total_cells * magnitude
    phi = right_parts(basis_ref[...])
    phi_ref[...] = phi
    equil_ref[...] = columns_product(left_parts(cells_ref[...]), phi)
    weight = weight_ref[...] / (velocities * groups)
    heat = 0.2 * (square - 2.5)
    for k, row in enumerate(
        (
            jnp.ones_like(cx),
            cx,
            cy,
            cz,
            2.0 / 3.0 * square - 1.0,
            2.0 * cx * cy,
            2.0 * cx * cz,
            2.0 * cy * cz,
            2.0 * (cx * cx - square / 3.0),
            2.0 * (cy * cy - square / 3.0),
            heat * cx,
            heat * cy,
            heat * cz,
            magnitude,
        )
    ):
        moment_ref[k : k + 1, :] = weight * row
    high = moment_ref[...].astype(jnp.bfloat16)
    psi_ref[0:16] = high
    psi_ref[16:32] = (moment_ref[...] - high.astype(jnp.float32)).astype(jnp.bfloat16)

    last = cells_x - 1
    large[0].wait()
    for half in range(halves):
        edge_ref = (left_ref, right_ref)[half]
        rows = slice(half * 8, half * 8 + 8)
        for tile in range(tiles):
            lanes = slice(tile * LANES, (tile + 1) * LANES)
            forward = jnp.broadcast_to(table_ref[0:1, lanes], (8, LANES)) > 0.5
            courant = jnp.broadcast_to(table_ref[1:2, lanes], (8, LANES))
            base = 1.0 + courant
            decay = []
            driven = []
            for x in range(cells_x):
                relax = spread_ref[x, rows]
                first = x * cells_y + half * 8
                equil = equil_ref[first : first + 8, lanes]
                inverse = 1.0 / (base + relax)
                decay.append(courant * inverse)
                driven.append((state_ref[x, rows, lanes] + relax * equil) * inverse)
            steps = [jnp.where(forward, decay[t], decay[last - t]) for t in range(cells_x)]
            gains = [jnp.where(forward, driven[t], driven[last - t]) for t in range(cells_x)]
            products = [steps[0]]
            runs = [gains[0]]
            for t in range(1, cells_x):
                products.append(steps[t] * products[-1])
                runs.append(steps[t] * runs[-1] + gains[t])
            for x in range(cells_x):
                reach_ref[x, rows, lanes] = jnp.where(forward, products[x], products[last - x])
                run_ref[x, rows, lanes] = jnp.where(forward, runs[x], runs[last - x])
            wall = spread_ref[cells_x, rows] > 0.5
            diffuse = jnp.logical_and(forward, wall)
            fixed = jnp.where(diffuse, 0.0, free_ref[rows, lanes])
            unit = jnp.where(diffuse, 1.0, 0.0)
            direction = jnp.where(forward, 1.0, 0.0)
            first_gain = gains[0]
            outward = jnp.where(forward, first_gain, 0.0)
            split_put(edge_ref, 0, lanes, outward)
            split_put(edge_ref, 8, lanes, first_gain - outward)
            for part in range(8 // QUAD):
                owner = (half * (8 // QUAD) + part) * tiles + tile
                quad = slice(part * QUAD, (part + 1) * QUAD)
                sent_ref[owner, 0:QUAD, :] = runs[last][quad]
                for slot, value in enumerate((fixed, unit, direction, courant)):
                    side_ref[owner, slot * QUAD : (slot + 1) * QUAD, :] = value[quad]
        if half + 1 < halves:
            large[half + 1].wait()
        edge_moments = split_moments(psi_ref, edge_ref)
        for n, k in enumerate(EDGE_ROWS):
            row = 1 + n // QUAD
            start = (n % QUAD) * 2 * cells_y + half * 16
            message_ref[row : row + 1, start : start + 16] = edge_moments[k : k + 1, :]
    message = message_ref[0:QUAD]
    for owner in range(sent_ref.shape[0]):
        sent_ref[owner, QUAD : 2 * QUAD, :] = message


def scan_kernel(cells_x, maps_ref, side_ref, sent_ref, edges_ref, entry_ref, product_ref):
    slabs = maps_ref.shape[0]
    me = lax.axis_index("gx")
    side = side_ref[me]
    fixed = side[0:QUAD]
    unit = side[QUAD : 2 * QUAD]
    forward = side[2 * QUAD : 3 * QUAD] > 0.5
    courant = side[3 * QUAD : 4 * QUAD]
    base = 1.0 + side[3 * QUAD : 3 * QUAD + 1]
    power = courant
    reach = 1
    while reach < cells_x:
        power = power * power
        reach *= 2
    below = jnp.maximum(me - 1, 0)
    above = jnp.minimum(me + 1, slabs - 1)
    edges_ref[0:QUAD] = maps_ref[below, QUAD : 2 * QUAD]
    edges_ref[QUAD : 2 * QUAD] = maps_ref[above, QUAD : 2 * QUAD]
    relax = jnp.concatenate([maps_ref[i, QUAD : QUAD + 1] for i in range(slabs)], axis=0).T
    cells_y = relax.shape[0] // cells_x
    quads = cells_y // QUAD
    index = me // (slabs // quads)
    high = index // 2 == 1
    odd = index % 2 == 1
    picked = []
    for x in range(cells_x):
        rows = relax[x * cells_y : (x + 1) * cells_y]
        rows = jnp.where(high, rows[8:16], rows[0:8])
        picked.append(jnp.where(odd, rows[QUAD:8], rows[0:QUAD]))
    relax = jnp.concatenate(picked, axis=0)
    cells = cells_x * QUAD
    for i in range(slabs):
        divisors = base + jnp.broadcast_to(relax[:, i : i + 1], (cells, LANES))
        product = divisors[0:8]
        for first in range(8, cells, 8):
            product = product * divisors[first : first + 8]
        product = product[0:QUAD] * product[QUAD:8]
        product_ref[i] = power * (1.0 / product)
    value = fixed
    for i in range(slabs - 1, -1, -1):
        entry_ref[i] = value
        value = product_ref[i] * value + maps_ref[i, 0:QUAD]
    leaving = value
    value = fixed
    answer = unit
    for i in range(slabs):
        sent_ref[i, 0:QUAD] = jnp.where(forward, value, entry_ref[i])
        sent_ref[i, QUAD : 2 * QUAD] = jnp.where(forward, answer, leaving)
        value = product_ref[i] * value + maps_ref[i, 0:QUAD]
        answer = product_ref[i] * answer


def whole_rows(back_ref, slot, tile, tiles, cells_y):
    return jnp.concatenate(
        [
            back_ref[quad * tiles + tile, slot * QUAD : (slot + 1) * QUAD]
            for quad in range(cells_y // QUAD)
        ],
        axis=0,
    )


def across_neighbours(m, cells_y):
    cells = m.shape[1]
    y = lax.broadcasted_iota(jnp.int32, m.shape, 1) % cells_y
    yp = jnp.where(y == cells_y - 1, pltpu.roll(m, cells_y - 1, 1), pltpu.roll(m, cells - 1, 1))
    ym = jnp.where(y == 0, pltpu.roll(m, cells - cells_y + 1, 1), pltpu.roll(m, 1, 1))
    return yp, ym


def moments_kernel(
    groups,
    slabs,
    reach_ref,
    run_ref,
    back_ref,
    psi_ref,
    table_ref,
    line_ref,
    edges_ref,
    sent_ref,
    left_ref,
    near_ref,
):
    cells_x, cells_y, velocities = reach_ref.shape
    tiles = velocities // LANES
    cells = cells_x * cells_y
    me = lax.axis_index("gx")
    from_left = jnp.where(me > 0, 1.0, 0.0)
    from_right = jnp.where(me < slabs - 1, 1.0, 0.0)

    def put(row, value, lanes):
        split_put(left_ref, row, lanes, value)

    near_ref[...] = jnp.zeros_like(near_ref)
    tile = edges_ref[...]
    place = lax.broadcasted_iota(jnp.int32, tile.shape, 1) % (2 * cells_y) // 8
    tile = jnp.where(
        place == 1,
        pltpu.roll(tile, cells - 8, 1),
        jnp.where(place == 2, pltpu.roll(tile, 8, 1), tile),
    )
    for n, k in enumerate(EDGE_ROWS):
        row = 1 + n // QUAD
        start = (n % QUAD) * 2 * cells_y
        near_ref[k : k + 1, 0:cells_y] = (
            tile[row : row + 1, start + cells_y : start + 2 * cells_y] * from_left
        )
        near_ref[k : k + 1, cells_y : 2 * cells_y] = (
            tile[QUAD + row : QUAD + row + 1, start : start + cells_y] * from_right
        )
    columns = edges_ref[...].T
    relax_left = jnp.broadcast_to(columns[cells - cells_y : cells, 0:1], (cells_y, LANES))
    relax_right = jnp.broadcast_to(columns[0:cells_y, QUAD : QUAD + 1], (cells_y, LANES))
    for tile in range(tiles):
        lanes = slice(tile * LANES, (tile + 1) * LANES)
        forward = jnp.broadcast_to(table_ref[0:1, lanes], (cells_y, LANES)) > 0.5
        courant = jnp.broadcast_to(table_ref[1:2, lanes], (cells_y, LANES))
        entry = whole_rows(back_ref, 0, tile, tiles, cells_y)
        mixed = whole_rows(back_ref, 1, tile, tiles, cells_y)
        answer = jnp.where(forward, mixed, 0.0)
        leaving = jnp.where(forward, 0.0, mixed)
        for x in range(cells_x):
            reach = reach_ref[x, :, lanes]
            value = reach * entry + run_ref[x, :, lanes]
            put(x * cells_y, value, lanes)
            put(cells + x * cells_y, reach * answer, lanes)
            if x == 0:
                outgoing = value
            if x == cells_x - 1:
                outgoing = jnp.where(forward, value, outgoing)
                outgoing_answer = reach * answer
        decay = courant / (1.0 + courant + jnp.where(forward, relax_right, relax_left))
        inside = jnp.where(forward, from_right, from_left)
        near = decay * outgoing * inside
        near_answer = decay * outgoing_answer * inside
        row = 2 * cells
        put(row, jnp.where(forward, entry * from_left, near), lanes)
        put(row + cells_y, jnp.where(forward, near, entry * from_right), lanes)
        put(row + 2 * cells_y, answer * from_left, lanes)
        put(row + 3 * cells_y, near_answer, lanes)
        put(row + 4 * cells_y, leaving, lanes)
        put(row + 5 * cells_y, jnp.where(forward, 1.0, 0.0), lanes)
        put(row + 6 * cells_y, jnp.zeros_like(entry), lanes)
        put(row + 7 * cells_y, jnp.zeros_like(entry), lanes)

    total = split_moments(psi_ref, left_ref)
    fixed = total[:, 0:cells]
    answer = total[:, cells : 2 * cells]
    edges = total[:, 2 * cells : 3 * cells] + near_ref[...]

    spread = line_ref[2:3, :]
    lane = lax.broadcasted_iota(jnp.int32, (16, cells), 1)

    def along(m, at_left, at_right):
        xm = jnp.where(lane < cells_y, at_left, pltpu.roll(m, cells_y, 1))
        xp = jnp.where(lane >= cells - cells_y, at_right, pltpu.roll(m, cells - cells_y, 1))
        dx = xp - xm
        flow = jnp.concatenate(
            [
                dx[1:2],
                dx[0:1] + dx[4:5] + dx[8:9],
                dx[5:6],
                dx[6:7],
                2.0 / 3.0 * (dx[1:2] + dx[10:11]),
            ],
            axis=0,
        )
        return (xp + xm - 4.0 * m)[0:5], flow

    def across(m):
        yp, ym = across_neighbours(m, cells_y)
        dy = yp - ym
        flow = jnp.concatenate(
            [
                dy[2:3],
                dy[5:6],
                dy[0:1] + dy[4:5] + dy[9:10],
                dy[7:8],
                2.0 / 3.0 * (dy[2:3] + dy[11:12]),
            ],
            axis=0,
        )
        return (yp + ym)[0:5], flow

    shifts = [0, cells - 2 * cells_y, cells - 2 * cells_y, cells - 4 * cells_y]
    placed = [edges if s == 0 else pltpu.roll(edges, s, 1) for s in shifts]
    laplace, flow = along(fixed, placed[0], placed[1])
    laplace_across, flow_across = across(fixed)
    change = spread * (laplace + laplace_across) - 0.25 * (flow + flow_across)
    laplace, flow = along(answer, placed[2], placed[3])
    change_answer = spread * laplace - 0.25 * flow
    message = [
        fixed[0:5],
        change,
        answer[0:5],
        answer[5:6],
        answer[7:8],
        answer[9:10],
        answer[11:12],
        change_answer,
        edges[13:14],
    ]
    spare = QUAD * (sent_ref.shape[2] // cells) - 25
    message = jnp.concatenate(message + [jnp.zeros((spare, cells), jnp.float32)], axis=0)
    for part in range(sent_ref.shape[2] // cells):
        piece = message[part * QUAD : (part + 1) * QUAD]
        for group in range(groups):
            sent_ref[group, :, part * cells : (part + 1) * cells] = piece


def finish_kernel(
    parts_ref,
    reach_ref,
    run_ref,
    back_ref,
    phi_ref,
    table_ref,
    line_ref,
    state_hbm,
    macro_hbm,
    state_ref,
    macro_ref,
    change_ref,
    entry_ref,
    sems,
):
    cells_x, cells_y, velocities = reach_ref.shape
    groups = parts_ref.shape[0]
    tiles = velocities // LANES
    cells = cells_x * cells_y
    sums = [parts_ref[group] for group in range(groups)]
    while len(sums) > 1:
        sums = [sums[n] + sums[n + 1] for n in range(0, len(sums), 2)]
    total = jnp.concatenate(
        [sums[0][:, n * cells : (n + 1) * cells] for n in range(parts_ref.shape[2] // cells)],
        axis=0,
    )
    lane = lax.broadcasted_iota(jnp.int32, (1, cells), 1)
    sums = total[24:25]
    here = jnp.logical_and(lane >= 4 * cells_y, lane < 5 * cells_y)
    incoming = jnp.where(here, pltpu.roll(sums, cells - cells_y, 1), 1.0)
    rho = jnp.where(here, sums, 0.0) / incoming
    width = cells_y
    while width < cells:
        rho = rho + pltpu.roll(rho, width, 1)
        width *= 2
    answer = rho * total[8:24]
    yp, ym = across_neighbours(answer, cells_y)
    dy = yp - ym
    flow = jnp.concatenate(
        [
            dy[4:5],
            dy[7:8],
            dy[2:3] + dy[6:7] + dy[9:10],
            dy[8:9],
            2.0 / 3.0 * (dy[4:5] + dy[10:11]),
        ],
        axis=0,
    )
    spread = line_ref[2:3, :]
    change = total[5:10] + rho * total[19:24] + spread * (yp + ym)[2:7] - 0.25 * flow
    updated = total[0:5] + answer[2:7] + change
    for x in range(cells_x):
        macro_ref[:, x, :] = updated[:, x * cells_y : (x + 1) * cells_y]
    macro_copy = pltpu.make_async_copy(macro_ref, macro_hbm, sems.at[cells_x])
    macro_copy.start()
    spare = jnp.zeros((3, cells), jnp.float32)
    change_ref[...] = columns_product(
        left_parts(jnp.concatenate([change, spare], axis=0)), phi_ref[...]
    )
    columns = jnp.broadcast_to(rho, (8, cells)).T
    density = jnp.broadcast_to(columns[0:cells_y, 0:1], (cells_y, LANES))
    for tile in range(tiles):
        lanes = slice(tile * LANES, (tile + 1) * LANES)
        forward = jnp.broadcast_to(table_ref[0:1, lanes], (cells_y, LANES)) > 0.5
        entry = whole_rows(back_ref, 0, tile, tiles, cells_y)
        mixed = whole_rows(back_ref, 1, tile, tiles, cells_y)
        entry_ref[:, lanes] = entry + jnp.where(forward, density * mixed, 0.0)
    copies = []
    span = 2
    for first in range(0, cells_x, span):
        for tile in range(tiles):
            lanes = slice(tile * LANES, (tile + 1) * LANES)
            entry = entry_ref[:, lanes]
            for x in range(first, first + span):
                change = change_ref[x * cells_y : (x + 1) * cells_y, lanes]
                value = reach_ref[x, :, lanes] * entry + run_ref[x, :, lanes] + change
                state_ref[x, :, lanes] = value
        copy = pltpu.make_async_copy(
            state_ref.at[pl.ds(first, span)], state_hbm.at[pl.ds(first, span)], sems.at[first]
        )
        copy.start()
        copies.append(copy)
    for copy in copies + [macro_copy]:
        copy.wait()


def local(state, macro, relax_rate, velocity, vel_sign, quad_weight, freestream, wall_flag):
    cells_x, cells_y, velocities = state.shape
    fields = macro.shape[0]
    slabs = lax.axis_size("gx")
    groups = lax.axis_size("vert")
    cells = cells_x * cells_y
    tiles = velocities // LANES
    assert slabs == tiles * (cells_y // QUAD) and cells == LANES
    f32 = jnp.float32
    sign = vel_sign.reshape(1, velocities)
    weight = quad_weight.reshape(1, velocities)
    wall = wall_flag.reshape(1, cells_y)
    shape = jax.ShapeDtypeStruct
    near = shape if INTERPRET else pltpu.VMEM

    def held(x):
        return x if INTERPRET else pltpu.with_memory_space_constraint(x, pltpu.VMEM)

    def call(body, outs, scratch, *args, **kwargs):
        return pl.pallas_call(
            body, out_shape=outs, scratch_shapes=scratch, interpret=INTERPRET, **kwargs
        )(*args)

    anywhere = pl.BlockSpec(memory_space=pl.ANY)
    sources = (state, macro, relax_rate, velocity, sign, weight, freestream, wall)
    reach, run, sent, side, psi, phi, table, line = call(
        lambda *refs: maps_kernel(float(cells_x * slabs), groups, *refs),
        (
            near(state.shape, f32),
            near(state.shape, f32),
            near((slabs, 2 * QUAD, LANES), f32),
            near((slabs, 4 * QUAD, LANES), f32),
            near((32, velocities), jnp.bfloat16),
            near((32, velocities), jnp.bfloat16),
            near((8, velocities), f32),
            near((8, cells), f32),
        ),
        [pltpu.VMEM(value.shape, value.dtype) for value in sources]
        + [
            pltpu.VMEM((8, cells), f32),
            pltpu.VMEM((8, velocities), f32),
            pltpu.VMEM((16, velocities), f32),
            pltpu.VMEM((cells, velocities), f32),
            pltpu.VMEM((cells_x + 1, cells_y, LANES), f32),
            pltpu.VMEM((32, velocities), jnp.bfloat16),
            pltpu.VMEM((32, velocities), jnp.bfloat16),
            pltpu.VMEM((8, LANES), f32),
            pltpu.SemaphoreType.DMA((cells_y // 8 + 7,)),
        ],
        *sources,
        in_specs=[anywhere] * len(sources),
    )
    reach, run, side = map(held, (reach, run, side))
    psi, phi, table, line = map(held, (psi, phi, table, line))
    maps = held(lax.all_to_all(sent, "gx", 0, 0))
    entries, edges = call(
        lambda *refs: scan_kernel(cells_x, *refs),
        (near((slabs, 2 * QUAD, LANES), f32), near((8, LANES), f32)),
        [pltpu.VMEM((slabs, QUAD, LANES), f32)] * 2,
        maps,
        side,
    )
    edges = held(edges)
    back = held(lax.all_to_all(entries, "gx", 0, 0))
    partial_sums = call(
        lambda *refs: moments_kernel(groups, slabs, *refs),
        near((groups, QUAD, SENT_PARTS * cells), f32),
        [
            pltpu.VMEM((6 * cells, velocities), jnp.bfloat16),
            pltpu.VMEM((16, cells), f32),
        ],
        reach,
        run,
        back,
        psi,
        table,
        line,
        edges,
    )
    parts = held(lax.all_to_all(partial_sums, "vert", 0, 0))
    new_state, new_macro = call(
        finish_kernel,
        (shape(state.shape, f32), shape(macro.shape, f32)),
        [
            pltpu.VMEM(state.shape, f32),
            pltpu.VMEM(macro.shape, f32),
            pltpu.VMEM((cells, velocities), f32),
            pltpu.VMEM((cells_y, velocities), f32),
            pltpu.SemaphoreType.DMA((cells_x + 1,)),
        ],
        parts,
        reach,
        run,
        back,
        phi,
        table,
        line,
        out_specs=(anywhere, anywhere),
    )
    return new_state, new_macro


def solution(mesh):
    return jax.shard_map(
        local,
        mesh=mesh,
        in_specs=(
            P("gx", None, "vert"),
            P(None, "gx", None),
            P("gx", None),
            P(None, "vert"),
            P("vert"),
            P("vert"),
            P(None, "vert"),
            P(),
        ),
        out_specs=(P("gx", None, "vert"), P(None, "gx", None)),
        check_vma=False,
    )
```

```python
import jax
import jax.numpy as jnp
from jax import lax
from jax.experimental import pallas as pl
from jax.experimental.pallas import tpu as pltpu
from jax.sharding import PartitionSpec as P

LANES = 128
QUAD = 4
EDGE_ROWS = (0, 1, 2, 3, 4, 5, 6, 8, 10)
SENT_PARTS = 7
INTERPRET = False


def left_parts(value):
    high = value.astype(jnp.bfloat16).astype(jnp.float32)
    return jnp.concatenate([high, value - high, high, jnp.zeros_like(high)], axis=0).astype(
        jnp.bfloat16
    )


def right_parts(value):
    high = value.astype(jnp.bfloat16).astype(jnp.float32)
    return jnp.concatenate([high, high, value - high, jnp.zeros_like(high)], axis=0).astype(
        jnp.bfloat16
    )


def columns_product(left, right):
    return lax.dot_general(
        left, right, (((0,), (0,)), ((), ())), preferred_element_type=jnp.float32
    )


def split_put(ref, row, lanes, value):
    half = ref.shape[0] // 2
    count = value.shape[0]
    high = value.astype(jnp.bfloat16)
    ref[row : row + count, lanes] = high
    ref[half + row : half + row + count, lanes] = (value - high.astype(jnp.float32)).astype(
        jnp.bfloat16
    )


def split_moments(psi_ref, left_ref):
    half = left_ref.shape[0] // 2
    product = lax.dot_general(
        psi_ref[...],
        left_ref[...],
        (((1,), (1,)), ((), ())),
        preferred_element_type=jnp.float32,
    )
    return product[0:16, 0:half] + product[16:32, 0:half] + product[0:16, half:]


def maps_kernel(
    total_cells,
    groups,
    state_hbm,
    macro_hbm,
    relax_hbm,
    velocity_hbm,
    sign_hbm,
    weight_hbm,
    free_hbm,
    wall_hbm,
    reach_ref,
    run_ref,
    sent_ref,
    side_ref,
    psi_ref,
    phi_ref,
    table_ref,
    line_ref,
    state_ref,
    macro_ref,
    relax_ref,
    velocity_ref,
    sign_ref,
    weight_ref,
    free_ref,
    wall_ref,
    cells_ref,
    basis_ref,
    moment_ref,
    equil_ref,
    spread_ref,
    left_ref,
    edge_decay_ref,
    edge_driven_ref,
    message_ref,
    sems,
):
    fields, cells_x, cells_y = macro_ref.shape
    velocities = state_ref.shape[2]
    tiles = velocities // LANES
    halves = cells_y // 8
    last = cells_x - 1
    large = [
        pltpu.make_async_copy(
            state_hbm.at[pl.ds(start, count)], state_ref.at[pl.ds(start, count)], sems.at[n]
        )
        for n, (start, count) in enumerate(((0, 1), (last, 1), (1, cells_x - 2)))
    ]
    small = [
        pltpu.make_async_copy(source, target, sems.at[len(large) + n])
        for n, (source, target) in enumerate(
            (
                (velocity_hbm, velocity_ref),
                (sign_hbm, sign_ref),
                (weight_hbm, weight_ref),
                (macro_hbm, macro_ref),
                (relax_hbm, relax_ref),
                (wall_hbm, wall_ref),
                (free_hbm, free_ref),
            )
        )
    ]
    for copy in large[0:2] + small + large[2:]:
        copy.start()
    for ref in (cells_ref, basis_ref, moment_ref, table_ref, line_ref, message_ref):
        ref[...] = jnp.zeros_like(ref)
    for copy in small:
        copy.wait()
    for x in range(cells_x):
        where = slice(x * cells_y, (x + 1) * cells_y)
        cells_ref[0:fields, where] = macro_ref[:, x, :]
        line_ref[0:1, where] = relax_ref[x : x + 1, :]
    line_ref[1:2, 0:cells_y] = (wall_ref[...] == 1).astype(jnp.float32)
    columns = line_ref[...].T
    for x in range(cells_x):
        spread_ref[x] = jnp.broadcast_to(
            columns[x * cells_y : (x + 1) * cells_y, 0:1], (cells_y, LANES)
        )
    spread_ref[cells_x] = jnp.broadcast_to(columns[0:cells_y, 1:2], (cells_y, LANES))
    relax_row = line_ref[0:1, :]
    line_ref[2:3, :] = 0.2 / (1.0 + relax_row)
    message_ref[0:1, :] = relax_row

    magnitude = velocity_ref[0:1, :]
    positive = sign_ref[...] == 1
    cx = jnp.where(positive, magnitude, -magnitude)
    cy = velocity_ref[1:2, :]
    cz = velocity_ref[2:3, :]
    square = cx * cx + cy * cy + cz * cz
    for k, row in enumerate((jnp.ones_like(cx), 2.0 * cx, 2.0 * cy, 2.0 * cz, square - 1.5)):
        basis_ref[k : k + 1, :] = row
    table_ref[0:1, :] = jnp.where(positive, 1.0, 0.0)
    table_ref[1:2, :] = total_cells * magnitude
    phi = right_parts(basis_ref[...])
    phi_ref[...] = phi
    equil_ref[...] = columns_product(left_parts(cells_ref[...]), phi)
    weight = weight_ref[...] / (velocities * groups)
    heat = 0.2 * (square - 2.5)
    for k, row in enumerate(
        (
            jnp.ones_like(cx),
            cx,
            cy,
            cz,
            2.0 / 3.0 * square - 1.0,
            2.0 * cx * cy,
            2.0 * cx * cz,
            2.0 * cy * cz,
            2.0 * (cx * cx - square / 3.0),
            2.0 * (cy * cy - square / 3.0),
            heat * cx,
            heat * cy,
            heat * cz,
            magnitude,
        )
    ):
        moment_ref[k : k + 1, :] = weight * row
    high = moment_ref[...].astype(jnp.bfloat16)
    psi_ref[0:16] = high
    psi_ref[16:32] = (moment_ref[...] - high.astype(jnp.float32)).astype(jnp.bfloat16)

    def cell(x, rows, lanes, courant):
        relax = spread_ref[x, rows]
        first = x * cells_y + rows.start
        inverse = 1.0 / (1.0 + courant + relax)
        gain = state_ref[x, rows, lanes] + relax * equil_ref[first : first + 8, lanes]
        return courant * inverse, gain * inverse

    def settings(lanes):
        forward = jnp.broadcast_to(table_ref[0:1, lanes], (8, LANES)) > 0.5
        return forward, jnp.broadcast_to(table_ref[1:2, lanes], (8, LANES))

    for copy in large[0:2]:
        copy.wait()
    for half in range(halves):
        rows = slice(half * 8, half * 8 + 8)
        for tile in range(tiles):
            lanes = slice(tile * LANES, (tile + 1) * LANES)
            forward, courant = settings(lanes)
            pair = [cell(x, rows, lanes, courant) for x in (0, last)]
            for n in range(2):
                edge_decay_ref[n, rows, lanes] = pair[n][0]
                edge_driven_ref[n, rows, lanes] = pair[n][1]
            split_put(left_ref, half * 8, lanes, jnp.where(forward, pair[0][1], 0.0))
            split_put(left_ref, cells_y + half * 8, lanes, jnp.where(forward, 0.0, pair[1][1]))
    large[2].wait()
    edge_moments = split_moments(psi_ref, left_ref)
    for n, k in enumerate(EDGE_ROWS):
        row = 1 + n // QUAD
        start = (n % QUAD) * 2 * cells_y
        message_ref[row : row + 1, start : start + 2 * cells_y] = edge_moments[k : k + 1, :]
    for half in range(halves):
        rows = slice(half * 8, half * 8 + 8)
        for tile in range(tiles):
            lanes = slice(tile * LANES, (tile + 1) * LANES)
            forward, courant = settings(lanes)
            decay = [edge_decay_ref[0, rows, lanes]]
            driven = [edge_driven_ref[0, rows, lanes]]
            for x in range(1, last):
                one, two = cell(x, rows, lanes, courant)
                decay.append(one)
                driven.append(two)
            decay.append(edge_decay_ref[1, rows, lanes])
            driven.append(edge_driven_ref[1, rows, lanes])
            steps = [jnp.where(forward, decay[t], decay[last - t]) for t in range(cells_x)]
            gains = [jnp.where(forward, driven[t], driven[last - t]) for t in range(cells_x)]
            products = [steps[0]]
            runs = [gains[0]]
            for t in range(1, cells_x):
                products.append(steps[t] * products[-1])
                runs.append(steps[t] * runs[-1] + gains[t])
            for x in range(cells_x):
                reach_ref[x, rows, lanes] = jnp.where(forward, products[x], products[last - x])
                run_ref[x, rows, lanes] = jnp.where(forward, runs[x], runs[last - x])
            wall = spread_ref[cells_x, rows] > 0.5
            diffuse = jnp.logical_and(forward, wall)
            fixed = jnp.where(diffuse, 0.0, free_ref[rows, lanes])
            unit = jnp.where(diffuse, 1.0, 0.0)
            direction = jnp.where(forward, 1.0, 0.0)
            for part in range(8 // QUAD):
                owner = (half * (8 // QUAD) + part) * tiles + tile
                quad = slice(part * QUAD, (part + 1) * QUAD)
                sent_ref[owner, 0:QUAD, :] = runs[last][quad]
                for slot, value in enumerate((fixed, unit, direction, courant)):
                    side_ref[owner, slot * QUAD : (slot + 1) * QUAD, :] = value[quad]
    message = message_ref[0:QUAD]
    for owner in range(sent_ref.shape[0]):
        sent_ref[owner, QUAD : 2 * QUAD, :] = message


def scan_kernel(cells_x, maps_ref, side_ref, sent_ref, edges_ref, entry_ref, product_ref):
    slabs = maps_ref.shape[0]
    me = lax.axis_index("gx")
    side = side_ref[me]
    fixed = side[0:QUAD]
    unit = side[QUAD : 2 * QUAD]
    forward = side[2 * QUAD : 3 * QUAD] > 0.5
    courant = side[3 * QUAD : 4 * QUAD]
    base = 1.0 + side[3 * QUAD : 3 * QUAD + 1]
    power = courant
    reach = 1
    while reach < cells_x:
        power = power * power
        reach *= 2
    below = jnp.maximum(me - 1, 0)
    above = jnp.minimum(me + 1, slabs - 1)
    edges_ref[0:QUAD] = maps_ref[below, QUAD : 2 * QUAD]
    edges_ref[QUAD : 2 * QUAD] = maps_ref[above, QUAD : 2 * QUAD]
    relax = jnp.concatenate([maps_ref[i, QUAD : QUAD + 1] for i in range(slabs)], axis=0).T
    cells_y = relax.shape[0] // cells_x
    quads = cells_y // QUAD
    index = me // (slabs // quads)
    high = index // 2 == 1
    odd = index % 2 == 1
    picked = []
    for x in range(cells_x):
        rows = relax[x * cells_y : (x + 1) * cells_y]
        rows = jnp.where(high, rows[8:16], rows[0:8])
        picked.append(jnp.where(odd, rows[QUAD:8], rows[0:QUAD]))
    relax = jnp.concatenate(picked, axis=0)
    cells = cells_x * QUAD
    for i in range(slabs):
        divisors = base + jnp.broadcast_to(relax[:, i : i + 1], (cells, LANES))
        product = divisors[0:8]
        for first in range(8, cells, 8):
            product = product * divisors[first : first + 8]
        product = product[0:QUAD] * product[QUAD:8]
        product_ref[i] = power * (1.0 / product)
    value = fixed
    for i in range(slabs - 1, -1, -1):
        entry_ref[i] = value
        value = product_ref[i] * value + maps_ref[i, 0:QUAD]
    leaving = value
    value = fixed
    answer = unit
    for i in range(slabs):
        sent_ref[i, 0:QUAD] = jnp.where(forward, value, entry_ref[i])
        sent_ref[i, QUAD : 2 * QUAD] = jnp.where(forward, answer, leaving)
        value = product_ref[i] * value + maps_ref[i, 0:QUAD]
        answer = product_ref[i] * answer


def whole_rows(back_ref, slot, tile, tiles, cells_y):
    return jnp.concatenate(
        [
            back_ref[quad * tiles + tile, slot * QUAD : (slot + 1) * QUAD]
            for quad in range(cells_y // QUAD)
        ],
        axis=0,
    )


def across_neighbours(m, cells_y):
    cells = m.shape[1]
    y = lax.broadcasted_iota(jnp.int32, m.shape, 1) % cells_y
    yp = jnp.where(y == cells_y - 1, pltpu.roll(m, cells_y - 1, 1), pltpu.roll(m, cells - 1, 1))
    ym = jnp.where(y == 0, pltpu.roll(m, cells - cells_y + 1, 1), pltpu.roll(m, 1, 1))
    return yp, ym


def moments_kernel(
    groups,
    slabs,
    reach_ref,
    run_ref,
    back_ref,
    psi_ref,
    table_ref,
    line_ref,
    edges_ref,
    sent_ref,
    left_ref,
    near_ref,
):
    cells_x, cells_y, velocities = reach_ref.shape
    tiles = velocities // LANES
    cells = cells_x * cells_y
    me = lax.axis_index("gx")
    from_left = jnp.where(me > 0, 1.0, 0.0)
    from_right = jnp.where(me < slabs - 1, 1.0, 0.0)

    def put(row, value, lanes):
        split_put(left_ref, row, lanes, value)

    near_ref[...] = jnp.zeros_like(near_ref)
    for n, k in enumerate(EDGE_ROWS):
        row = 1 + n // QUAD
        start = (n % QUAD) * 2 * cells_y
        near_ref[k : k + 1, 0:cells_y] = (
            edges_ref[row : row + 1, start + cells_y : start + 2 * cells_y] * from_left
        )
        near_ref[k : k + 1, cells_y : 2 * cells_y] = (
            edges_ref[QUAD + row : QUAD + row + 1, start : start + cells_y] * from_right
        )
    columns = edges_ref[...].T
    relax_left = jnp.broadcast_to(columns[cells - cells_y : cells, 0:1], (cells_y, LANES))
    relax_right = jnp.broadcast_to(columns[0:cells_y, QUAD : QUAD + 1], (cells_y, LANES))
    for tile in range(tiles):
        lanes = slice(tile * LANES, (tile + 1) * LANES)
        forward = jnp.broadcast_to(table_ref[0:1, lanes], (cells_y, LANES)) > 0.5
        courant = jnp.broadcast_to(table_ref[1:2, lanes], (cells_y, LANES))
        entry = whole_rows(back_ref, 0, tile, tiles, cells_y)
        mixed = whole_rows(back_ref, 1, tile, tiles, cells_y)
        answer = jnp.where(forward, mixed, 0.0)
        leaving = jnp.where(forward, 0.0, mixed)
        for x in range(cells_x):
            reach = reach_ref[x, :, lanes]
            value = reach * entry + run_ref[x, :, lanes]
            put(x * cells_y, value, lanes)
            put(cells + x * cells_y, reach * answer, lanes)
            if x == 0:
                outgoing = value
            if x == cells_x - 1:
                outgoing = jnp.where(forward, value, outgoing)
                outgoing_answer = reach * answer
        decay = courant / (1.0 + courant + jnp.where(forward, relax_right, relax_left))
        inside = jnp.where(forward, from_right, from_left)
        near = decay * outgoing * inside
        near_answer = decay * outgoing_answer * inside
        row = 2 * cells
        put(row, jnp.where(forward, entry * from_left, near), lanes)
        put(row + cells_y, jnp.where(forward, near, entry * from_right), lanes)
        put(row + 2 * cells_y, answer * from_left, lanes)
        put(row + 3 * cells_y, near_answer, lanes)
        put(row + 4 * cells_y, leaving, lanes)
        put(row + 5 * cells_y, jnp.where(forward, 1.0, 0.0), lanes)
        put(row + 6 * cells_y, jnp.zeros_like(entry), lanes)
        put(row + 7 * cells_y, jnp.zeros_like(entry), lanes)

    total = split_moments(psi_ref, left_ref)
    fixed = total[:, 0:cells]
    answer = total[:, cells : 2 * cells]
    edges = total[:, 2 * cells : 3 * cells] + near_ref[...]

    spread = line_ref[2:3, :]
    lane = lax.broadcasted_iota(jnp.int32, (16, cells), 1)

    def along(m, at_left, at_right):
        xm = jnp.where(lane < cells_y, at_left, pltpu.roll(m, cells_y, 1))
        xp = jnp.where(lane >= cells - cells_y, at_right, pltpu.roll(m, cells - cells_y, 1))
        dx = xp - xm
        flow = jnp.concatenate(
            [
                dx[1:2],
                dx[0:1] + dx[4:5] + dx[8:9],
                dx[5:6],
                dx[6:7],
                2.0 / 3.0 * (dx[1:2] + dx[10:11]),
            ],
            axis=0,
        )
        return (xp + xm - 4.0 * m)[0:5], flow

    def across(m):
        yp, ym = across_neighbours(m, cells_y)
        dy = yp - ym
        flow = jnp.concatenate(
            [
                dy[2:3],
                dy[5:6],
                dy[0:1] + dy[4:5] + dy[9:10],
                dy[7:8],
                2.0 / 3.0 * (dy[2:3] + dy[11:12]),
            ],
            axis=0,
        )
        return (yp + ym)[0:5], flow

    shifts = [0, cells - 2 * cells_y, cells - 2 * cells_y, cells - 4 * cells_y]
    placed = [edges if s == 0 else pltpu.roll(edges, s, 1) for s in shifts]
    laplace, flow = along(fixed, placed[0], placed[1])
    laplace_across, flow_across = across(fixed)
    change = spread * (laplace + laplace_across) - 0.25 * (flow + flow_across)
    laplace, flow = along(answer, placed[2], placed[3])
    change_answer = spread * laplace - 0.25 * flow
    message = [
        fixed[0:5],
        change,
        answer[0:5],
        answer[5:6],
        answer[7:8],
        answer[9:10],
        answer[11:12],
        change_answer,
        edges[13:14],
    ]
    spare = QUAD * (sent_ref.shape[2] // cells) - 25
    message = jnp.concatenate(message + [jnp.zeros((spare, cells), jnp.float32)], axis=0)
    for part in range(sent_ref.shape[2] // cells):
        piece = message[part * QUAD : (part + 1) * QUAD]
        for group in range(groups):
            sent_ref[group, :, part * cells : (part + 1) * cells] = piece


def finish_kernel(
    parts_ref,
    reach_ref,
    run_ref,
    back_ref,
    phi_ref,
    table_ref,
    line_ref,
    state_hbm,
    macro_hbm,
    state_ref,
    macro_ref,
    change_ref,
    entry_ref,
    sems,
):
    cells_x, cells_y, velocities = reach_ref.shape
    groups = parts_ref.shape[0]
    tiles = velocities // LANES
    cells = cells_x * cells_y
    sums = [parts_ref[group] for group in range(groups)]
    while len(sums) > 1:
        sums = [sums[n] + sums[n + 1] for n in range(0, len(sums), 2)]
    total = jnp.concatenate(
        [sums[0][:, n * cells : (n + 1) * cells] for n in range(parts_ref.shape[2] // cells)],
        axis=0,
    )
    lane = lax.broadcasted_iota(jnp.int32, (1, cells), 1)
    sums = total[24:25]
    here = jnp.logical_and(lane >= 4 * cells_y, lane < 5 * cells_y)
    incoming = jnp.where(here, pltpu.roll(sums, cells - cells_y, 1), 1.0)
    rho = jnp.where(here, sums, 0.0) / incoming
    width = cells_y
    while width < cells:
        rho = rho + pltpu.roll(rho, width, 1)
        width *= 2
    answer = rho * total[8:24]
    yp, ym = across_neighbours(answer, cells_y)
    dy = yp - ym
    flow = jnp.concatenate(
        [
            dy[4:5],
            dy[7:8],
            dy[2:3] + dy[6:7] + dy[9:10],
            dy[8:9],
            2.0 / 3.0 * (dy[4:5] + dy[10:11]),
        ],
        axis=0,
    )
    spread = line_ref[2:3, :]
    change = total[5:10] + rho * total[19:24] + spread * (yp + ym)[2:7] - 0.25 * flow
    updated = total[0:5] + answer[2:7] + change
    for x in range(cells_x):
        macro_ref[:, x, :] = updated[:, x * cells_y : (x + 1) * cells_y]
    macro_copy = pltpu.make_async_copy(macro_ref, macro_hbm, sems.at[cells_x])
    macro_copy.start()
    spare = jnp.zeros((3, cells), jnp.float32)
    change_ref[...] = columns_product(
        left_parts(jnp.concatenate([change, spare], axis=0)), phi_ref[...]
    )
    columns = jnp.broadcast_to(rho, (8, cells)).T
    density = jnp.broadcast_to(columns[0:cells_y, 0:1], (cells_y, LANES))
    for tile in range(tiles):
        lanes = slice(tile * LANES, (tile + 1) * LANES)
        forward = jnp.broadcast_to(table_ref[0:1, lanes], (cells_y, LANES)) > 0.5
        entry = whole_rows(back_ref, 0, tile, tiles, cells_y)
        mixed = whole_rows(back_ref, 1, tile, tiles, cells_y)
        entry_ref[:, lanes] = entry + jnp.where(forward, density * mixed, 0.0)
    copies = []
    span = 2
    for first in range(0, cells_x, span):
        for tile in range(tiles):
            lanes = slice(tile * LANES, (tile + 1) * LANES)
            entry = entry_ref[:, lanes]
            for x in range(first, first + span):
                change = change_ref[x * cells_y : (x + 1) * cells_y, lanes]
                value = reach_ref[x, :, lanes] * entry + run_ref[x, :, lanes] + change
                state_ref[x, :, lanes] = value
        copy = pltpu.make_async_copy(
            state_ref.at[pl.ds(first, span)], state_hbm.at[pl.ds(first, span)], sems.at[first]
        )
        copy.start()
        copies.append(copy)
    for copy in copies + [macro_copy]:
        copy.wait()


def local(state, macro, relax_rate, velocity, vel_sign, quad_weight, freestream, wall_flag):
    cells_x, cells_y, velocities = state.shape
    fields = macro.shape[0]
    slabs = lax.axis_size("gx")
    groups = lax.axis_size("vert")
    cells = cells_x * cells_y
    tiles = velocities // LANES
    assert slabs == tiles * (cells_y // QUAD) and cells == LANES
    f32 = jnp.float32
    sign = vel_sign.reshape(1, velocities)
    weight = quad_weight.reshape(1, velocities)
    wall = wall_flag.reshape(1, cells_y)
    shape = jax.ShapeDtypeStruct
    near = shape if INTERPRET else pltpu.VMEM

    def held(x):
        return x if INTERPRET else pltpu.with_memory_space_constraint(x, pltpu.VMEM)

    def call(body, outs, scratch, *args, **kwargs):
        return pl.pallas_call(
            body, out_shape=outs, scratch_shapes=scratch, interpret=INTERPRET, **kwargs
        )(*args)

    anywhere = pl.BlockSpec(memory_space=pl.ANY)
    sources = (state, macro, relax_rate, velocity, sign, weight, freestream, wall)
    reach, run, sent, side, psi, phi, table, line = call(
        lambda *refs: maps_kernel(float(cells_x * slabs), groups, *refs),
        (
            near(state.shape, f32),
            near(state.shape, f32),
            near((slabs, 2 * QUAD, LANES), f32),
            near((slabs, 4 * QUAD, LANES), f32),
            near((32, velocities), jnp.bfloat16),
            near((32, velocities), jnp.bfloat16),
            near((8, velocities), f32),
            near((8, cells), f32),
        ),
        [pltpu.VMEM(value.shape, value.dtype) for value in sources]
        + [
            pltpu.VMEM((8, cells), f32),
            pltpu.VMEM((8, velocities), f32),
            pltpu.VMEM((16, velocities), f32),
            pltpu.VMEM((cells, velocities), f32),
            pltpu.VMEM((cells_x + 1, cells_y, LANES), f32),
            pltpu.VMEM((4 * cells_y, velocities), jnp.bfloat16),
            pltpu.VMEM((2, cells_y, velocities), f32),
            pltpu.VMEM((2, cells_y, velocities), f32),
            pltpu.VMEM((8, LANES), f32),
            pltpu.SemaphoreType.DMA((10,)),
        ],
        *sources,
        in_specs=[anywhere] * len(sources),
    )
    reach, run, side = map(held, (reach, run, side))
    psi, phi, table, line = map(held, (psi, phi, table, line))
    maps = held(lax.all_to_all(sent, "gx", 0, 0))
    entries, edges = call(
        lambda *refs: scan_kernel(cells_x, *refs),
        (near((slabs, 2 * QUAD, LANES), f32), near((8, LANES), f32)),
        [pltpu.VMEM((slabs, QUAD, LANES), f32)] * 2,
        maps,
        side,
    )
    edges = held(edges)
    back = held(lax.all_to_all(entries, "gx", 0, 0))
    partial_sums = call(
        lambda *refs: moments_kernel(groups, slabs, *refs),
        near((groups, QUAD, SENT_PARTS * cells), f32),
        [
            pltpu.VMEM((6 * cells, velocities), jnp.bfloat16),
            pltpu.VMEM((16, cells), f32),
        ],
        reach,
        run,
        back,
        psi,
        table,
        line,
        edges,
    )
    parts = held(lax.all_to_all(partial_sums, "vert", 0, 0))
    new_state, new_macro = call(
        finish_kernel,
        (shape(state.shape, f32), shape(macro.shape, f32)),
        [
            pltpu.VMEM(state.shape, f32),
            pltpu.VMEM(macro.shape, f32),
            pltpu.VMEM((cells, velocities), f32),
            pltpu.VMEM((cells_y, velocities), f32),
            pltpu.SemaphoreType.DMA((cells_x + 1,)),
        ],
        parts,
        reach,
        run,
        back,
        phi,
        table,
        line,
        out_specs=(anywhere, anywhere),
    )
    return new_state, new_macro


def solution(mesh):
    return jax.shard_map(
        local,
        mesh=mesh,
        in_specs=(
            P("gx", None, "vert"),
            P(None, "gx", None),
            P("gx", None),
            P(None, "vert"),
            P("vert"),
            P("vert"),
            P(None, "vert"),
            P(),
        ),
        out_specs=(P("gx", None, "vert"), P(None, "gx", None)),
        check_vma=False,
    )
```

```python
import jax
import jax.numpy as jnp
from jax import lax
from jax.experimental import pallas as pl
from jax.experimental.pallas import tpu as pltpu
from jax.sharding import PartitionSpec as P

LANES = 128
QUAD = 4
EDGE_ROWS = (0, 1, 2, 3, 4, 5, 6, 8, 10)
INTERPRET = False


def left_parts(value):
    high = value.astype(jnp.bfloat16).astype(jnp.float32)
    return jnp.concatenate([high, value - high, high, jnp.zeros_like(high)], axis=0).astype(
        jnp.bfloat16
    )


def right_parts(value):
    high = value.astype(jnp.bfloat16).astype(jnp.float32)
    return jnp.concatenate([high, high, value - high, jnp.zeros_like(high)], axis=0).astype(
        jnp.bfloat16
    )


def columns_product(left, right):
    return lax.dot_general(
        left, right, (((0,), (0,)), ((), ())), preferred_element_type=jnp.float32
    )


def split_put(ref, row, lanes, value):
    half = ref.shape[0] // 2
    count = value.shape[0]
    high = value.astype(jnp.bfloat16)
    ref[row : row + count, lanes] = high
    ref[half + row : half + row + count, lanes] = (value - high.astype(jnp.float32)).astype(
        jnp.bfloat16
    )


def split_moments(psi_ref, left_ref):
    half = left_ref.shape[0] // 2
    product = lax.dot_general(
        psi_ref[...],
        left_ref[...],
        (((1,), (1,)), ((), ())),
        preferred_element_type=jnp.float32,
    )
    return product[0:16, 0:half] + product[16:32, 0:half] + product[0:16, half:]


def maps_kernel(
    total_cells,
    groups,
    state_hbm,
    macro_hbm,
    relax_hbm,
    velocity_hbm,
    sign_hbm,
    weight_hbm,
    free_hbm,
    wall_hbm,
    reach_ref,
    run_ref,
    sent_ref,
    side_ref,
    psi_ref,
    phi_ref,
    table_ref,
    line_ref,
    state_ref,
    macro_ref,
    relax_ref,
    velocity_ref,
    sign_ref,
    weight_ref,
    free_ref,
    wall_ref,
    cells_ref,
    basis_ref,
    moment_ref,
    equil_ref,
    spread_ref,
    left_ref,
    edge_decay_ref,
    edge_driven_ref,
    message_ref,
    sems,
):
    fields, cells_x, cells_y = macro_ref.shape
    velocities = state_ref.shape[2]
    tiles = velocities // LANES
    halves = cells_y // 8
    last = cells_x - 1
    large = [
        pltpu.make_async_copy(
            state_hbm.at[pl.ds(start, count)], state_ref.at[pl.ds(start, count)], sems.at[n]
        )
        for n, (start, count) in enumerate(((0, 1), (last, 1), (1, cells_x - 2)))
    ]
    small = [
        pltpu.make_async_copy(source, target, sems.at[len(large) + n])
        for n, (source, target) in enumerate(
            (
                (velocity_hbm, velocity_ref),
                (sign_hbm, sign_ref),
                (weight_hbm, weight_ref),
                (macro_hbm, macro_ref),
                (relax_hbm, relax_ref),
                (wall_hbm, wall_ref),
                (free_hbm, free_ref),
            )
        )
    ]
    for copy in large[0:2] + small + large[2:]:
        copy.start()
    for ref in (cells_ref, basis_ref, moment_ref, table_ref, line_ref, message_ref):
        ref[...] = jnp.zeros_like(ref)
    for copy in small:
        copy.wait()
    for x in range(cells_x):
        where = slice(x * cells_y, (x + 1) * cells_y)
        cells_ref[0:fields, where] = macro_ref[:, x, :]
        line_ref[0:1, where] = relax_ref[x : x + 1, :]
    line_ref[1:2, 0:cells_y] = (wall_ref[...] == 1).astype(jnp.float32)
    columns = line_ref[...].T
    for x in range(cells_x):
        spread_ref[x] = jnp.broadcast_to(
            columns[x * cells_y : (x + 1) * cells_y, 0:1], (cells_y, LANES)
        )
    spread_ref[cells_x] = jnp.broadcast_to(columns[0:cells_y, 1:2], (cells_y, LANES))
    relax_row = line_ref[0:1, :]
    line_ref[2:3, :] = 0.2 / (1.0 + relax_row)
    message_ref[0:1, :] = relax_row

    magnitude = velocity_ref[0:1, :]
    positive = sign_ref[...] == 1
    cx = jnp.where(positive, magnitude, -magnitude)
    cy = velocity_ref[1:2, :]
    cz = velocity_ref[2:3, :]
    square = cx * cx + cy * cy + cz * cz
    for k, row in enumerate((jnp.ones_like(cx), 2.0 * cx, 2.0 * cy, 2.0 * cz, square - 1.5)):
        basis_ref[k : k + 1, :] = row
    table_ref[0:1, :] = jnp.where(positive, 1.0, 0.0)
    table_ref[1:2, :] = total_cells * magnitude
    phi = right_parts(basis_ref[...])
    phi_ref[...] = phi
    equil_ref[...] = columns_product(left_parts(cells_ref[...]), phi)
    weight = weight_ref[...] / (velocities * groups)
    heat = 0.2 * (square - 2.5)
    for k, row in enumerate(
        (
            jnp.ones_like(cx),
            cx,
            cy,
            cz,
            2.0 / 3.0 * square - 1.0,
            2.0 * cx * cy,
            2.0 * cx * cz,
            2.0 * cy * cz,
            2.0 * (cx * cx - square / 3.0),
            2.0 * (cy * cy - square / 3.0),
            heat * cx,
            heat * cy,
            heat * cz,
            magnitude,
        )
    ):
        moment_ref[k : k + 1, :] = weight * row
    high = moment_ref[...].astype(jnp.bfloat16)
    psi_ref[0:16] = high
    psi_ref[16:32] = (moment_ref[...] - high.astype(jnp.float32)).astype(jnp.bfloat16)

    def cell(x, rows, lanes, courant):
        relax = spread_ref[x, rows]
        first = x * cells_y + rows.start
        inverse = 1.0 / (1.0 + courant + relax)
        gain = state_ref[x, rows, lanes] + relax * equil_ref[first : first + 8, lanes]
        return courant * inverse, gain * inverse

    def settings(lanes):
        forward = jnp.broadcast_to(table_ref[0:1, lanes], (8, LANES)) > 0.5
        return forward, jnp.broadcast_to(table_ref[1:2, lanes], (8, LANES))

    for copy in large[0:2]:
        copy.wait()
    for half in range(halves):
        rows = slice(half * 8, half * 8 + 8)
        for tile in range(tiles):
            lanes = slice(tile * LANES, (tile + 1) * LANES)
            forward, courant = settings(lanes)
            pair = [cell(x, rows, lanes, courant) for x in (0, last)]
            for n in range(2):
                edge_decay_ref[n, rows, lanes] = pair[n][0]
                edge_driven_ref[n, rows, lanes] = pair[n][1]
            split_put(left_ref, half * 8, lanes, jnp.where(forward, pair[0][1], 0.0))
            split_put(left_ref, cells_y + half * 8, lanes, jnp.where(forward, 0.0, pair[1][1]))
    large[2].wait()
    edge_moments = split_moments(psi_ref, left_ref)
    for n, k in enumerate(EDGE_ROWS):
        row = 1 + n // QUAD
        start = (n % QUAD) * 2 * cells_y
        message_ref[row : row + 1, start : start + 2 * cells_y] = edge_moments[k : k + 1, :]
    for half in range(halves):
        rows = slice(half * 8, half * 8 + 8)
        for tile in range(tiles):
            lanes = slice(tile * LANES, (tile + 1) * LANES)
            forward, courant = settings(lanes)
            decay = [edge_decay_ref[0, rows, lanes]]
            driven = [edge_driven_ref[0, rows, lanes]]
            for x in range(1, last):
                one, two = cell(x, rows, lanes, courant)
                decay.append(one)
                driven.append(two)
            decay.append(edge_decay_ref[1, rows, lanes])
            driven.append(edge_driven_ref[1, rows, lanes])
            steps = [jnp.where(forward, decay[t], decay[last - t]) for t in range(cells_x)]
            gains = [jnp.where(forward, driven[t], driven[last - t]) for t in range(cells_x)]
            products = [steps[0]]
            runs = [gains[0]]
            for t in range(1, cells_x):
                products.append(steps[t] * products[-1])
                runs.append(steps[t] * runs[-1] + gains[t])
            for x in range(cells_x):
                reach_ref[x, rows, lanes] = jnp.where(forward, products[x], products[last - x])
                run_ref[x, rows, lanes] = jnp.where(forward, runs[x], runs[last - x])
            wall = spread_ref[cells_x, rows] > 0.5
            diffuse = jnp.logical_and(forward, wall)
            fixed = jnp.where(diffuse, 0.0, free_ref[rows, lanes])
            unit = jnp.where(diffuse, 1.0, 0.0)
            direction = jnp.where(forward, 1.0, 0.0)
            for part in range(8 // QUAD):
                owner = (half * (8 // QUAD) + part) * tiles + tile
                quad = slice(part * QUAD, (part + 1) * QUAD)
                sent_ref[owner, 0:QUAD, :] = runs[last][quad]
                for slot, value in enumerate((fixed, unit, direction, courant)):
                    side_ref[owner, slot * QUAD : (slot + 1) * QUAD, :] = value[quad]
    message = message_ref[0:QUAD]
    for owner in range(sent_ref.shape[0]):
        sent_ref[owner, QUAD : 2 * QUAD, :] = message


def scan_kernel(cells_x, maps_ref, side_ref, sent_ref, edges_ref, entry_ref, product_ref):
    slabs = maps_ref.shape[0]
    me = lax.axis_index("gx")
    side = side_ref[me]
    fixed = side[0:QUAD]
    unit = side[QUAD : 2 * QUAD]
    forward = side[2 * QUAD : 3 * QUAD] > 0.5
    courant = side[3 * QUAD : 4 * QUAD]
    base = 1.0 + side[3 * QUAD : 3 * QUAD + 1]
    power = courant
    reach = 1
    while reach < cells_x:
        power = power * power
        reach *= 2
    below = jnp.maximum(me - 1, 0)
    above = jnp.minimum(me + 1, slabs - 1)
    edges_ref[0:QUAD] = maps_ref[below, QUAD : 2 * QUAD]
    edges_ref[QUAD : 2 * QUAD] = maps_ref[above, QUAD : 2 * QUAD]
    relax = jnp.concatenate([maps_ref[i, QUAD : QUAD + 1] for i in range(slabs)], axis=0).T
    cells_y = relax.shape[0] // cells_x
    quads = cells_y // QUAD
    index = me // (slabs // quads)
    high = index // 2 == 1
    odd = index % 2 == 1
    picked = []
    for x in range(cells_x):
        rows = relax[x * cells_y : (x + 1) * cells_y]
        rows = jnp.where(high, rows[8:16], rows[0:8])
        picked.append(jnp.where(odd, rows[QUAD:8], rows[0:QUAD]))
    relax = jnp.concatenate(picked, axis=0)
    cells = cells_x * QUAD
    for i in range(slabs):
        divisors = base + jnp.broadcast_to(relax[:, i : i + 1], (cells, LANES))
        product = divisors[0:8]
        for first in range(8, cells, 8):
            product = product * divisors[first : first + 8]
        product = product[0:QUAD] * product[QUAD:8]
        product_ref[i] = power * (1.0 / product)
    value = fixed
    for i in range(slabs - 1, -1, -1):
        entry_ref[i] = value
        value = product_ref[i] * value + maps_ref[i, 0:QUAD]
    leaving = value
    value = fixed
    answer = unit
    for i in range(slabs):
        sent_ref[i, 0:QUAD] = jnp.where(forward, value, entry_ref[i])
        sent_ref[i, QUAD : 2 * QUAD] = jnp.where(forward, answer, leaving)
        value = product_ref[i] * value + maps_ref[i, 0:QUAD]
        answer = product_ref[i] * answer


def whole_rows(back_ref, slot, tile, tiles, cells_y):
    return jnp.concatenate(
        [
            back_ref[quad * tiles + tile, slot * QUAD : (slot + 1) * QUAD]
            for quad in range(cells_y // QUAD)
        ],
        axis=0,
    )


def across_neighbours(m, cells_y):
    cells = m.shape[1]
    y = lax.broadcasted_iota(jnp.int32, m.shape, 1) % cells_y
    yp = jnp.where(y == cells_y - 1, pltpu.roll(m, cells_y - 1, 1), pltpu.roll(m, cells - 1, 1))
    ym = jnp.where(y == 0, pltpu.roll(m, cells - cells_y + 1, 1), pltpu.roll(m, 1, 1))
    return yp, ym


def moments_kernel(
    groups,
    slabs,
    reach_ref,
    run_ref,
    back_ref,
    psi_ref,
    table_ref,
    line_ref,
    edges_ref,
    sent_ref,
    left_ref,
    near_ref,
):
    cells_x, cells_y, velocities = reach_ref.shape
    tiles = velocities // LANES
    cells = cells_x * cells_y
    me = lax.axis_index("gx")
    from_left = jnp.where(me > 0, 1.0, 0.0)
    from_right = jnp.where(me < slabs - 1, 1.0, 0.0)

    def put(row, value, lanes):
        split_put(left_ref, row, lanes, value)

    near_ref[...] = jnp.zeros_like(near_ref)
    for n, k in enumerate(EDGE_ROWS):
        row = 1 + n // QUAD
        start = (n % QUAD) * 2 * cells_y
        near_ref[k : k + 1, 0:cells_y] = (
            edges_ref[row : row + 1, start + cells_y : start + 2 * cells_y] * from_left
        )
        near_ref[k : k + 1, cells_y : 2 * cells_y] = (
            edges_ref[QUAD + row : QUAD + row + 1, start : start + cells_y] * from_right
        )
    columns = edges_ref[...].T
    relax_left = jnp.broadcast_to(columns[cells - cells_y : cells, 0:1], (cells_y, LANES))
    relax_right = jnp.broadcast_to(columns[0:cells_y, QUAD : QUAD + 1], (cells_y, LANES))
    for tile in range(tiles):
        lanes = slice(tile * LANES, (tile + 1) * LANES)
        forward = jnp.broadcast_to(table_ref[0:1, lanes], (cells_y, LANES)) > 0.5
        courant = jnp.broadcast_to(table_ref[1:2, lanes], (cells_y, LANES))
        entry = whole_rows(back_ref, 0, tile, tiles, cells_y)
        mixed = whole_rows(back_ref, 1, tile, tiles, cells_y)
        answer = jnp.where(forward, mixed, 0.0)
        leaving = jnp.where(forward, 0.0, mixed)
        for x in range(cells_x):
            reach = reach_ref[x, :, lanes]
            value = reach * entry + run_ref[x, :, lanes]
            put(x * cells_y, value, lanes)
            put(cells + x * cells_y, reach * answer, lanes)
            if x == 0:
                outgoing = value
            if x == cells_x - 1:
                outgoing = jnp.where(forward, value, outgoing)
                outgoing_answer = reach * answer
        decay = courant / (1.0 + courant + jnp.where(forward, relax_right, relax_left))
        inside = jnp.where(forward, from_right, from_left)
        near = decay * outgoing * inside
        near_answer = decay * outgoing_answer * inside
        row = 2 * cells
        put(row, jnp.where(forward, entry * from_left, near), lanes)
        put(row + cells_y, jnp.where(forward, near, entry * from_right), lanes)
        put(row + 2 * cells_y, answer * from_left, lanes)
        put(row + 3 * cells_y, near_answer, lanes)
        put(row + 4 * cells_y, leaving, lanes)
        put(row + 5 * cells_y, jnp.where(forward, 1.0, 0.0), lanes)
        put(row + 6 * cells_y, jnp.zeros_like(entry), lanes)
        put(row + 7 * cells_y, jnp.zeros_like(entry), lanes)

    total = split_moments(psi_ref, left_ref)
    fixed = total[:, 0:cells]
    answer = total[:, cells : 2 * cells]
    edges = total[:, 2 * cells : 3 * cells] + near_ref[...]

    spread = line_ref[2:3, :]
    lane = lax.broadcasted_iota(jnp.int32, (16, cells), 1)

    def along(m, at_left, at_right):
        xm = jnp.where(lane < cells_y, at_left, pltpu.roll(m, cells_y, 1))
        xp = jnp.where(lane >= cells - cells_y, at_right, pltpu.roll(m, cells - cells_y, 1))
        dx = xp - xm
        flow = jnp.concatenate(
            [
                dx[1:2],
                dx[0:1] + dx[4:5] + dx[8:9],
                dx[5:6],
                dx[6:7],
                2.0 / 3.0 * (dx[1:2] + dx[10:11]),
            ],
            axis=0,
        )
        return (xp + xm - 4.0 * m)[0:5], flow

    def across(m):
        yp, ym = across_neighbours(m, cells_y)
        dy = yp - ym
        flow = jnp.concatenate(
            [
                dy[2:3],
                dy[5:6],
                dy[0:1] + dy[4:5] + dy[9:10],
                dy[7:8],
                2.0 / 3.0 * (dy[2:3] + dy[11:12]),
            ],
            axis=0,
        )
        return (yp + ym)[0:5], flow

    shifts = [0, cells - 2 * cells_y, cells - 2 * cells_y, cells - 4 * cells_y]
    placed = [edges if s == 0 else pltpu.roll(edges, s, 1) for s in shifts]
    laplace, flow = along(fixed, placed[0], placed[1])
    laplace_across, flow_across = across(fixed)
    change = spread * (laplace + laplace_across) - 0.25 * (flow + flow_across)
    laplace, flow = along(answer, placed[2], placed[3])
    change_answer = spread * laplace - 0.25 * flow
    lane = lax.broadcasted_iota(jnp.int32, (1, cells), 1)
    final = jnp.where(
        lane < 6 * cells_y, edges[13:14], pltpu.roll(answer[5:6], 6 * cells_y, 1)
    )
    message = jnp.concatenate(
        [
            fixed[0:5],
            change,
            answer[0:5],
            answer[7:8],
            answer[9:10],
            answer[11:12],
            change_answer,
            final,
        ],
        axis=0,
    )
    for group in range(groups):
        sent_ref[group] = message


def finish_kernel(
    total_cells,
    parts_ref,
    reach_ref,
    run_ref,
    back_ref,
    phi_ref,
    table_ref,
    line_ref,
    state_hbm,
    macro_hbm,
    state_ref,
    macro_ref,
    change_ref,
    entry_ref,
    sems,
):
    cells_x, cells_y, velocities = reach_ref.shape
    groups = parts_ref.shape[0]
    tiles = velocities // LANES
    cells = cells_x * cells_y
    sums = [parts_ref[group] for group in range(groups)]
    while len(sums) > 1:
        sums = [sums[n] + sums[n + 1] for n in range(0, len(sums), 2)]
    total = sums[0]
    lane = lax.broadcasted_iota(jnp.int32, (1, cells), 1)
    sums = total[23:24]
    here = jnp.logical_and(lane >= 4 * cells_y, lane < 5 * cells_y)
    incoming = jnp.where(here, pltpu.roll(sums, cells - cells_y, 1), 1.0)
    rho = jnp.where(here, sums, 0.0) / incoming
    start = jnp.logical_and(lane >= 6 * cells_y, lane < 7 * cells_y)
    across_flow = jnp.where(start, sums, 0.0)
    lost = jnp.where(lane >= cells_y, (1.0 + line_ref[0:1, :]) * total[12:13], 0.0)
    width = cells_y
    while width < cells:
        rho = rho + pltpu.roll(rho, width, 1)
        across_flow = across_flow + pltpu.roll(across_flow, width, 1)
        lost = lost + jnp.where(lane >= width, pltpu.roll(lost, width, 1), 0.0)
        width *= 2
    across_flow = across_flow - (2.0 / total_cells) * lost
    answer = rho * jnp.concatenate([total[8:23], across_flow], axis=0)
    yp, ym = across_neighbours(answer, cells_y)
    dy = yp - ym
    flow = jnp.concatenate(
        [
            dy[4:5],
            dy[15:16],
            dy[2:3] + dy[6:7] + dy[8:9],
            dy[7:8],
            2.0 / 3.0 * (dy[4:5] + dy[9:10]),
        ],
        axis=0,
    )
    spread = line_ref[2:3, :]
    change = total[5:10] + rho * total[18:23] + spread * (yp + ym)[2:7] - 0.25 * flow
    updated = total[0:5] + answer[2:7] + change
    for x in range(cells_x):
        macro_ref[:, x, :] = updated[:, x * cells_y : (x + 1) * cells_y]
    macro_copy = pltpu.make_async_copy(macro_ref, macro_hbm, sems.at[cells_x])
    macro_copy.start()
    spare = jnp.zeros((3, cells), jnp.float32)
    change_ref[...] = columns_product(
        left_parts(jnp.concatenate([change, spare], axis=0)), phi_ref[...]
    )
    columns = jnp.broadcast_to(rho, (8, cells)).T
    density = jnp.broadcast_to(columns[0:cells_y, 0:1], (cells_y, LANES))
    for tile in range(tiles):
        lanes = slice(tile * LANES, (tile + 1) * LANES)
        forward = jnp.broadcast_to(table_ref[0:1, lanes], (cells_y, LANES)) > 0.5
        entry = whole_rows(back_ref, 0, tile, tiles, cells_y)
        mixed = whole_rows(back_ref, 1, tile, tiles, cells_y)
        entry_ref[:, lanes] = entry + jnp.where(forward, density * mixed, 0.0)
    copies = []
    span = 2
    for first in range(0, cells_x, span):
        for tile in range(tiles):
            lanes = slice(tile * LANES, (tile + 1) * LANES)
            entry = entry_ref[:, lanes]
            for x in range(first, first + span):
                change = change_ref[x * cells_y : (x + 1) * cells_y, lanes]
                value = reach_ref[x, :, lanes] * entry + run_ref[x, :, lanes] + change
                state_ref[x, :, lanes] = value
        copy = pltpu.make_async_copy(
            state_ref.at[pl.ds(first, span)], state_hbm.at[pl.ds(first, span)], sems.at[first]
        )
        copy.start()
        copies.append(copy)
    for copy in copies + [macro_copy]:
        copy.wait()


def local(state, macro, relax_rate, velocity, vel_sign, quad_weight, freestream, wall_flag):
    cells_x, cells_y, velocities = state.shape
    fields = macro.shape[0]
    slabs = lax.axis_size("gx")
    groups = lax.axis_size("vert")
    cells = cells_x * cells_y
    tiles = velocities // LANES
    assert slabs == tiles * (cells_y // QUAD) and cells == LANES
    f32 = jnp.float32
    sign = vel_sign.reshape(1, velocities)
    weight = quad_weight.reshape(1, velocities)
    wall = wall_flag.reshape(1, cells_y)
    shape = jax.ShapeDtypeStruct
    near = shape if INTERPRET else pltpu.VMEM

    def held(x):
        return x if INTERPRET else pltpu.with_memory_space_constraint(x, pltpu.VMEM)

    def call(body, outs, scratch, *args, **kwargs):
        return pl.pallas_call(
            body, out_shape=outs, scratch_shapes=scratch, interpret=INTERPRET, **kwargs
        )(*args)

    anywhere = pl.BlockSpec(memory_space=pl.ANY)
    sources = (state, macro, relax_rate, velocity, sign, weight, freestream, wall)
    reach, run, sent, side, psi, phi, table, line = call(
        lambda *refs: maps_kernel(float(cells_x * slabs), groups, *refs),
        (
            near(state.shape, f32),
            near(state.shape, f32),
            near((slabs, 2 * QUAD, LANES), f32),
            near((slabs, 4 * QUAD, LANES), f32),
            near((32, velocities), jnp.bfloat16),
            near((32, velocities), jnp.bfloat16),
            near((8, velocities), f32),
            near((8, cells), f32),
        ),
        [pltpu.VMEM(value.shape, value.dtype) for value in sources]
        + [
            pltpu.VMEM((8, cells), f32),
            pltpu.VMEM((8, velocities), f32),
            pltpu.VMEM((16, velocities), f32),
            pltpu.VMEM((cells, velocities), f32),
            pltpu.VMEM((cells_x + 1, cells_y, LANES), f32),
            pltpu.VMEM((4 * cells_y, velocities), jnp.bfloat16),
            pltpu.VMEM((2, cells_y, velocities), f32),
            pltpu.VMEM((2, cells_y, velocities), f32),
            pltpu.VMEM((8, LANES), f32),
            pltpu.SemaphoreType.DMA((10,)),
        ],
        *sources,
        in_specs=[anywhere] * len(sources),
    )
    reach, run, side = map(held, (reach, run, side))
    psi, phi, table, line = map(held, (psi, phi, table, line))
    maps = held(lax.all_to_all(sent, "gx", 0, 0))
    entries, edges = call(
        lambda *refs: scan_kernel(cells_x, *refs),
        (near((slabs, 2 * QUAD, LANES), f32), near((8, LANES), f32)),
        [pltpu.VMEM((slabs, QUAD, LANES), f32)] * 2,
        maps,
        side,
    )
    edges = held(edges)
    back = held(lax.all_to_all(entries, "gx", 0, 0))
    partial_sums = call(
        lambda *refs: moments_kernel(groups, slabs, *refs),
        near((groups, 24, cells), f32),
        [
            pltpu.VMEM((6 * cells, velocities), jnp.bfloat16),
            pltpu.VMEM((16, cells), f32),
        ],
        reach,
        run,
        back,
        psi,
        table,
        line,
        edges,
    )
    parts = held(lax.all_to_all(partial_sums, "vert", 0, 0))
    new_state, new_macro = call(
        lambda *refs: finish_kernel(float(cells_x * slabs), *refs),
        (shape(state.shape, f32), shape(macro.shape, f32)),
        [
            pltpu.VMEM(state.shape, f32),
            pltpu.VMEM(macro.shape, f32),
            pltpu.VMEM((cells, velocities), f32),
            pltpu.VMEM((cells_y, velocities), f32),
            pltpu.SemaphoreType.DMA((cells_x + 1,)),
        ],
        parts,
        reach,
        run,
        back,
        phi,
        table,
        line,
        out_specs=(anywhere, anywhere),
    )
    return new_state, new_macro


def solution(mesh):
    return jax.shard_map(
        local,
        mesh=mesh,
        in_specs=(
            P("gx", None, "vert"),
            P(None, "gx", None),
            P("gx", None),
            P(None, "vert"),
            P("vert"),
            P("vert"),
            P(None, "vert"),
            P(),
        ),
        out_specs=(P("gx", None, "vert"), P(None, "gx", None)),
        check_vma=False,
    )
```
